32 devices in a mesh: seq: 2 (over core), hid: 16 (over z, y, x).
Axes of the slice: x: 2, y: 2, z: 4, core: 2. Of those that a mesh axis runs over, the one named last changes fastest.
Arguments:
- inputs: bfloat16 [2, 768, 2048], P('seq', 'hid'), may hold values from -6 to 6
- cotangent: bfloat16 [2, 768, 2048], P('seq', 'hid'), may hold values from -6 to 6
- lengths: int32 [12], replicated, may hold values from 1 to 1024, 1536 in all
- first_gain: float32 [2048], replicated, may hold values from 0.25 to 1.75
- q_weight: bfloat16 [2048, 2048], P(('seq', 'hid')), may hold values from -0.125 to 0.125
- f_weight: bfloat16 [2048, 2048], P(('seq', 'hid')), may hold values from -0.125 to 0.125
- i_weight: bfloat16 [2048, 2048], P(('seq', 'hid')), may hold values from -0.125 to 0.125
- o_weight: bfloat16 [2048, 2048], P(('seq', 'hid')), may hold values from -0.125 to 0.125
- group_gain: float32 [128], replicated, may hold values from 0.25 to 1.75
- gap_log: float32 [2048], replicated, may hold values from -11.5 to -3.5
- second_gain: float32 [2048], replicated, may hold values from 0.25 to 1.75
- gate_weight: bfloat16 [2048, 5632], P(('seq', 'hid')), may hold values from -0.125 to 0.125
- up_weight: bfloat16 [2048, 5632], P(('seq', 'hid')), may hold values from -0.125 to 0.125
- down_weight: bfloat16 [2048, 5632], P(('seq', 'hid')), may hold values from -0.078125 to 0.078125
Outputs:
- output: bfloat16 [2, 768, 2048], P('seq', 'hid')
- input_grad: float32 [2, 768, 2048], P('seq', 'hid')
- first_grad: float32 [2048], replicated
- q_grad: float32 [2048, 2048], P(('seq', 'hid'))
- f_grad: float32 [2048, 2048], P(('seq', 'hid'))
- i_grad: float32 [2048, 2048], P(('seq', 'hid'))
- o_grad: float32 [2048, 2048], P(('seq', 'hid'))
- group_grad: float32 [128], replicated
- gap_grad: float32 [2048], replicated
- second_grad: float32 [2048], replicated
- gate_grad: float32 [2048, 5632], P(('seq', 'hid'))
- up_grad: float32 [2048, 5632], P(('seq', 'hid'))
- down_grad: float32 [2048, 5632], P(('seq', 'hid'))
The draws below stay inside these ranges and needn't reach their ends.
Inputs may be any that keep to these rules, and one draw needn't show every extreme that they name: The 12 documents fill the 1536 positions in order; the lengths sum to 1536 and the largest is exactly 1024.
All inputs are finite; a program needn't handle non-finite values.
Results may differ from the reference program's by a relative error of at most 0.015.
Values may be sent and summed in bfloat16 or wider, within the bound.
A program may use at most 320 MiB of HBM per device.

```python
import math
from functools import partial
import jax
import jax.numpy as jnp
import numpy as np
from jax import lax

D = 2048
H = 16
FF = 5632
SPAN = 128
DOCS = 12
HD = 128
BLOCKS = 2
BLOCK_LEN = 768
TOKENS = 1536
LONGEST = 1024


def block_scale(stream_key, dims, shards, low, top_value):
    factor_of, own = 1.0, jax.random.fold_in(stream_key, 6)
    for dim, parts in shards:
        draws = jnp.exp(jax.random.uniform(jax.random.fold_in(own, dim), (parts,), jnp.float32, low / len(shards), top_value / len(shards)))
        factor_of = factor_of * jnp.repeat(draws, dims[dim] // parts).reshape([-1 if axis == dim else 1 for axis in range(len(dims))])
    return factor_of


def length_profile(amount, total, reach, slope):
    weights = [(1 << 20) // math.isqrt(rank ** slope) + 1 for rank in range(2, amount + 1)]
    rest, given = total - reach - (amount - 1), [1] * (amount - 1)
    while rest > 0:
        free = [i for i in range(amount - 1) if given[i] < reach]
        mass, budget = sum([weights[i] for i in free]), rest
        for i in free:
            addition = min(reach - given[i], max(1, budget * weights[i] // mass), rest)
            given[i] = given[i] + addition
            rest = rest - addition
    return np.array([reach] + given)


def uneven_parts(rng, number_of, total, reach, slope):
    if number_of == 2:
        one = jax.random.randint(rng, (), max(1, total - reach), min(reach, total - 1) + 1)
        return jnp.stack([one, total - one])
    tallies = jnp.asarray(length_profile(number_of, total, reach, slope), jnp.int32)
    pairs = (number_of - 1) // 2
    giver, receiver = tallies[1:1 + 2 * pairs:2], tallies[2:2 + 2 * pairs:2]
    slack = jnp.minimum(giver - 1, reach - receiver)
    shifted = jax.random.randint(jax.random.fold_in(rng, 1), (pairs,), 0, 1 << 20) % (slack + 1)
    tallies = tallies.at[1:1 + 2 * pairs:2].set(giver - shifted).at[2:2 + 2 * pairs:2].set(receiver + shifted)
    return tallies[jax.random.permutation(jax.random.fold_in(rng, 2), number_of)]


def noise(key, shape, width, bound, split=(), kind=jnp.bfloat16):
    gain = block_scale(key, shape, split, -0.22, 0.18) if split else 1.0
    values = jax.random.normal(key, shape, jnp.float32) * width * gain
    return jnp.minimum(jnp.maximum(values, -bound), bound).astype(kind)


def setup_inputs(seed: int = 0) -> dict:
    streams_of = jax.random.split(jax.random.key(seed), 15)
    inputs = noise(streams_of[0], (BLOCKS, BLOCK_LEN, D), 1.0, 6.0, ((0, 2), (1, 16)))
    cotangent = noise(streams_of[1], (BLOCKS, BLOCK_LEN, D), 1.0, 6.0, ((0, 2), (1, 16)))
    lengths = uneven_parts(streams_of[2], DOCS, TOKENS, LONGEST, 2).astype(jnp.int32)
    first_gain = jnp.clip(1.0 + 0.15 * jax.random.normal(streams_of[3], (D,), jnp.float32), 0.25, 1.75)
    q_weight = noise(streams_of[4], (D, D), D ** -0.5, 0.125, ((0, 32),))
    f_weight = noise(streams_of[5], (D, D), D ** -0.5, 0.125, ((0, 32),))
    i_weight = noise(streams_of[6], (D, D), D ** -0.5, 0.125, ((0, 32),))
    o_weight = noise(streams_of[7], (D, D), D ** -0.5, 0.125, ((0, 32),))
    group_gain = jnp.clip(1.0 + 0.15 * jax.random.normal(streams_of[8], (HD,), jnp.float32), 0.25, 1.75)
    gap_log = jnp.clip(jax.random.uniform(streams_of[9], (D,), jnp.float32, -11.5, -3.5), -11.5, -3.5)
    second_gain = jnp.clip(1.0 + 0.15 * jax.random.normal(streams_of[10], (D,), jnp.float32), 0.25, 1.75)
    gate_weight = noise(streams_of[11], (D, FF), D ** -0.5, 0.125, ((0, 32),))
    up_weight = noise(streams_of[12], (D, FF), D ** -0.5, 0.125, ((0, 32),))
    down_weight = noise(streams_of[13], (D, FF), FF ** -0.5, 0.078125, ((0, 32),))
    return {"inputs": inputs, "cotangent": cotangent, "lengths": lengths, "first_gain": first_gain, "q_weight": q_weight, "f_weight": f_weight, "i_weight": i_weight, "o_weight": o_weight, "group_gain": group_gain, "gap_log": gap_log, "second_gain": second_gain, "gate_weight": gate_weight, "up_weight": up_weight, "down_weight": down_weight}


EPS = 1e-06
HIGH_PRECISION = lax.Precision.HIGHEST

@jax.custom_vjp
def low(v):
    return lax.optimization_barrier(v.astype(jnp.bfloat16)).astype(jnp.float32)

@jax.custom_vjp
def low_back(v):
    return v

def low_keep(v):
    return (low(v), None)

def low_pass(kept, grad):
    return (grad,)

def back_keep(v):
    return (v, None)

def back_low(kept, grad):
    return (low(grad),)
low.defvjp(low_keep, low_pass)
low_back.defvjp(back_keep, back_low)

def normed(entries, gain_vec):
    factor = lax.rsqrt(lax.optimization_barrier(jnp.mean(entries * entries, axis=-1, keepdims=True)) + EPS)
    return entries * factor * gain_vec

def gates(q_part, f_part, gap_piece):
    key_gate = jnp.exp(gap_piece) * jax.nn.sigmoid(-f_part)
    return (jax.nn.silu(q_part), key_gate, jnp.log1p(-key_gate))

def doc_ids(lengths, positions):
    lengths = lengths.astype(jnp.int32)
    starts = (jnp.cumsum(lengths) - lengths).astype(jnp.int32)
    covered = (starts[None, :] <= positions[:, None]).astype(jnp.int32)
    return (lax.optimization_barrier(jnp.sum(covered, axis=1)) - 1).astype(jnp.int32)

def span_step(memory_state, pieces):
    queries, key_gate, value_rows, log_decay, documents, before = pieces
    cumulative = jnp.cumsum(log_decay, axis=1)
    query_decayed = queries * jnp.exp(cumulative)
    k_grown = key_gate * jnp.exp(-cumulative)
    extent = documents.shape[0]
    row_ids = lax.broadcasted_iota(jnp.int32, (extent, extent), 0)
    col_ids = lax.broadcasted_iota(jnp.int32, (extent, extent), 1)
    same_doc = jnp.logical_and(documents[:, None] == documents[None, :], row_ids >= col_ids).astype(jnp.float32)
    scores = jnp.einsum('hck,hsk->hcs', query_decayed, k_grown, precision=HIGH_PRECISION) * same_doc[None]
    within_block = jnp.einsum('hcs,hsv->hcv', scores, value_rows, precision=HIGH_PRECISION)
    carried_state = (documents == before).astype(jnp.float32)[None, :, None]
    output_rows = within_block + carried_state * jnp.einsum('awn,ani->awi', query_decayed, memory_state, precision=HIGH_PRECISION)
    last_cum = cumulative[:, -1:, :]
    keep_mask = (documents == documents[-1]).astype(jnp.float32)[None, :, None]
    tail_key_rows = jnp.exp(last_cum - cumulative) * key_gate * keep_mask
    whole_block = (documents[-1] == before).astype(jnp.float32)
    fresh_state = jnp.einsum('wfx,wfg->wxg', tail_key_rows, value_rows, precision=HIGH_PRECISION)
    memory_state = jnp.exp(last_cum[:, 0, :])[:, :, None] * whole_block * memory_state + fresh_state
    return (memory_state, output_rows)

def recur(queries, key_gate, value_rows, log_decay, documents, before, memory_state):
    head_count, extent, columns = queries.shape
    span_count = extent // SPAN

    def by_span(tensor):
        return jnp.swapaxes(tensor.reshape(head_count, span_count, SPAN, tensor.shape[-1]), 0, 1)
    doc_rows = documents.reshape(span_count, SPAN)
    befores = jnp.concatenate([jnp.reshape(before, (1,)).astype(jnp.int32), doc_rows[:-1, -1].astype(jnp.int32)]).astype(jnp.int32)
    memory_state, span_out = lax.scan(jax.checkpoint(span_step), memory_state, (by_span(queries), by_span(key_gate), by_span(value_rows), by_span(log_decay), doc_rows, befores))
    return (jnp.swapaxes(span_out, 0, 1).reshape(head_count, extent, value_rows.shape[-1]), memory_state)

def layer(entries, first_gain, q_weight, f_weight, i_weight, o_weight, group_gain, gap_log, second_gain, gate_weight, up_weight, down_weight, documents):
    token_count = entries.shape[0]
    first_norm = low(normed(entries, first_gain))
    q_lin = low_back(jnp.dot(first_norm, q_weight, precision=HIGH_PRECISION, preferred_element_type=jnp.float32))
    f_lin = low_back(jnp.dot(first_norm, f_weight, precision=HIGH_PRECISION, preferred_element_type=jnp.float32))
    i_lin = low_back(jnp.dot(first_norm, i_weight, precision=HIGH_PRECISION, preferred_element_type=jnp.float32))
    queries, key_gate, log_decay = gates(q_lin, f_lin, gap_log)

    def by_head(tensor):
        return jnp.swapaxes(tensor.reshape(token_count, H, HD), 0, 1)
    mixed_out, _ = recur(by_head(queries), by_head(key_gate), by_head(i_lin), by_head(log_decay), documents, jnp.int32(-1), jnp.zeros((H, HD, HD), jnp.float32))
    head_normed = low(normed(mixed_out, group_gain))
    flattened = jnp.swapaxes(head_normed, 0, 1).reshape(token_count, H * HD)
    mix_out = low_back(lax.dot_general(flattened, o_weight, (((1,), (1,)), ((), ())), precision=HIGH_PRECISION, preferred_element_type=jnp.float32))
    middle = entries + mix_out
    second_norm = low(normed(middle, second_gain))
    gate_lin = low_back(jnp.dot(second_norm, gate_weight, precision=HIGH_PRECISION, preferred_element_type=jnp.float32))
    upward = low_back(jnp.dot(second_norm, up_weight, precision=HIGH_PRECISION, preferred_element_type=jnp.float32))
    hidden = low(jax.nn.silu(gate_lin) * upward)
    return middle + lax.dot_general(hidden, down_weight, (((1,), (1,)), ((), ())), precision=HIGH_PRECISION, preferred_element_type=jnp.float32)

def reference(inputs, cotangent, lengths, first_gain, q_weight, f_weight, i_weight, o_weight, group_gain, gap_log, second_gain, gate_weight, up_weight, down_weight):
    token_count = TOKENS
    documents = doc_ids(lengths, jnp.arange(token_count, dtype=jnp.int32))
    primals = (inputs.reshape(token_count, D).astype(jnp.float32), first_gain.astype(jnp.float32), q_weight.astype(jnp.float32), f_weight.astype(jnp.float32), i_weight.astype(jnp.float32), o_weight.astype(jnp.float32), group_gain.astype(jnp.float32), gap_log.astype(jnp.float32), second_gain.astype(jnp.float32), gate_weight.astype(jnp.float32), up_weight.astype(jnp.float32), down_weight.astype(jnp.float32))
    layer_fn = partial(layer, documents=documents)
    result, pullback = jax.vjp(layer_fn, *primals)
    grads = pullback(cotangent.reshape(token_count, D).astype(jnp.float32))
    return (result.astype(jnp.bfloat16).reshape(BLOCKS, BLOCK_LEN, D), grads[0].reshape(BLOCKS, BLOCK_LEN, D), grads[1], grads[2], grads[3], grads[4], grads[5], grads[6], grads[7], grads[8], grads[9], grads[10], grads[11])
```

```python
import functools

import jax
import jax.numpy as jnp
from jax import lax
from jax.experimental import pallas as pl
from jax.experimental.pallas import tpu as pltpu
from jax.sharding import PartitionSpec as P

H = 16
SPAN = 128


EPS = 1e-06
HIGH_PRECISION = lax.Precision.HIGHEST


def from_behind(block, axis, distance):
    devices = range(lax.axis_size(axis))
    route = [(i - distance, i) for i in devices if i - distance in devices]
    return lax.ppermute(block, axis, route)


def normed(entries, gain_vec):
    factor = lax.rsqrt(jnp.mean(entries * entries, axis=-1, keepdims=True) + EPS)
    return entries * factor * gain_vec


def gates(q_part, f_part, gap_piece):
    key_gate = jnp.exp(gap_piece) * jax.nn.sigmoid(-f_part)
    return (jax.nn.silu(q_part), key_gate, jnp.log1p(-key_gate))


def doc_starts(lengths):
    count = lengths.shape[0]
    earlier = lax.broadcasted_iota(jnp.int32, (count, count), 0) > lax.broadcasted_iota(
        jnp.int32, (count, count), 1
    )
    return jnp.sum(jnp.where(earlier, lengths[None, :], 0), axis=1)


def running_sum(rows):
    extent = rows.shape[-2]
    lower = (
        lax.broadcasted_iota(jnp.int32, (extent, extent), 0)
        >= lax.broadcasted_iota(jnp.int32, (extent, extent), 1)
    ).astype(jnp.float32)
    return jnp.einsum("ts,...sk->...tk", lower, rows, precision=HIGH_PRECISION)


def doc_ids(lengths, positions):
    starts = doc_starts(lengths)
    covered = (starts[None, :] <= positions[:, None]).astype(jnp.int32)
    return jnp.sum(covered, axis=1) - 1


def span_step(memory_state, pieces):
    queries, key_gate, value_rows, log_decay, documents, before = pieces
    cumulative = running_sum(log_decay)
    query_decayed = queries * jnp.exp(cumulative)
    k_grown = key_gate * jnp.exp(-cumulative)
    extent = documents.shape[0]
    row_ids = lax.broadcasted_iota(jnp.int32, (extent, extent), 0)
    col_ids = lax.broadcasted_iota(jnp.int32, (extent, extent), 1)
    same_doc = jnp.logical_and(documents[:, None] == documents[None, :], row_ids >= col_ids).astype(
        jnp.float32
    )
    scores = (
        jnp.einsum("hck,hsk->hcs", query_decayed, k_grown, precision=HIGH_PRECISION)
        * same_doc[None]
    )
    within_block = jnp.einsum("hcs,hsv->hcv", scores, value_rows, precision=HIGH_PRECISION)
    carried_state = (documents == before).astype(jnp.float32)[None, :, None]
    output_rows = within_block + carried_state * jnp.einsum(
        "awn,ani->awi", query_decayed, memory_state, precision=HIGH_PRECISION
    )
    last_cum = cumulative[:, -1:, :]
    keep_mask = (documents == documents[-1]).astype(jnp.float32)[None, :, None]
    tail_key_rows = jnp.exp(last_cum - cumulative) * key_gate * keep_mask
    whole_block = (documents[-1] == before).astype(jnp.float32)
    fresh_state = jnp.einsum("wfx,wfg->wxg", tail_key_rows, value_rows, precision=HIGH_PRECISION)
    memory_state = jnp.exp(last_cum[:, 0, :])[:, :, None] * whole_block * memory_state + fresh_state
    return (memory_state, output_rows)


def recur(queries, key_gate, value_rows, log_decay, documents, before, memory_state):
    head_count, extent, columns = queries.shape
    span_count = extent // SPAN

    def by_span(tensor):
        return jnp.swapaxes(tensor.reshape(head_count, span_count, SPAN, tensor.shape[-1]), 0, 1)

    doc_rows = documents.reshape(span_count, SPAN)
    befores = jnp.concatenate([jnp.reshape(before, (1,)), doc_rows[:-1, -1]])
    memory_state, span_out = lax.scan(
        jax.checkpoint(span_step),
        memory_state,
        (
            by_span(queries),
            by_span(key_gate),
            by_span(value_rows),
            by_span(log_decay),
            doc_rows,
            befores,
        ),
    )
    return (
        jnp.swapaxes(span_out, 0, 1).reshape(head_count, extent, value_rows.shape[-1]),
        memory_state,
    )


def spread_cols(weight, copies):
    row_count = weight.shape[0]
    shaped = weight.reshape(row_count, 1, H, weight.shape[1] // H)
    return jnp.broadcast_to(shaped, (row_count, copies, H, shaped.shape[3])).reshape(
        row_count, copies * weight.shape[1]
    )


def fold_copies(received, copies):
    row_count = received.shape[0]
    return jnp.sum(received.reshape(row_count, copies, received.shape[1] // copies), axis=1)


def fan_rows(local_rows):
    blocks_here, row_count, columns = local_rows.shape
    return jnp.broadcast_to(local_rows[:, None], (blocks_here, H, row_count, columns)).reshape(
        blocks_here * H * row_count, columns
    )


def sum_heads(received, blocks_here):
    total_rows, columns = received.shape
    return jnp.sum(
        received.reshape(blocks_here, H, total_rows // (blocks_here * H), columns), axis=1
    )


def times_t(left_mat, right_mat):
    return lax.dot_general(
        left_mat, right_mat, (((1,), (1,)), ((), ())), preferred_element_type=jnp.float32
    )


def outer_sum(left_mat, right_mat):
    return lax.dot_general(
        left_mat, right_mat, (((0,), (0,)), ((), ())), preferred_element_type=jnp.float32
    )


def outer_high(left_mat, right_mat):
    return lax.dot_general(
        left_mat,
        right_mat,
        (((0,), (0,)), ((), ())),
        precision=HIGH_PRECISION,
        preferred_element_type=jnp.float32,
    )


def wide_body(
    inputs,
    cotangent,
    lengths,
    first_gain,
    q_weight,
    f_weight,
    i_weight,
    o_weight,
    group_gain,
    gap_log,
    second_gain,
    gate_weight,
    up_weight,
    down_weight,
):
    hid_size = lax.axis_size("hid")
    per_seq = hid_size // H
    block_total = lax.axis_size("seq") * per_seq
    hid_place = lax.axis_index("hid")
    head_id = hid_place % H
    block_id = lax.axis_index("seq") * per_seq + hid_place // H
    model = inputs.shape[2]
    head_width = model // H
    block_len = hid_size * inputs.shape[1]
    entries = inputs.astype(jnp.float32)
    q_block, f_block, i_block, o_block, gate_block, up_block, down_block = (
        lax.all_to_all(
            spread_cols(q_weight, block_total),
            ("seq", "hid"),
            split_axis=1,
            concat_axis=0,
            tiled=True,
        ),
        lax.all_to_all(
            spread_cols(f_weight, block_total),
            ("seq", "hid"),
            split_axis=1,
            concat_axis=0,
            tiled=True,
        ),
        lax.all_to_all(
            spread_cols(i_weight, block_total),
            ("seq", "hid"),
            split_axis=1,
            concat_axis=0,
            tiled=True,
        ),
        lax.all_to_all(
            spread_cols(o_weight, block_total),
            ("seq", "hid"),
            split_axis=1,
            concat_axis=0,
            tiled=True,
        ),
        lax.all_to_all(
            spread_cols(gate_weight, block_total),
            ("seq", "hid"),
            split_axis=1,
            concat_axis=0,
            tiled=True,
        ),
        lax.all_to_all(
            spread_cols(up_weight, block_total),
            ("seq", "hid"),
            split_axis=1,
            concat_axis=0,
            tiled=True,
        ),
        lax.all_to_all(
            spread_cols(down_weight, block_total),
            ("seq", "hid"),
            split_axis=1,
            concat_axis=0,
            tiled=True,
        ),
    )
    positions = block_id * block_len + lax.iota(jnp.int32, block_len)
    documents = doc_ids(lengths, positions)
    before = doc_ids(lengths, jnp.reshape(block_id * block_len - 1, (1,)))[0]
    first_norm, first_back = jax.vjp(normed, entries, first_gain)
    first_low = first_norm.astype(jnp.bfloat16)
    first_rows = lax.all_to_all(fan_rows(first_low), "hid", split_axis=0, concat_axis=0, tiled=True)
    q_lin = jnp.dot(first_rows, q_block, preferred_element_type=jnp.float32)
    f_lin = jnp.dot(first_rows, f_block, preferred_element_type=jnp.float32)
    i_lin = jnp.dot(first_rows, i_block, preferred_element_type=jnp.float32)
    gap_part = lax.dynamic_slice_in_dim(gap_log, head_id * head_width, head_width)
    queries, key_gate, log_decay = gates(q_lin, f_lin, gap_part)
    cumulative = running_sum(log_decay)
    last_cum = cumulative[-1]
    tail_key_rows = (
        jnp.exp(last_cum[None, :] - cumulative)
        * key_gate
        * (documents == documents[-1]).astype(jnp.float32)[:, None]
    )
    local_state = outer_high(tail_key_rows, i_lin)
    decay = jnp.exp(last_cum) * (documents[-1] == before).astype(jnp.float32)
    state_in = jnp.zeros_like(local_state)
    for number in range(block_total - 1):
        state_out = decay[:, None] * state_in + local_state
        state_in = from_behind(state_out.astype(jnp.bfloat16), ("seq", "hid"), H).astype(
            state_out.dtype
        )

    def core(q_part, f_part, i_part, gap_piece):
        queries_in, keys_in, logs_in = gates(q_part, f_part, gap_piece)
        mixed_all, memory_state = recur(
            queries_in[None],
            keys_in[None],
            i_part[None],
            logs_in[None],
            documents,
            before,
            state_in[None],
        )
        return (mixed_all[0], memory_state[0])

    (mixed_out, _), core_back = jax.vjp(core, q_lin, f_lin, i_lin, gap_part)
    head_normed, norm_back = jax.vjp(normed, mixed_out, group_gain)
    head_low = head_normed.astype(jnp.bfloat16)
    mix_out = sum_heads(
        lax.all_to_all(
            times_t(head_low, o_block).astype(jnp.bfloat16),
            "hid",
            split_axis=0,
            concat_axis=0,
            tiled=True,
        ).astype(jnp.float32),
        per_seq,
    )
    middle = entries + mix_out
    second_norm, second_back = jax.vjp(normed, middle, second_gain)
    second_low = second_norm.astype(jnp.bfloat16)
    second_rows, cot_rows = (
        lax.all_to_all(fan_rows(second_low), "hid", split_axis=0, concat_axis=0, tiled=True),
        lax.all_to_all(fan_rows(cotangent), "hid", split_axis=0, concat_axis=0, tiled=True),
    )
    gate_lin = jnp.dot(second_rows, gate_block, preferred_element_type=jnp.float32)
    up_lin = jnp.dot(second_rows, up_block, preferred_element_type=jnp.float32)
    hidden = (jax.nn.silu(gate_lin) * up_lin).astype(jnp.bfloat16)
    glu_out = sum_heads(
        lax.all_to_all(
            times_t(hidden, down_block).astype(jnp.bfloat16),
            "hid",
            split_axis=0,
            concat_axis=0,
            tiled=True,
        ).astype(jnp.float32),
        per_seq,
    )
    output = (middle + glu_out).astype(jnp.bfloat16)
    down_part = outer_sum(cot_rows, hidden)
    hidden_grad = jnp.dot(cot_rows, down_block, preferred_element_type=jnp.float32)
    gate_sig = jax.nn.sigmoid(gate_lin)
    gate_low = (hidden_grad * up_lin * gate_sig * (1.0 + gate_lin * (1.0 - gate_sig))).astype(
        jnp.bfloat16
    )
    up_low = (hidden_grad * gate_lin * gate_sig).astype(jnp.bfloat16)
    gate_part = outer_sum(second_rows, gate_low)
    up_part = outer_sum(second_rows, up_low)
    second_sum = lax.all_to_all(
        (times_t(gate_low, gate_block) + times_t(up_low, up_block)).astype(jnp.bfloat16),
        "hid",
        split_axis=0,
        concat_axis=0,
        tiled=True,
    ).astype(jnp.float32)
    middle_part, second_part = second_back(sum_heads(second_sum, per_seq))
    middle_grad = cotangent.astype(jnp.float32) + middle_part
    mix_grad = middle_grad.astype(jnp.bfloat16)
    mix_rows = lax.all_to_all(fan_rows(mix_grad), "hid", split_axis=0, concat_axis=0, tiled=True)
    normed_grad = jnp.dot(mix_rows, o_block, preferred_element_type=jnp.float32)
    o_part = outer_sum(mix_rows, head_low)
    mixed_grad, group_part = norm_back(normed_grad)
    carried_state = (documents == before).astype(jnp.float32)[:, None]
    grad_local = outer_high(queries * jnp.exp(cumulative) * carried_state, mixed_grad)
    state_grad = jnp.zeros_like(grad_local)
    for number in range(block_total - 1):
        grad_in = decay[:, None] * state_grad + grad_local
        state_grad = from_behind(grad_in.astype(jnp.bfloat16), ("seq", "hid"), -H).astype(
            grad_in.dtype
        )
    q_grad_lin, f_grad_lin, i_grad_lin, gap_piece_grad = core_back((mixed_grad, state_grad))
    q_low = q_grad_lin.astype(jnp.bfloat16)
    f_low = f_grad_lin.astype(jnp.bfloat16)
    i_low = i_grad_lin.astype(jnp.bfloat16)
    q_part = outer_sum(first_rows, q_low)
    f_part = outer_sum(first_rows, f_low)
    i_part = outer_sum(first_rows, i_low)
    first_sum = lax.all_to_all(
        (times_t(q_low, q_block) + times_t(f_low, f_block) + times_t(i_low, i_block)).astype(
            jnp.bfloat16
        ),
        "hid",
        split_axis=0,
        concat_axis=0,
        tiled=True,
    ).astype(jnp.float32)
    entry_part, first_part = first_back(sum_heads(first_sum, per_seq))
    input_grad = middle_grad + entry_part
    q_back, f_back, i_back, o_back, gate_back, up_back, down_back = (
        lax.all_to_all(
            q_part.astype(jnp.bfloat16), ("seq", "hid"), split_axis=0, concat_axis=1, tiled=True
        ).astype(q_part.dtype),
        lax.all_to_all(
            f_part.astype(jnp.bfloat16), ("seq", "hid"), split_axis=0, concat_axis=1, tiled=True
        ).astype(f_part.dtype),
        lax.all_to_all(
            i_part.astype(jnp.bfloat16), ("seq", "hid"), split_axis=0, concat_axis=1, tiled=True
        ).astype(i_part.dtype),
        lax.all_to_all(
            o_part.astype(jnp.bfloat16), ("seq", "hid"), split_axis=0, concat_axis=1, tiled=True
        ).astype(o_part.dtype),
        lax.all_to_all(
            gate_part.astype(jnp.bfloat16), ("seq", "hid"), split_axis=0, concat_axis=1, tiled=True
        ).astype(gate_part.dtype),
        lax.all_to_all(
            up_part.astype(jnp.bfloat16), ("seq", "hid"), split_axis=0, concat_axis=1, tiled=True
        ).astype(up_part.dtype),
        lax.all_to_all(
            down_part.astype(jnp.bfloat16), ("seq", "hid"), split_axis=0, concat_axis=1, tiled=True
        ).astype(down_part.dtype),
    )
    o_grad = fold_copies(o_back, block_total)
    head_pick = (lax.iota(jnp.int32, H) == head_id).astype(jnp.float32)
    gap_full = (head_pick[:, None] * gap_piece_grad[None, :]).reshape(model)
    first_grad, second_grad, group_grad, gap_grad = lax.psum(
        (first_part, second_part, group_part, gap_full), ("seq", "hid")
    )
    return (
        output,
        input_grad,
        first_grad,
        fold_copies(q_back, block_total),
        fold_copies(f_back, block_total),
        fold_copies(i_back, block_total),
        o_grad,
        group_grad,
        gap_grad,
        second_grad,
        fold_copies(gate_back, block_total),
        fold_copies(up_back, block_total),
        fold_copies(down_back, block_total),
    )


F32 = jnp.float32
BF = jnp.bfloat16
MESH = pl.DeviceIdType.MESH
DMA = pltpu.SemaphoreType.DMA
VMEM = pltpu.VMEM
SUBS = 3
LAG = 2
VSPEC = pl.BlockSpec(memory_space=pltpu.VMEM)
ASPEC = pl.BlockSpec(memory_space=pl.ANY)
SSPEC = pl.BlockSpec(memory_space=pltpu.SMEM)


def place():
    h = lax.axis_index("hid")
    return h, h // 4, lax.rem(h // 2, 2), lax.rem(h, 2)


def partners():
    h, z, y, x = place()
    column = [lax.rem(z + k, 4) * 4 + lax.rem(h, 4) for k in (1, 2, 3)]
    return column, h + 2 - 4 * y, h + 1 - 2 * x


def greet(chips, core=False):
    gate = pltpu.get_barrier_semaphore()
    for chip in chips:
        pl.semaphore_signal(gate, inc=1, device_id={"hid": chip}, device_id_type=MESH)
    if core:
        other = 1 - lax.axis_index("seq")
        pl.semaphore_signal(gate, inc=1, device_id={"seq": other}, device_id_type=MESH)
    pl.semaphore_wait(gate, len(chips) + int(core))


def to_chip(src, dst, send, recv, chip):
    return pltpu.make_async_remote_copy(
        src_ref=src,
        dst_ref=dst,
        send_sem=send,
        recv_sem=recv,
        device_id={"hid": chip},
        device_id_type=MESH,
    )


def to_core(src, dst, send, recv):
    return pltpu.make_async_remote_copy(
        src_ref=src,
        dst_ref=dst,
        send_sem=send,
        recv_sem=recv,
        device_id={"seq": 1 - lax.axis_index("seq")},
        device_id_type=MESH,
    )


def comm_params(collective_id):
    return pltpu.CompilerParams(
        collective_id=collective_id, has_side_effects=True, vmem_limit_bytes=48 << 20
    )


def cut_list():
    return [(i, j) for i in range(SUBS) for j in range(2)]


def gather_kernel(x_ref, o_ref, s1, r1, s2, r2, s3, r3, ls):
    h, z, y, x = place()
    column, py, px = partners()
    rows, half = x_ref.shape[0] // SUBS, x_ref.shape[1] // 2
    greet(column + [py, px])
    cuts = cut_list()

    def cut(i, j):
        return pl.ds(i * rows, rows), pl.ds(j * half, half)

    own = pltpu.make_async_copy(x_ref, o_ref.at[z, y, x], ls)
    own.start()
    c1, c2, c3 = {}, {}, {}
    for c, (i, j) in enumerate(cuts):
        a, b = cut(i, j)
        for k in range(3):
            c1[c, k] = to_chip(
                x_ref.at[a, b], o_ref.at[z, y, x, a, b], s1.at[c, k], r1.at[c, k], column[k]
            )
            c1[c, k].start()
    own.wait()
    n = len(cuts)
    for t in range(n + LAG):
        if t < n:
            i, j = cuts[t]
            a, b = cut(i, j)
            for k in range(3):
                c1[t, k].wait_recv()
            ref = o_ref.at[:, y, x, a, b]
            c2[t] = to_chip(ref, ref, s2.at[t], r2.at[t], py if j else px)
            c2[t].start()
        if t >= LAG:
            c = t - LAG
            i, j = cuts[c]
            a, b = cut(i, j)
            c2[c].wait_recv()
            ref = o_ref.at[:, :, x, a, b] if j else o_ref.at[:, y, :, a, b]
            c3[c] = to_chip(ref, ref, s3.at[c], r3.at[c], px if j else py)
            c3[c].start()
    for c in range(n):
        c3[c].wait_recv()
    for c in range(n):
        for k in range(3):
            c1[c, k].wait_send()
        c2[c].wait_send()
        c3[c].wait_send()


def gather_rows(local, collective_id):
    n = 2 * SUBS
    out = pl.pallas_call(
        gather_kernel,
        out_shape=jax.ShapeDtypeStruct((4, 2, 2) + local.shape, local.dtype),
        in_specs=[VSPEC],
        out_specs=VSPEC,
        scratch_shapes=[DMA((n, 3)), DMA((n, 3)), DMA((n,)), DMA((n,)), DMA((n,)), DMA((n,)), DMA],
        compiler_params=comm_params(collective_id),
    )(local)
    return out.reshape(H * local.shape[0], local.shape[1])


def scatter_kernel(p_ref, o_ref, b1, t1, b2, t2, b3, s1, r1, s2, r2, s3, r3):
    h, z, y, x = place()
    column, py, px = partners()
    rows, half = o_ref.shape[0] // SUBS, o_ref.shape[1] // 2
    greet(column + [py, px])
    cuts = cut_list()

    def cut(i, j):
        return pl.ds(i * rows, rows), pl.ds(j * half, half)

    c1, c2, c3 = {}, {}, {}
    for c, (i, j) in enumerate(cuts):
        a, b = cut(i, j)
        src = p_ref.at[:, :, 1 - x, a, b] if j else p_ref.at[:, 1 - y, :, a, b]
        c1[c] = to_chip(src, b1.at[c], s1.at[c], r1.at[c], px if j else py)
        c1[c].start()

    def second(c):
        i, j = cuts[c]
        a, b = cut(i, j)
        c1[c].wait_recv()
        mine = p_ref[:, :, x, a, b] if j else p_ref[:, y, :, a, b]
        t1[c] = mine.astype(F32) + b1[c].astype(F32)
        q = y if j else x
        b1[c, :, 0] = t1[c, :, 1 - q].astype(BF)
        c2[c] = to_chip(b1.at[c, :, 0], b2.at[c], s2.at[c], r2.at[c], py if j else px)
        c2[c].start()

    def third(c):
        i, j = cuts[c]
        c2[c].wait_recv()
        q = y if j else x
        t2[c] = t1[c, :, q] + b2[c].astype(F32)
        b2[c] = t2[c].astype(BF)
        for k in range(3):
            c3[c, k] = to_chip(
                b2.at[c, lax.rem(z + k + 1, 4)],
                b3.at[c, k],
                s3.at[c, k],
                r3.at[c, k],
                column[k],
            )
            c3[c, k].start()

    def last(c):
        i, j = cuts[c]
        a, b = cut(i, j)
        for k in range(3):
            c3[c, k].wait_recv()
        o_ref[a, b] = t2[c, z] + b3[c, 0].astype(F32) + b3[c, 1].astype(F32) + b3[c, 2].astype(F32)

    n = len(cuts)
    for t in range(n + 2 * LAG):
        if t < n:
            second(t)
        if 0 <= t - LAG < n:
            third(t - LAG)
        if 0 <= t - 2 * LAG < n:
            last(t - 2 * LAG)
    for c in range(n):
        c1[c].wait_send()
        c2[c].wait_send()
        for k in range(3):
            c3[c, k].wait_send()


def scatter_rows(part, collective_id):
    n, rows, cols = 2 * SUBS, part.shape[0] // H, part.shape[1]
    r, w = rows // SUBS, cols // 2
    return pl.pallas_call(
        scatter_kernel,
        out_shape=jax.ShapeDtypeStruct((rows, cols), F32),
        in_specs=[VSPEC],
        out_specs=VSPEC,
        scratch_shapes=[
            VMEM((n, 4, 2, r, w), BF),
            VMEM((n, 4, 2, r, w), F32),
            VMEM((n, 4, r, w), BF),
            VMEM((n, 4, r, w), F32),
            VMEM((n, 3, r, w), BF),
            DMA((n,)),
            DMA((n,)),
            DMA((n,)),
            DMA((n,)),
            DMA((n, 3)),
            DMA((n, 3)),
        ],
        compiler_params=comm_params(collective_id),
    )(part.reshape(4, 2, 2, rows, cols))


def unit_span(tiles, h):
    first = (tiles * h) // H
    return first, (tiles * (h + 1)) // H - first


def lanes(tile, count):
    return pl.ds(pl.multiple_of(tile * 128, 128), count * 128)


def sized(tiles, h, act):
    least = tiles // H
    if tiles % H == 0:
        act(least)
        return
    _, count = unit_span(tiles, h)
    for number in (least, least + 1):
        pl.when(count == number)(functools.partial(act, number))


def weights_kernel(tiles, q, f, i, o, g, u, d, wqfi, wo, wg, wu, wd, ss, rs, ls, xs, xr):
    h, b = lax.axis_index("hid"), lax.axis_index("seq")
    greet([lax.rem(h + k, H) for k in range(1, H)], core=True)
    depth = q.shape[0]
    mine = pl.ds(pl.multiple_of((b * H + h) * depth, depth), depth)
    heads = [(q, wqfi, 0), (f, wqfi, 1), (i, wqfi, 2), (o, wo, 0)]
    units = [(g, wg), (u, wu), (d, wd)]

    def head_copy(n, k, chip):
        src, dst, at = heads[n]
        return to_chip(
            src.at[:, lanes(chip, 1)], dst.at[mine, lanes(at, 1)], ss.at[n, k], rs.at[n, k], chip
        )

    def unit_copy(n, k, chip, count):
        src, dst = units[n]
        first, _ = unit_span(tiles, chip)
        return to_chip(
            src.at[:, lanes(first, count)],
            dst.at[mine, lanes(0, count)],
            ss.at[4 + n, k],
            rs.at[4 + n, k],
            chip,
        )

    for n in range(4):
        for k in range(1, H):
            head_copy(n, k, lax.rem(h + k, H)).start()
    for n in range(3):
        for k in range(1, H):
            chip = lax.rem(h + k, H)
            sized(tiles, chip, lambda count: unit_copy(n, k, chip, count).start())
    own = [
        pltpu.make_async_copy(src.at[:, lanes(h, 1)], dst.at[mine, lanes(at, 1)], ls.at[n])
        for n, (src, dst, at) in enumerate(heads)
    ]
    for copy in own:
        copy.start()

    def own_units(act):
        def run(count):
            for n, (src, dst) in enumerate(units):
                first, _ = unit_span(tiles, h)
                act(
                    pltpu.make_async_copy(
                        src.at[:, lanes(first, count)], dst.at[mine, lanes(0, count)], ls.at[4 + n]
                    )
                )

        sized(tiles, h, run)

    own_units(lambda copy: copy.start())
    wide = wg.shape[1] // 128
    if tiles % H:

        @pl.when(unit_span(tiles, h)[1] < wide)
        def _():
            for _, dst in units:
                dst[:, (wide - 1) * 128 :] = jnp.zeros((dst.shape[0], 128), BF)

    for copy in own:
        copy.wait()
    own_units(lambda copy: copy.wait())
    half = wqfi.shape[0] // 2
    ours = pl.ds(pl.multiple_of(b * half, half), half)
    swaps = []

    def swap(n, ref, cols=None):
        view = ref.at[ours] if cols is None else ref.at[ours, cols]
        copy = to_core(view, view, xs.at[n], xr.at[n])
        copy.start()
        swaps.append(copy)

    for n in range(3):
        for k in range(1, H):
            head_copy(n, k, h).wait_recv()
    swap(0, wqfi)
    for k in range(1, H):
        head_copy(3, k, h).wait_recv()
    swap(1, wo)
    for n in range(3):
        for k in range(1, H):
            sized(tiles, h, lambda count: unit_copy(n, k, h, count).wait_recv())
        least = tiles // H
        if tiles % H == 0:
            swap(2 + n, units[n][1])
        else:
            ref = units[n][1].at[ours, pl.ds(0, least * 128)]
            copy = to_core(ref, ref, xs.at[2 + n], xr.at[2 + n])
            copy.start()
            swaps.append(copy)

            @pl.when(unit_span(tiles, h)[1] > least)
            def _():
                more = units[n][1].at[ours, pl.ds(least * 128, 128)]
                to_core(more, more, xs.at[5 + n], xr.at[5 + n]).start()

    for copy in swaps:
        copy.wait()
    if tiles % H:

        @pl.when(unit_span(tiles, h)[1] > least)
        def _():
            for n in range(3):
                more = units[n][1].at[ours, pl.ds(least * 128, 128)]
                to_core(more, more, xs.at[5 + n], xr.at[5 + n]).wait()

    for n in range(4):
        for k in range(1, H):
            head_copy(n, k, lax.rem(h + k, H)).wait_send()
    for n in range(3):
        for k in range(1, H):
            chip = lax.rem(h + k, H)
            sized(tiles, chip, lambda count: unit_copy(n, k, chip, count).wait_send())


def fetch_weights(weights, collective_id):
    depth, model = weights[0].shape
    rows, tiles = 2 * H * depth, weights[4].shape[1] // 128
    wide = -(-tiles // H) * 128
    shape = lambda cols: jax.ShapeDtypeStruct((rows, cols), BF)
    return pl.pallas_call(
        functools.partial(weights_kernel, tiles),
        out_shape=[shape(384), shape(128), shape(wide), shape(wide), shape(wide)],
        in_specs=[ASPEC] * 7,
        out_specs=[VSPEC] * 5,
        scratch_shapes=[DMA((7, H)), DMA((7, H)), DMA((7,)), DMA((8,)), DMA((8,))],
        compiler_params=comm_params(collective_id),
    )(*weights)


def grads_kernel(tiles, pqfi, po, pg, pu, pd, q, f, i, o, g, u, d, rq, ro, rg, ru, rd, *sems):
    ss, rs, ls, xs, xr = sems
    h, b = lax.axis_index("hid"), lax.axis_index("seq")
    greet([lax.rem(h + k, H) for k in range(1, H)], core=True)
    parts, sums = [pqfi, po, pg, pu, pd], [rq, ro, rg, ru, rd]
    half = pqfi.shape[0] // 2
    ours = pl.ds(pl.multiple_of(b * half, half), half)
    theirs = pl.ds(pl.multiple_of((1 - b) * half, half), half)
    order = [4, 2, 3, 1, 0]
    swaps = {n: to_core(parts[n].at[theirs], sums[n], xs.at[n], xr.at[n]) for n in order}
    for n in order:
        swaps[n].start()
    depth = half // H
    heads = [(rq, 0, q), (rq, 1, f), (rq, 2, i), (ro, 0, o)]
    units = [(rg, g), (ru, u), (rd, d)]

    def rows_of(chip):
        return pl.ds(pl.multiple_of(chip * depth, depth), depth)

    def head_copy(n, k, chip, source):
        src, at, dst = heads[n]
        return to_chip(
            src.at[rows_of(chip), lanes(at, 1)],
            dst.at[:, lanes(source, 1)],
            ss.at[n, k],
            rs.at[n, k],
            chip,
        )

    def unit_copy(n, k, chip, source, count):
        src, dst = units[n]
        first, _ = unit_span(tiles, source)
        return to_chip(
            src.at[rows_of(chip), lanes(0, count)],
            dst.at[:, lanes(first, count)],
            ss.at[4 + n, k],
            rs.at[4 + n, k],
            chip,
        )

    def add(n):
        swaps[n].wait()
        step = 64

        @pl.loop(0, half // step)
        def _(t):
            at = pl.ds(pl.multiple_of(t * step, step), step)
            own = pl.ds(pl.multiple_of(b * half + t * step, step), step)
            sums[n][at] = (sums[n][at].astype(F32) + parts[n][own].astype(F32)).astype(BF)

    def own_heads(ns, act):
        for n in ns:
            src, at, dst = heads[n]
            act(
                pltpu.make_async_copy(
                    src.at[rows_of(h), lanes(at, 1)], dst.at[:, lanes(h, 1)], ls.at[n]
                )
            )

    def own_unit(n, act):
        src, dst = units[n]

        def run(count):
            first, _ = unit_span(tiles, h)
            act(
                pltpu.make_async_copy(
                    src.at[rows_of(h), lanes(0, count)], dst.at[:, lanes(first, count)], ls.at[4 + n]
                )
            )

        sized(tiles, h, run)

    for n in order:
        add(n)
        if n >= 2:
            for k in range(1, H):
                chip = lax.rem(h + k, H)
                sized(tiles, h, lambda count: unit_copy(n - 2, k, chip, h, count).start())
            own_unit(n - 2, lambda copy: copy.start())
        else:
            for m in (3,) if n else (0, 1, 2):
                for k in range(1, H):
                    head_copy(m, k, lax.rem(h + k, H), h).start()
            own_heads((3,) if n else (0, 1, 2), lambda copy: copy.start())
    own_heads(range(4), lambda copy: copy.wait())
    for n in range(3):
        own_unit(n, lambda copy: copy.wait())
    for k in range(1, H):
        chip, source = lax.rem(h + k, H), lax.rem(h + H - k, H)
        for n in range(4):
            head_copy(n, k, chip, source).wait_recv()
            head_copy(n, k, chip, h).wait_send()
        for n in range(3):
            sized(
                tiles, source, lambda count: unit_copy(n, k, chip, source, count).wait_recv()
            )
            sized(tiles, h, lambda count: unit_copy(n, k, chip, h, count).wait_send())


def return_grads(parts, model, units, collective_id):
    rows, tiles = parts[0].shape[0], units // 128
    depth = rows // (2 * H)
    shape = lambda cols: jax.ShapeDtypeStruct((depth, cols), BF)
    return pl.pallas_call(
        functools.partial(grads_kernel, tiles),
        out_shape=[shape(model)] * 4 + [shape(units)] * 3,
        in_specs=[VSPEC] * 5,
        out_specs=[VSPEC] * 7,
        scratch_shapes=[VMEM((rows // 2, p.shape[1]), BF) for p in parts]
        + [DMA((7, H)), DMA((7, H)), DMA((7,)), DMA((5,)), DMA((5,))],
        compiler_params=comm_params(collective_id),
    )(*parts)


def mm(left, right, at_left, at_right):
    return lax.dot_general(
        left.astype(BF),
        right.astype(BF),
        (((at_left,), (at_right,)), ((), ())),
        preferred_element_type=F32,
    )


def tri_sum(rows, reverse=False):
    r = lax.broadcasted_iota(jnp.int32, (SPAN, SPAN), 0)
    c = lax.broadcasted_iota(jnp.int32, (SPAN, SPAN), 1)
    picked = jnp.where((r <= c) if reverse else (r >= c), 1.0, 0.0).astype(BF)
    high = rows.astype(BF)
    rest = rows - high.astype(F32)
    middle = rest.astype(BF)
    low = rest - middle.astype(F32)
    return mm(picked, high, 1, 0) + mm(picked, middle, 1, 0) + mm(picked, low, 1, 0)


def span_gates(lin_ref, gap_ref, at):
    q_lin, f_lin, values = lin_ref[at, 0:128], lin_ref[at, 128:256], lin_ref[at, 256:384]
    s = jax.nn.sigmoid(q_lin)
    key = jnp.exp(gap_ref[...]) * jax.nn.sigmoid(-f_lin)
    return q_lin, f_lin, values, s, key


def span_masks(dcol_ref, drow_ref, marks_ref, c, at):
    r = lax.broadcasted_iota(jnp.int32, (SPAN, SPAN), 0)
    k = lax.broadcasted_iota(jnp.int32, (SPAN, SPAN), 1)
    dcol, drow = dcol_ref[at], drow_ref[c : c + 1]
    before, end = marks_ref[0, c], marks_ref[1, c]
    same = jnp.where(jnp.logical_and(dcol == drow, r >= k), 1.0, 0.0)
    carried = jnp.where(dcol == before, 1.0, 0.0)
    keep = jnp.where(dcol == end, 1.0, 0.0)
    whole = jnp.where(end == before, 1.0, 0.0)
    return same, carried, keep, whole


def spans(extent):
    return [(c, pl.ds(c * SPAN, SPAN)) for c in range(extent // SPAN)]


def mix_kernel(
    lin_ref, gap_ref, gain_ref, dcol_ref, drow_ref, marks_ref,
    mixed_ref, states_ref, head_ref, cum_ref, out_ref, in_ref, send, recv,
):
    greet([], core=True)
    extent = lin_ref.shape[0]
    steps = spans(extent)
    state = jnp.zeros((SPAN, SPAN), F32)
    for c, at in steps:
        q_lin, f_lin, values, s, key = span_gates(lin_ref, gap_ref, at)
        same, carried, keep, whole = span_masks(dcol_ref, drow_ref, marks_ref, c, at)
        cum = tri_sum(jnp.log1p(-key))
        cum_ref[at] = cum
        end = cum[SPAN - 1 : SPAN]
        fresh = mm(values, jnp.exp(end - cum) * key * keep, 0, 0)
        states_ref[c] = fresh
        state = state * (jnp.exp(end) * whole) + fresh
    out_ref[...] = state
    copy = to_core(out_ref, in_ref, send, recv)
    copy.start()
    copy.wait()
    state = in_ref[...] * lax.axis_index("seq").astype(F32)
    for c, at in steps:
        q_lin, f_lin, values, s, key = span_gates(lin_ref, gap_ref, at)
        same, carried, keep, whole = span_masks(dcol_ref, drow_ref, marks_ref, c, at)
        cum = cum_ref[at]
        end = cum[SPAN - 1 : SPAN]
        fresh = states_ref[c]
        states_ref[c] = state
        decayed = q_lin * s * jnp.exp(cum)
        scores = mm(decayed, key * jnp.exp(-cum), 1, 1) * same
        mixed = mm(scores, values, 1, 0) + carried * mm(decayed, state, 1, 1)
        mixed_ref[at] = mixed
        factor = lax.rsqrt(jnp.mean(mixed * mixed, axis=-1, keepdims=True) + EPS)
        head_ref[at] = (mixed * factor * gain_ref[...]).astype(BF)
        state = state * (jnp.exp(end) * whole) + fresh


def mix_forward(lin, gap_row, gain_row, dcol, drow, marks, collective_id):
    extent = lin.shape[0]
    tile = jax.ShapeDtypeStruct((extent, SPAN), F32)
    return pl.pallas_call(
        mix_kernel,
        out_shape=[
            tile,
            jax.ShapeDtypeStruct((extent // SPAN, SPAN, SPAN), F32),
            jax.ShapeDtypeStruct((extent, SPAN), BF),
            tile,
        ],
        in_specs=[VSPEC] * 5 + [SSPEC],
        out_specs=[VSPEC] * 4,
        scratch_shapes=[VMEM((SPAN, SPAN), F32), VMEM((SPAN, SPAN), F32), DMA, DMA],
        compiler_params=comm_params(collective_id),
    )(lin, gap_row, gain_row, dcol, drow, marks)


def unmix_kernel(
    lin_ref, gap_ref, gain_ref, dcol_ref, drow_ref, marks_ref, mixed_ref, states_ref, cum_ref, dhead_ref,
    dlin_ref, gapg_ref, groupg_ref, do_ref, back_ref, out_ref, in_ref, send, recv,
):
    greet([], core=True)
    extent = lin_ref.shape[0]
    steps = spans(extent)
    group = jnp.zeros((1, SPAN), F32)
    adjoint = jnp.zeros((SPAN, SPAN), F32)
    for c, at in reversed(steps):
        mixed, dy = mixed_ref[at], dhead_ref[at]
        factor = lax.rsqrt(jnp.mean(mixed * mixed, axis=-1, keepdims=True) + EPS)
        normal = mixed * factor
        group = group + jnp.sum(dy * normal, axis=0, keepdims=True)
        scaled = dy * gain_ref[...]
        d_mixed = factor * (scaled - normal * jnp.mean(scaled * normal, axis=-1, keepdims=True))
        do_ref[at] = d_mixed
        q_lin, f_lin, values, s, key = span_gates(lin_ref, gap_ref, at)
        same, carried, keep, whole = span_masks(dcol_ref, drow_ref, marks_ref, c, at)
        cum = cum_ref[at]
        back = mm(d_mixed, carried * (q_lin * s * jnp.exp(cum)), 0, 0)
        back_ref[c] = back
        adjoint = adjoint * (jnp.exp(cum[SPAN - 1 : SPAN]) * whole) + back
    groupg_ref[...] = group
    out_ref[...] = adjoint
    copy = to_core(out_ref, in_ref, send, recv)
    copy.start()
    copy.wait()
    adjoint = in_ref[...] * (1 - lax.axis_index("seq")).astype(F32)
    gap = jnp.zeros((1, SPAN), F32)
    for c, at in reversed(steps):
        q_lin, f_lin, values, s, key = span_gates(lin_ref, gap_ref, at)
        same, carried, keep, whole = span_masks(dcol_ref, drow_ref, marks_ref, c, at)
        cum, d_mixed, state = cum_ref[at], do_ref[at], states_ref[c]
        grow, shrink = jnp.exp(-cum), jnp.exp(cum)
        end = cum[SPAN - 1 : SPAN]
        decayed, grown = q_lin * s * shrink, key * grow
        rest = jnp.exp(end - cum) * keep
        tail, through = rest * key, jnp.exp(end) * whole
        scores = mm(decayed, grown, 1, 1) * same
        d_scores = mm(d_mixed, values, 1, 1) * same
        d_values = mm(scores, d_mixed, 0, 0) + mm(tail, adjoint, 1, 1)
        d_decayed = mm(d_scores, grown, 1, 0) + carried * mm(d_mixed, state, 1, 0)
        d_grown = mm(d_scores, decayed, 0, 0)
        d_tail = mm(values, adjoint, 1, 0)
        held = tail * d_tail
        d_cum = decayed * d_decayed - grown * d_grown - held
        d_end = jnp.sum(held, axis=0, keepdims=True) + through * jnp.sum(
            state * adjoint, axis=0, keepdims=True
        )
        d_log = tri_sum(d_cum, reverse=True) + d_end
        d_key = d_grown * grow + d_tail * rest - d_log / (1.0 - key)
        scaled = d_key * key
        gap = gap + jnp.sum(scaled, axis=0, keepdims=True)
        dlin_ref[at, 0:128] = (d_decayed * shrink * s * (1.0 + q_lin * (1.0 - s))).astype(BF)
        dlin_ref[at, 128:256] = (-scaled * jax.nn.sigmoid(f_lin)).astype(BF)
        dlin_ref[at, 256:384] = d_values.astype(BF)
        adjoint = adjoint * through + back_ref[c]
    gapg_ref[...] = gap


def mix_backward(lin, gap_row, gain_row, dcol, drow, marks, mixed, states, cum, d_head, collective_id):
    extent = lin.shape[0]
    row = jax.ShapeDtypeStruct((1, SPAN), F32)
    return pl.pallas_call(
        unmix_kernel,
        out_shape=[jax.ShapeDtypeStruct(lin.shape, BF), row, row],
        in_specs=[VSPEC] * 5 + [SSPEC] + [VSPEC] * 4,
        out_specs=[VSPEC] * 3,
        scratch_shapes=[
            VMEM((extent, SPAN), F32),
            VMEM((extent // SPAN, SPAN, SPAN), F32),
            VMEM((SPAN, SPAN), F32),
            VMEM((SPAN, SPAN), F32),
            DMA,
            DMA,
        ],
        compiler_params=comm_params(collective_id),
    )(lin, gap_row, gain_row, dcol, drow, marks, mixed, states, cum, d_head)


def dot_low(left, right):
    return jnp.dot(left, right, preferred_element_type=F32).astype(BF)


def fast_body(
    inputs,
    cotangent,
    lengths,
    first_gain,
    q_weight,
    f_weight,
    i_weight,
    o_weight,
    group_gain,
    gap_log,
    second_gain,
    gate_weight,
    up_weight,
    down_weight,
):
    rows, model = inputs.shape[1:]
    units = gate_weight.shape[1]
    head_id, block_id = lax.axis_index("hid"), lax.axis_index("seq")
    block_len = H * rows
    entries = inputs[0].astype(F32)
    cot_low = cotangent[0]
    positions = block_id * block_len + lax.iota(jnp.int32, block_len)
    documents = doc_ids(lengths, positions)
    before = doc_ids(lengths, jnp.reshape(block_id * block_len - 1, (1,)))
    drow = documents.reshape(block_len // SPAN, SPAN)
    ends = drow[:, -1]
    marks = jnp.stack([jnp.concatenate([before, ends[:-1]]), ends])
    gap_row = lax.dynamic_slice_in_dim(gap_log, head_id * SPAN, SPAN)[None]
    gain_row = group_gain[None]
    aids = (gap_row, gain_row, documents[:, None], drow, marks)

    first_norm, first_back = jax.vjp(normed, entries, first_gain)
    qfi_block, o_block, gate_block, up_block, down_block = fetch_weights(
        (q_weight, f_weight, i_weight, o_weight, gate_weight, up_weight, down_weight), 1
    )
    first_rows = gather_rows(first_norm.astype(BF), 2)
    cot_rows = gather_rows(cot_low, 2)
    lin = jnp.dot(first_rows, qfi_block, preferred_element_type=F32)
    mixed, states, head_low, cum = mix_forward(lin, *aids, 3)
    mix_out = scatter_rows(times_t(head_low, o_block).astype(BF), 4)
    middle = entries + mix_out
    second_norm, second_back = jax.vjp(normed, middle, second_gain)
    second_rows = gather_rows(second_norm.astype(BF), 2)
    gate_lin = jnp.dot(second_rows, gate_block, preferred_element_type=F32)
    up_lin = jnp.dot(second_rows, up_block, preferred_element_type=F32)
    gate_sig = jax.nn.sigmoid(gate_lin)
    hidden = (gate_lin * gate_sig * up_lin).astype(BF)
    hidden_grad = jnp.dot(cot_rows, down_block, preferred_element_type=F32)
    gate_low = (hidden_grad * up_lin * gate_sig * (1.0 + gate_lin * (1.0 - gate_sig))).astype(BF)
    up_low = (hidden_grad * gate_lin * gate_sig).astype(BF)
    second_sum = scatter_rows(
        (times_t(gate_low, gate_block) + times_t(up_low, up_block)).astype(BF), 4
    )
    middle_part, second_part = second_back(second_sum)
    middle_grad = cot_low.astype(F32) + middle_part
    mix_rows = gather_rows(middle_grad.astype(BF), 2)
    d_head = jnp.dot(mix_rows, o_block, preferred_element_type=F32)
    d_lin, gap_part, group_part = mix_backward(lin, *aids, mixed, states, cum, d_head, 5)
    first_sum = scatter_rows(times_t(d_lin, qfi_block).astype(BF), 4)
    entry_part, first_part = first_back(first_sum)
    input_grad = middle_grad + entry_part
    glu_out = scatter_rows(times_t(hidden, down_block).astype(BF), 4)
    output = (middle + glu_out).astype(BF)
    grads = return_grads(
        (
            outer_sum(first_rows, d_lin).astype(BF),
            outer_sum(mix_rows, head_low).astype(BF),
            outer_sum(second_rows, gate_low).astype(BF),
            outer_sum(second_rows, up_low).astype(BF),
            outer_sum(cot_rows, hidden).astype(BF),
        ),
        model,
        units,
        6,
    )
    q_grad, f_grad, i_grad, o_grad, gate_grad, up_grad, down_grad = (
        grad.astype(F32) for grad in grads
    )
    head_pick = (lax.iota(jnp.int32, H) == head_id).astype(F32)
    gap_full = (head_pick[:, None] * gap_part).reshape(model)
    first_grad, second_grad, group_grad, gap_grad = lax.psum(
        (first_part, second_part, group_part[0], gap_full), ("seq", "hid")
    )
    return (
        output[None],
        input_grad[None],
        first_grad,
        q_grad,
        f_grad,
        i_grad,
        o_grad,
        group_grad,
        gap_grad,
        second_grad,
        gate_grad,
        up_grad,
        down_grad,
    )


def solution(mesh):
    placed = (
        P("seq", "hid", None),
        P("seq", "hid", None),
        P(),
        P(),
        P(("seq", "hid"), None),
        P(("seq", "hid"), None),
        P(("seq", "hid"), None),
        P(("seq", "hid"), None),
        P(),
        P(),
        P(),
        P(("seq", "hid"), None),
        P(("seq", "hid"), None),
        P(("seq", "hid"), None),
    )
    body = fast_body if mesh.shape["hid"] == H else wide_body
    return jax.shard_map(
        body,
        mesh=mesh,
        in_specs=placed,
        out_specs=(
            P("seq", "hid", None),
            P("seq", "hid", None),
            P(),
            P(("seq", "hid"), None),
            P(("seq", "hid"), None),
            P(("seq", "hid"), None),
            P(("seq", "hid"), None),
            P(),
            P(),
            P(),
            P(("seq", "hid"), None),
            P(("seq", "hid"), None),
            P(("seq", "hid"), None),
        ),
        check_vma=False,
    )
```

```python
import functools

import jax
import jax.numpy as jnp
from jax import lax
from jax.experimental import pallas as pl
from jax.experimental.pallas import tpu as pltpu
from jax.sharding import PartitionSpec as P

H = 16
SPAN = 128


EPS = 1e-06
HIGH_PRECISION = lax.Precision.HIGHEST


def from_behind(block, axis, distance):
    devices = range(lax.axis_size(axis))
    route = [(i - distance, i) for i in devices if i - distance in devices]
    return lax.ppermute(block, axis, route)


def normed(entries, gain_vec):
    factor = lax.rsqrt(jnp.mean(entries * entries, axis=-1, keepdims=True) + EPS)
    return entries * factor * gain_vec


def gates(q_part, f_part, gap_piece):
    key_gate = jnp.exp(gap_piece) * jax.nn.sigmoid(-f_part)
    return (jax.nn.silu(q_part), key_gate, jnp.log1p(-key_gate))


def doc_starts(lengths):
    count = lengths.shape[0]
    earlier = lax.broadcasted_iota(jnp.int32, (count, count), 0) > lax.broadcasted_iota(
        jnp.int32, (count, count), 1
    )
    return jnp.sum(jnp.where(earlier, lengths[None, :], 0), axis=1)


def running_sum(rows):
    extent = rows.shape[-2]
    lower = (
        lax.broadcasted_iota(jnp.int32, (extent, extent), 0)
        >= lax.broadcasted_iota(jnp.int32, (extent, extent), 1)
    ).astype(jnp.float32)
    return jnp.einsum("ts,...sk->...tk", lower, rows, precision=HIGH_PRECISION)


def doc_ids(lengths, positions):
    starts = doc_starts(lengths)
    covered = (starts[None, :] <= positions[:, None]).astype(jnp.int32)
    return jnp.sum(covered, axis=1) - 1


def span_step(memory_state, pieces):
    queries, key_gate, value_rows, log_decay, documents, before = pieces
    cumulative = running_sum(log_decay)
    query_decayed = queries * jnp.exp(cumulative)
    k_grown = key_gate * jnp.exp(-cumulative)
    extent = documents.shape[0]
    row_ids = lax.broadcasted_iota(jnp.int32, (extent, extent), 0)
    col_ids = lax.broadcasted_iota(jnp.int32, (extent, extent), 1)
    same_doc = jnp.logical_and(documents[:, None] == documents[None, :], row_ids >= col_ids).astype(
        jnp.float32
    )
    scores = (
        jnp.einsum("hck,hsk->hcs", query_decayed, k_grown, precision=HIGH_PRECISION)
        * same_doc[None]
    )
    within_block = jnp.einsum("hcs,hsv->hcv", scores, value_rows, precision=HIGH_PRECISION)
    carried_state = (documents == before).astype(jnp.float32)[None, :, None]
    output_rows = within_block + carried_state * jnp.einsum(
        "awn,ani->awi", query_decayed, memory_state, precision=HIGH_PRECISION
    )
    last_cum = cumulative[:, -1:, :]
    keep_mask = (documents == documents[-1]).astype(jnp.float32)[None, :, None]
    tail_key_rows = jnp.exp(last_cum - cumulative) * key_gate * keep_mask
    whole_block = (documents[-1] == before).astype(jnp.float32)
    fresh_state = jnp.einsum("wfx,wfg->wxg", tail_key_rows, value_rows, precision=HIGH_PRECISION)
    memory_state = jnp.exp(last_cum[:, 0, :])[:, :, None] * whole_block * memory_state + fresh_state
    return (memory_state, output_rows)


def recur(queries, key_gate, value_rows, log_decay, documents, before, memory_state):
    head_count, extent, columns = queries.shape
    span_count = extent // SPAN

    def by_span(tensor):
        return jnp.swapaxes(tensor.reshape(head_count, span_count, SPAN, tensor.shape[-1]), 0, 1)

    doc_rows = documents.reshape(span_count, SPAN)
    befores = jnp.concatenate([jnp.reshape(before, (1,)), doc_rows[:-1, -1]])
    memory_state, span_out = lax.scan(
        jax.checkpoint(span_step),
        memory_state,
        (
            by_span(queries),
            by_span(key_gate),
            by_span(value_rows),
            by_span(log_decay),
            doc_rows,
            befores,
        ),
    )
    return (
        jnp.swapaxes(span_out, 0, 1).reshape(head_count, extent, value_rows.shape[-1]),
        memory_state,
    )


def spread_cols(weight, copies):
    row_count = weight.shape[0]
    shaped = weight.reshape(row_count, 1, H, weight.shape[1] // H)
    return jnp.broadcast_to(shaped, (row_count, copies, H, shaped.shape[3])).reshape(
        row_count, copies * weight.shape[1]
    )


def fold_copies(received, copies):
    row_count = received.shape[0]
    return jnp.sum(received.reshape(row_count, copies, received.shape[1] // copies), axis=1)


def fan_rows(local_rows):
    blocks_here, row_count, columns = local_rows.shape
    return jnp.broadcast_to(local_rows[:, None], (blocks_here, H, row_count, columns)).reshape(
        blocks_here * H * row_count, columns
    )


def sum_heads(received, blocks_here):
    total_rows, columns = received.shape
    return jnp.sum(
        received.reshape(blocks_here, H, total_rows // (blocks_here * H), columns), axis=1
    )


def times_t(left_mat, right_mat):
    return lax.dot_general(
        left_mat, right_mat, (((1,), (1,)), ((), ())), preferred_element_type=jnp.float32
    )


def outer_sum(left_mat, right_mat):
    return lax.dot_general(
        left_mat, right_mat, (((0,), (0,)), ((), ())), preferred_element_type=jnp.float32
    )


def outer_high(left_mat, right_mat):
    return lax.dot_general(
        left_mat,
        right_mat,
        (((0,), (0,)), ((), ())),
        precision=HIGH_PRECISION,
        preferred_element_type=jnp.float32,
    )


def wide_body(
    inputs,
    cotangent,
    lengths,
    first_gain,
    q_weight,
    f_weight,
    i_weight,
    o_weight,
    group_gain,
    gap_log,
    second_gain,
    gate_weight,
    up_weight,
    down_weight,
):
    hid_size = lax.axis_size("hid")
    per_seq = hid_size // H
    block_total = lax.axis_size("seq") * per_seq
    hid_place = lax.axis_index("hid")
    head_id = hid_place % H
    block_id = lax.axis_index("seq") * per_seq + hid_place // H
    model = inputs.shape[2]
    head_width = model // H
    block_len = hid_size * inputs.shape[1]
    entries = inputs.astype(jnp.float32)
    q_block, f_block, i_block, o_block, gate_block, up_block, down_block = (
        lax.all_to_all(
            spread_cols(q_weight, block_total),
            ("seq", "hid"),
            split_axis=1,
            concat_axis=0,
            tiled=True,
        ),
        lax.all_to_all(
            spread_cols(f_weight, block_total),
            ("seq", "hid"),
            split_axis=1,
            concat_axis=0,
            tiled=True,
        ),
        lax.all_to_all(
            spread_cols(i_weight, block_total),
            ("seq", "hid"),
            split_axis=1,
            concat_axis=0,
            tiled=True,
        ),
        lax.all_to_all(
            spread_cols(o_weight, block_total),
            ("seq", "hid"),
            split_axis=1,
            concat_axis=0,
            tiled=True,
        ),
        lax.all_to_all(
            spread_cols(gate_weight, block_total),
            ("seq", "hid"),
            split_axis=1,
            concat_axis=0,
            tiled=True,
        ),
        lax.all_to_all(
            spread_cols(up_weight, block_total),
            ("seq", "hid"),
            split_axis=1,
            concat_axis=0,
            tiled=True,
        ),
        lax.all_to_all(
            spread_cols(down_weight, block_total),
            ("seq", "hid"),
            split_axis=1,
            concat_axis=0,
            tiled=True,
        ),
    )
    positions = block_id * block_len + lax.iota(jnp.int32, block_len)
    documents = doc_ids(lengths, positions)
    before = doc_ids(lengths, jnp.reshape(block_id * block_len - 1, (1,)))[0]
    first_norm, first_back = jax.vjp(normed, entries, first_gain)
    first_low = first_norm.astype(jnp.bfloat16)
    first_rows = lax.all_to_all(fan_rows(first_low), "hid", split_axis=0, concat_axis=0, tiled=True)
    q_lin = jnp.dot(first_rows, q_block, preferred_element_type=jnp.float32)
    f_lin = jnp.dot(first_rows, f_block, preferred_element_type=jnp.float32)
    i_lin = jnp.dot(first_rows, i_block, preferred_element_type=jnp.float32)
    gap_part = lax.dynamic_slice_in_dim(gap_log, head_id * head_width, head_width)
    queries, key_gate, log_decay = gates(q_lin, f_lin, gap_part)
    cumulative = running_sum(log_decay)
    last_cum = cumulative[-1]
    tail_key_rows = (
        jnp.exp(last_cum[None, :] - cumulative)
        * key_gate
        * (documents == documents[-1]).astype(jnp.float32)[:, None]
    )
    local_state = outer_high(tail_key_rows, i_lin)
    decay = jnp.exp(last_cum) * (documents[-1] == before).astype(jnp.float32)
    state_in = jnp.zeros_like(local_state)
    for number in range(block_total - 1):
        state_out = decay[:, None] * state_in + local_state
        state_in = from_behind(state_out.astype(jnp.bfloat16), ("seq", "hid"), H).astype(
            state_out.dtype
        )

    def core(q_part, f_part, i_part, gap_piece):
        queries_in, keys_in, logs_in = gates(q_part, f_part, gap_piece)
        mixed_all, memory_state = recur(
            queries_in[None],
            keys_in[None],
            i_part[None],
            logs_in[None],
            documents,
            before,
            state_in[None],
        )
        return (mixed_all[0], memory_state[0])

    (mixed_out, _), core_back = jax.vjp(core, q_lin, f_lin, i_lin, gap_part)
    head_normed, norm_back = jax.vjp(normed, mixed_out, group_gain)
    head_low = head_normed.astype(jnp.bfloat16)
    mix_out = sum_heads(
        lax.all_to_all(
            times_t(head_low, o_block).astype(jnp.bfloat16),
            "hid",
            split_axis=0,
            concat_axis=0,
            tiled=True,
        ).astype(jnp.float32),
        per_seq,
    )
    middle = entries + mix_out
    second_norm, second_back = jax.vjp(normed, middle, second_gain)
    second_low = second_norm.astype(jnp.bfloat16)
    second_rows, cot_rows = (
        lax.all_to_all(fan_rows(second_low), "hid", split_axis=0, concat_axis=0, tiled=True),
        lax.all_to_all(fan_rows(cotangent), "hid", split_axis=0, concat_axis=0, tiled=True),
    )
    gate_lin = jnp.dot(second_rows, gate_block, preferred_element_type=jnp.float32)
    up_lin = jnp.dot(second_rows, up_block, preferred_element_type=jnp.float32)
    hidden = (jax.nn.silu(gate_lin) * up_lin).astype(jnp.bfloat16)
    glu_out = sum_heads(
        lax.all_to_all(
            times_t(hidden, down_block).astype(jnp.bfloat16),
            "hid",
            split_axis=0,
            concat_axis=0,
            tiled=True,
        ).astype(jnp.float32),
        per_seq,
    )
    output = (middle + glu_out).astype(jnp.bfloat16)
    down_part = outer_sum(cot_rows, hidden)
    hidden_grad = jnp.dot(cot_rows, down_block, preferred_element_type=jnp.float32)
    gate_sig = jax.nn.sigmoid(gate_lin)
    gate_low = (hidden_grad * up_lin * gate_sig * (1.0 + gate_lin * (1.0 - gate_sig))).astype(
        jnp.bfloat16
    )
    up_low = (hidden_grad * gate_lin * gate_sig).astype(jnp.bfloat16)
    gate_part = outer_sum(second_rows, gate_low)
    up_part = outer_sum(second_rows, up_low)
    second_sum = lax.all_to_all(
        (times_t(gate_low, gate_block) + times_t(up_low, up_block)).astype(jnp.bfloat16),
        "hid",
        split_axis=0,
        concat_axis=0,
        tiled=True,
    ).astype(jnp.float32)
    middle_part, second_part = second_back(sum_heads(second_sum, per_seq))
    middle_grad = cotangent.astype(jnp.float32) + middle_part
    mix_grad = middle_grad.astype(jnp.bfloat16)
    mix_rows = lax.all_to_all(fan_rows(mix_grad), "hid", split_axis=0, concat_axis=0, tiled=True)
    normed_grad = jnp.dot(mix_rows, o_block, preferred_element_type=jnp.float32)
    o_part = outer_sum(mix_rows, head_low)
    mixed_grad, group_part = norm_back(normed_grad)
    carried_state = (documents == before).astype(jnp.float32)[:, None]
    grad_local = outer_high(queries * jnp.exp(cumulative) * carried_state, mixed_grad)
    state_grad = jnp.zeros_like(grad_local)
    for number in range(block_total - 1):
        grad_in = decay[:, None] * state_grad + grad_local
        state_grad = from_behind(grad_in.astype(jnp.bfloat16), ("seq", "hid"), -H).astype(
            grad_in.dtype
        )
    q_grad_lin, f_grad_lin, i_grad_lin, gap_piece_grad = core_back((mixed_grad, state_grad))
    q_low = q_grad_lin.astype(jnp.bfloat16)
    f_low = f_grad_lin.astype(jnp.bfloat16)
    i_low = i_grad_lin.astype(jnp.bfloat16)
    q_part = outer_sum(first_rows, q_low)
    f_part = outer_sum(first_rows, f_low)
    i_part = outer_sum(first_rows, i_low)
    first_sum = lax.all_to_all(
        (times_t(q_low, q_block) + times_t(f_low, f_block) + times_t(i_low, i_block)).astype(
            jnp.bfloat16
        ),
        "hid",
        split_axis=0,
        concat_axis=0,
        tiled=True,
    ).astype(jnp.float32)
    entry_part, first_part = first_back(sum_heads(first_sum, per_seq))
    input_grad = middle_grad + entry_part
    q_back, f_back, i_back, o_back, gate_back, up_back, down_back = (
        lax.all_to_all(
            q_part.astype(jnp.bfloat16), ("seq", "hid"), split_axis=0, concat_axis=1, tiled=True
        ).astype(q_part.dtype),
        lax.all_to_all(
            f_part.astype(jnp.bfloat16), ("seq", "hid"), split_axis=0, concat_axis=1, tiled=True
        ).astype(f_part.dtype),
        lax.all_to_all(
            i_part.astype(jnp.bfloat16), ("seq", "hid"), split_axis=0, concat_axis=1, tiled=True
        ).astype(i_part.dtype),
        lax.all_to_all(
            o_part.astype(jnp.bfloat16), ("seq", "hid"), split_axis=0, concat_axis=1, tiled=True
        ).astype(o_part.dtype),
        lax.all_to_all(
            gate_part.astype(jnp.bfloat16), ("seq", "hid"), split_axis=0, concat_axis=1, tiled=True
        ).astype(gate_part.dtype),
        lax.all_to_all(
            up_part.astype(jnp.bfloat16), ("seq", "hid"), split_axis=0, concat_axis=1, tiled=True
        ).astype(up_part.dtype),
        lax.all_to_all(
            down_part.astype(jnp.bfloat16), ("seq", "hid"), split_axis=0, concat_axis=1, tiled=True
        ).astype(down_part.dtype),
    )
    o_grad = fold_copies(o_back, block_total)
    head_pick = (lax.iota(jnp.int32, H) == head_id).astype(jnp.float32)
    gap_full = (head_pick[:, None] * gap_piece_grad[None, :]).reshape(model)
    first_grad, second_grad, group_grad, gap_grad = lax.psum(
        (first_part, second_part, group_part, gap_full), ("seq", "hid")
    )
    return (
        output,
        input_grad,
        first_grad,
        fold_copies(q_back, block_total),
        fold_copies(f_back, block_total),
        fold_copies(i_back, block_total),
        o_grad,
        group_grad,
        gap_grad,
        second_grad,
        fold_copies(gate_back, block_total),
        fold_copies(up_back, block_total),
        fold_copies(down_back, block_total),
    )


F32 = jnp.float32
BF = jnp.bfloat16
MESH = pl.DeviceIdType.MESH
DMA = pltpu.SemaphoreType.DMA
VMEM = pltpu.VMEM
PIECES = 3
PARTS = 4
CUTS = PIECES * PARTS
AHEAD = (4, 4, 4, 4)
PACE = (4, 5)
VSPEC = pl.BlockSpec(memory_space=pltpu.VMEM)
ASPEC = pl.BlockSpec(memory_space=pl.ANY)
SSPEC = pl.BlockSpec(memory_space=pltpu.SMEM)


def place():
    h = lax.axis_index("hid")
    return h, h // 4, lax.rem(h // 2, 2), lax.rem(h, 2)


def partners():
    h, z, y, x = place()
    column = [lax.rem(z + k, 4) * 4 + lax.rem(h, 4) for k in (1, 2, 3)]
    return column, h + 2 - 4 * y, h + 1 - 2 * x


def greet(chips, core=False):
    gate = pltpu.get_barrier_semaphore()
    for chip in chips:
        pl.semaphore_signal(gate, inc=1, device_id={"hid": chip}, device_id_type=MESH)
    if core:
        other = 1 - lax.axis_index("seq")
        pl.semaphore_signal(gate, inc=1, device_id={"seq": other}, device_id_type=MESH)
    pl.semaphore_wait(gate, len(chips) + int(core))


def to_chip(src, dst, send, recv, chip):
    return pltpu.make_async_remote_copy(
        src_ref=src,
        dst_ref=dst,
        send_sem=send,
        recv_sem=recv,
        device_id={"hid": chip},
        device_id_type=MESH,
    )


def to_core(src, dst, send, recv):
    return pltpu.make_async_remote_copy(
        src_ref=src,
        dst_ref=dst,
        send_sem=send,
        recv_sem=recv,
        device_id={"seq": 1 - lax.axis_index("seq")},
        device_id_type=MESH,
    )


def comm_params(collective_id):
    return pltpu.CompilerParams(
        collective_id=collective_id, has_side_effects=True, vmem_limit_bytes=56 << 20
    )


class Cuts:
    def cut(self, c):
        i, j = c // PARTS, c % PARTS
        rows, cols = self.ref.shape[3] // PIECES, self.ref.shape[4] // PARTS
        return pl.ds(i * rows, rows), pl.ds(j * cols, cols), j % 2


class Gather(Cuts):
    def __init__(self, ref, sems):
        self.ref, self.sems = ref, sems
        self.one, self.two, self.three = {}, {}, {}

    def start(self, c):
        h, z, y, x = place()
        column, py, px = partners()
        a, b, j = self.cut(c)
        ref = self.ref.at[z, y, x, a, b]
        for k in range(3):
            self.one[c, k] = to_chip(
                ref, ref, self.sems[0].at[c, k], self.sems[1].at[c, k], column[k]
            )
            self.one[c, k].start()

    def second(self, c):
        h, z, y, x = place()
        column, py, px = partners()
        a, b, j = self.cut(c)
        for k in range(3):
            self.one[c, k].wait_recv()
        ref = self.ref.at[:, y, x, a, b]
        self.two[c] = to_chip(ref, ref, self.sems[2].at[c], self.sems[3].at[c], py if j else px)
        self.two[c].start()

    def third(self, c):
        h, z, y, x = place()
        column, py, px = partners()
        a, b, j = self.cut(c)
        self.two[c].wait_recv()
        ref = self.ref.at[:, :, x, a, b] if j else self.ref.at[:, y, :, a, b]
        self.three[c] = to_chip(ref, ref, self.sems[4].at[c], self.sems[5].at[c], px if j else py)
        self.three[c].start()

    def finish(self):
        for c in self.three:
            self.three[c].wait_recv()
        for c in self.three:
            for k in range(3):
                self.one[c, k].wait_send()
            self.two[c].wait_send()
            self.three[c].wait_send()


def gather_sems():
    n = CUTS
    return [DMA((n, 3)), DMA((n, 3)), DMA((n,)), DMA((n,)), DMA((n,)), DMA((n,))]


class Scatter(Cuts):
    def __init__(self, ref, scratch):
        self.ref, self.bufs, self.sems = ref, scratch[:5], scratch[5:]
        self.one, self.two, self.three = {}, {}, {}

    def start(self, c):
        h, z, y, x = place()
        column, py, px = partners()
        a, b, j = self.cut(c)
        src = self.ref.at[:, :, 1 - x, a, b] if j else self.ref.at[:, 1 - y, :, a, b]
        self.one[c] = to_chip(
            src, self.bufs[0].at[c], self.sems[0].at[c], self.sems[1].at[c], px if j else py
        )
        self.one[c].start()

    def second(self, c):
        h, z, y, x = place()
        column, py, px = partners()
        b1, t1, b2 = self.bufs[:3]
        a, b, j = self.cut(c)
        q = y if j else x
        self.one[c].wait_recv()
        theirs = self.ref[:, 1 - q, x, a, b] if j else self.ref[:, y, 1 - q, a, b]
        b1[c, :, 1 - q] = (theirs.astype(F32) + b1[c, :, 1 - q].astype(F32)).astype(BF)
        self.two[c] = to_chip(
            b1.at[c, :, 1 - q], b2.at[c], self.sems[2].at[c], self.sems[3].at[c], py if j else px
        )
        self.two[c].start()
        mine = self.ref[:, q, x, a, b] if j else self.ref[:, y, q, a, b]
        t1[c] = mine.astype(F32) + b1[c, :, q].astype(F32)

    def third(self, c):
        h, z, y, x = place()
        column, py, px = partners()
        b1, t1, b2, t2, b3 = self.bufs
        self.two[c].wait_recv()
        t2[c] = t1[c] + b2[c].astype(F32)
        b2[c] = t2[c].astype(BF)
        for k in range(3):
            self.three[c, k] = to_chip(
                b2.at[c, lax.rem(z + k + 1, 4)],
                b3.at[c, k],
                self.sems[4].at[c, k],
                self.sems[5].at[c, k],
                column[k],
            )
            self.three[c, k].start()

    def last(self, c):
        h, z, y, x = place()
        b3, t2 = self.bufs[4], self.bufs[3]
        for k in range(3):
            self.three[c, k].wait_recv()
        return t2[c, z] + b3[c, 0].astype(F32) + b3[c, 1].astype(F32) + b3[c, 2].astype(F32)

    def finish(self):
        for c in self.one:
            self.one[c].wait_send()
            self.two[c].wait_send()
            for k in range(3):
                self.three[c, k].wait_send()


def scatter_scratch(rows, cols):
    n, r, w = CUTS, rows // PIECES, cols // PARTS
    return [
        VMEM((n, 4, 2, r, w), BF),
        VMEM((n, 4, r, w), F32),
        VMEM((n, 4, r, w), BF),
        VMEM((n, 4, r, w), F32),
        VMEM((n, 3, r, w), BF),
        DMA((n,)),
        DMA((n,)),
        DMA((n,)),
        DMA((n,)),
        DMA((n, 3)),
        DMA((n, 3)),
    ]


def all_chips():
    h = lax.axis_index("hid")
    return [lax.rem(h + k, H) for k in range(1, H)]


class Queue:
    def __init__(self, jobs):
        self.jobs = list(jobs)

    def run(self, number):
        for job in self.jobs[:number]:
            job()
        self.jobs = self.jobs[number:]


def unit_span(tiles, h):
    first = (tiles * h) // H
    return first, (tiles * (h + 1)) // H - first


def lanes(tile, count):
    return pl.ds(pl.multiple_of(tile * 128, 128), count * 128)


class Bulk:
    def __init__(self, items, tiles, depth, sems):
        self.items, self.tiles, self.depth = items, tiles, depth
        self.ss, self.rs, self.ls, self.xs, self.xr = sems
        self.least = tiles // H

    def sized(self, n, chip, act):
        if not self.items[n][3]:
            act(chip, 1)
            return
        first, count = unit_span(self.tiles, chip)
        if self.tiles % H == 0:
            act(first, self.least)
            return
        for number in (self.least, self.least + 1):
            pl.when(count == number)(functools.partial(act, first, number))

    def ours(self, view):
        half = H * self.depth
        return pl.ds(pl.multiple_of(view * half, half), half)

    def row(self, core, chip):
        return pl.ds(pl.multiple_of((core * H + chip) * self.depth, self.depth), self.depth)


class Fetch(Bulk):
    def copy(self, n, k, chip, first, count):
        h, b = lax.axis_index("hid"), lax.axis_index("seq")
        src, dst, at, _ = self.items[n]
        return to_chip(
            src.at[:, lanes(first, count)],
            dst.at[self.row(b, h), lanes(at, count)],
            self.ss.at[n, k],
            self.rs.at[n, k],
            chip,
        )

    def own(self, n, first, count):
        h, b = lax.axis_index("hid"), lax.axis_index("seq")
        src, dst, at, _ = self.items[n]
        return pltpu.make_async_copy(
            src.at[:, lanes(first, count)], dst.at[self.row(b, h), lanes(at, count)], self.ls.at[n]
        )

    def job(self, n, k):
        def run():
            chip = lax.rem(lax.axis_index("hid") + k, H)
            self.sized(
                n, chip, lambda first, count: self.copy(n, k, chip, first, count).start()
            )

        return run

    def jobs(self):
        return [self.job(n, k) for n in range(len(self.items)) for k in range(1, H)]

    def start_own(self):
        h = lax.axis_index("hid")
        for n, (_, dst, _, split) in enumerate(self.items):
            self.sized(n, h, lambda first, count: self.own(n, first, count).start())
            if split and self.tiles % H:

                @pl.when(unit_span(self.tiles, h)[1] == self.least)
                def _():
                    dst[:, self.least * 128 :] = jnp.zeros((dst.shape[0], 128), BF)

    def swap(self, n, tile, count, slot):
        b = lax.axis_index("seq")
        view = self.items[n][1].at[self.ours(b), lanes(tile, count)]
        return to_core(view, view, self.xs.at[n, slot], self.xr.at[n, slot])

    def each_swap(self, n, act):
        at, split = self.items[n][2:]
        act(self.swap(n, at, self.least if split else 1, 0))
        if split and self.tiles % H:

            @pl.when(unit_span(self.tiles, lax.axis_index("hid"))[1] > self.least)
            def _():
                act(self.swap(n, self.least, 1, 1))

    def arrive(self, n):
        h = lax.axis_index("hid")
        self.sized(n, h, lambda first, count: self.own(n, first, count).wait())
        for k in range(1, H):
            self.sized(
                n, h, lambda first, count: self.copy(n, k, h, first, count).wait_recv()
            )
        self.each_swap(n, lambda copy: copy.start())

    def finish(self):
        for n in range(len(self.items)):
            self.each_swap(n, lambda copy: copy.wait())
            for k in range(1, H):
                chip = lax.rem(lax.axis_index("hid") + k, H)
                self.sized(
                    n, chip, lambda first, count: self.copy(n, k, chip, first, count).wait_send()
                )


class Return(Bulk):
    def __init__(self, items, parts, tiles, depth, sems):
        super().__init__(items, tiles, depth, sems)
        self.parts = parts

    def swap(self, p):
        part, total, _ = self.parts[p]
        return to_core(
            part.at[self.ours(1 - lax.axis_index("seq"))], total, self.xs.at[p, 0], self.xr.at[p, 0]
        )

    def start_swaps(self):
        for p in range(len(self.parts)):
            self.swap(p).start()

    def add(self, p):
        def run():
            part, total, _ = self.parts[p]
            b = lax.axis_index("seq")
            self.swap(p).wait()
            half, step = total.shape[0], 128

            @pl.loop(0, half // step)
            def _(t):
                at = pl.ds(pl.multiple_of(t * step, step), step)
                own = pl.ds(pl.multiple_of(b * half + t * step, step), step)
                total[at] = (total[at].astype(F32) + part[own].astype(F32)).astype(BF)

            for n in self.parts[p][2]:
                h = lax.axis_index("hid")
                self.sized(n, h, lambda first, count: self.own(n, first, count).start())

        return run

    def copy(self, n, k, chip, first, count):
        dst, src, at, _ = self.items[n]
        return to_chip(
            src.at[self.row(0, chip), lanes(at, count)],
            dst.at[:, lanes(first, count)],
            self.ss.at[n, k],
            self.rs.at[n, k],
            chip,
        )

    def own(self, n, first, count):
        dst, src, at, _ = self.items[n]
        return pltpu.make_async_copy(
            src.at[self.row(0, lax.axis_index("hid")), lanes(at, count)],
            dst.at[:, lanes(first, count)],
            self.ls.at[n],
        )

    def job(self, n, k):
        def run():
            h = lax.axis_index("hid")
            chip = lax.rem(h + k, H)
            self.sized(n, h, lambda first, count: self.copy(n, k, chip, first, count).start())

        return run

    def jobs(self):
        made = []
        for p, (_, _, ns) in enumerate(self.parts):
            made.append(self.add(p))
            made += [self.job(n, k) for n in ns for k in range(1, H)]
        return made

    def finish(self):
        h = lax.axis_index("hid")
        for n in range(len(self.items)):
            self.sized(n, h, lambda first, count: self.own(n, first, count).wait())
            for k in range(1, H):
                chip, source = lax.rem(h + k, H), lax.rem(h + H - k, H)
                self.sized(
                    n, source, lambda first, count: self.copy(n, k, chip, first, count).wait_recv()
                )
                self.sized(
                    n, h, lambda first, count: self.copy(n, k, chip, first, count).wait_send()
                )


def bulk_sems(n):
    return [DMA((n, H)), DMA((n, H)), DMA((n,)), DMA((n, 2)), DMA((n, 2))]


def split_refs(refs, *counts):
    groups, at = [], 0
    for count in counts:
        groups.append(refs[at : at + count])
        at += count
    assert at == len(refs)
    return groups


def row_norm(rows):
    return lax.rsqrt(jnp.mean(rows * rows, axis=-1, keepdims=True) + EPS)


def open_kernel(tiles, *refs):
    (x_ref, c_ref, *weights), (first, cot, wqfi, wo, wg, wu, wd), s1, s2, bulk, (ls,) = split_refs(
        refs, 9, 7, 6, 6, 5, 1
    )
    q, f, i, o, g, u, d = weights
    h, z, y, x = place()
    greet(all_chips(), core=True)
    own = [
        pltpu.make_async_copy(src, dst.at[z, y, x], ls.at[n])
        for n, (src, dst) in enumerate(((x_ref, first), (c_ref, cot)))
    ]
    for copy in own:
        copy.start()
    fetch = Fetch(
        [
            (q, wqfi, 0, False),
            (f, wqfi, 1, False),
            (i, wqfi, 2, False),
            (o, wo, 0, False),
            (g, wg, 0, True),
            (u, wu, 0, True),
            (d, wd, 0, True),
        ],
        tiles,
        q.shape[0],
        bulk,
    )
    for copy in own:
        copy.wait()
    queue = Queue(fetch.jobs())
    gathers = [Gather(first, s1), Gather(cot, s2)]
    cuts = [(g, c) for g in gathers for c in range(CUTS)]
    for g, c in cuts[: AHEAD[0]]:
        g.start(c)
    queue.run(PACE[0])
    fetch.start_own()
    n = len(cuts)
    for t in range(n + PARTS):
        if t < n:
            cuts[t][0].second(cuts[t][1])
        if t + AHEAD[0] < n:
            g, c = cuts[t + AHEAD[0]]
            g.start(c)
        if t >= PARTS:
            cuts[t - PARTS][0].third(cuts[t - PARTS][1])
        queue.run(PACE[0])
    queue.run(len(queue.jobs))
    for k in range(len(weights)):
        fetch.arrive(k)
    for g in gathers:
        g.finish()
    fetch.finish()


def open_segment(first_low, cot_low, weights, collective_id):
    depth, units = weights[-1].shape
    tiles = units // 128
    wide = -(-tiles // H) * 128
    shape = lambda cols: jax.ShapeDtypeStruct((2 * H * depth, cols), BF)
    rows = jax.ShapeDtypeStruct((4, 2, 2) + first_low.shape, BF)
    first, cot, *blocks = pl.pallas_call(
        functools.partial(open_kernel, tiles),
        out_shape=[rows, rows] + [shape(cols) for cols in (384, 128, wide, wide, wide)],
        in_specs=[VSPEC] * 2 + [ASPEC] * 7,
        out_specs=[VSPEC] * 7,
        scratch_shapes=gather_sems() + gather_sems() + bulk_sems(7) + [DMA((2,))],
        compiler_params=comm_params(collective_id),
    )(first_low, cot_low, *weights)
    flat = lambda rows: rows.reshape(-1, rows.shape[-1])
    return flat(first), flat(cot), *blocks


def turn_steps(scatter, gather, ahead, rows_done):
    n, lag, held = CUTS, PARTS, []
    for c in range(min(ahead, n)):
        scatter.start(c)
    for t in range(n + 5 * lag):
        if t < n:
            scatter.second(t)
            if t + ahead < n:
                scatter.start(t + ahead)
        if 0 <= t - lag // 2 < n:
            scatter.third(t - lag // 2)
        c = t - lag - lag // 2
        if 0 <= c < n:
            held.append(scatter.last(c))
            if len(held) == PARTS:
                rows_done(c // PARTS, jnp.concatenate(held, axis=1))
                held = []
                for k in range(c + 1 - PARTS, c + 1):
                    gather.start(k)
        c -= lag + PARTS - 1
        if 0 <= c < n:
            gather.second(c)
        if 0 <= c - lag < n:
            gather.third(c - lag)
    scatter.finish()
    gather.finish()


def forward_kernel(p_ref, x_ref, gain_ref, middle, second, *scratch):
    h, z, y, x = place()
    column, py, px = partners()
    greet(column + [py, px])
    s1, s2 = split_refs(scratch, 11, 6)
    scatter, gather = Scatter(p_ref, s1), Gather(second, s2)
    size = x_ref.shape[0] // PIECES

    def rows_done(i, total):
        at = pl.ds(i * size, size)
        rows = x_ref[at] + total
        middle[at] = rows
        second[z, y, x, at] = (rows * row_norm(rows) * gain_ref[...]).astype(BF)

    turn_steps(scatter, gather, AHEAD[1], rows_done)


def forward_segment(part, entries, gain, collective_id):
    rows, cols = entries.shape
    middle, second = pl.pallas_call(
        forward_kernel,
        out_shape=[
            jax.ShapeDtypeStruct((rows, cols), F32),
            jax.ShapeDtypeStruct((4, 2, 2, rows, cols), BF),
        ],
        in_specs=[VSPEC] * 3,
        out_specs=[VSPEC] * 2,
        scratch_shapes=scatter_scratch(rows, cols) + gather_sems(),
        compiler_params=comm_params(collective_id),
    )(part.reshape(4, 2, 2, rows, cols), entries, gain[None])
    return middle, second.reshape(-1, cols)


def norm_back(rows, grad, gain):
    factor = row_norm(rows)
    normal = rows * factor
    scaled = grad * gain
    back = factor * (scaled - normal * jnp.mean(scaled * normal, axis=-1, keepdims=True))
    return back, jnp.sum(grad * normal, axis=0, keepdims=True)


def backward_kernel(p_ref, m_ref, c_ref, gain_ref, grad, mix, part, *scratch):
    h, z, y, x = place()
    column, py, px = partners()
    greet(column + [py, px])
    s1, s2 = split_refs(scratch, 11, 6)
    scatter, gather = Scatter(p_ref, s1), Gather(mix, s2)
    size = m_ref.shape[0] // PIECES

    def rows_done(i, total):
        at = pl.ds(i * size, size)
        back, gains = norm_back(m_ref[at], total, gain_ref[...])
        part[...] = gains if i == 0 else part[...] + gains
        rows = c_ref[at].astype(F32) + back
        grad[at] = rows
        mix[z, y, x, at] = rows.astype(BF)

    turn_steps(scatter, gather, AHEAD[2], rows_done)


def backward_segment(part, middle, cot_low, gain, collective_id):
    rows, cols = middle.shape
    grad, mix, gains = pl.pallas_call(
        backward_kernel,
        out_shape=[
            jax.ShapeDtypeStruct((rows, cols), F32),
            jax.ShapeDtypeStruct((4, 2, 2, rows, cols), BF),
            jax.ShapeDtypeStruct((1, cols), F32),
        ],
        in_specs=[VSPEC] * 4,
        out_specs=[VSPEC] * 3,
        scratch_shapes=scatter_scratch(rows, cols) + gather_sems(),
        compiler_params=comm_params(collective_id),
    )(part.reshape(4, 2, 2, rows, cols), middle, cot_low, gain[None])
    return grad, mix.reshape(-1, cols), gains


def close_kernel(tiles, *refs):
    (
        (p_ref, l_ref, x_ref, mg_ref, m_ref, gain_ref, vec_ref, pqfi, po, pg, pu, pd),
        (in_grad, out, totals, q, f, i, o, g, u, d),
        s1,
        s2,
        (tqfi, to, tg, tu, td),
        (mine, theirs, chips, vs, vr, ws, wr),
        bulk,
    ) = split_refs(refs, 12, 10, 11, 11, 5, 7, 5)
    h, z, y, x = place()
    greet(all_chips(), core=True)
    giver = Return(
        [
            (d, td, 0, True),
            (g, tg, 0, True),
            (u, tu, 0, True),
            (o, to, 0, False),
            (q, tqfi, 0, False),
            (f, tqfi, 1, False),
            (i, tqfi, 2, False),
        ],
        [(pd, td, (0,)), (pg, tg, (1,)), (pu, tu, (2,)), (po, to, (3,)), (pqfi, tqfi, (4, 5, 6))],
        tiles,
        q.shape[0],
        bulk,
    )
    first, glu = Scatter(p_ref, s1), Scatter(l_ref, s2)
    size = x_ref.shape[0] // PIECES
    queue = Queue(giver.jobs())
    cuts = [(s, c) for s in (first, glu) for c in range(CUTS)]
    giver.start_swaps()
    for s, c in cuts[: AHEAD[3]]:
        s.start(c)
    held, sent = [], {}
    total, lag = len(cuts), PARTS
    for t in range(total + lag + lag // 2):
        if t < total:
            cuts[t][0].second(cuts[t][1])
            if t + AHEAD[3] < total:
                s, c = cuts[t + AHEAD[3]]
                s.start(c)
        if 0 <= t - lag // 2 < total:
            s, c = cuts[t - lag // 2]
            s.third(c)
        if 0 <= t - lag - lag // 2 < total:
            s, c = cuts[t - lag - lag // 2]
            held.append(s.last(c))
            if len(held) == PARTS:
                at = pl.ds(c // PARTS * size, size)
                rows = jnp.concatenate(held, axis=1)
                held = []
                if s is first:
                    back, gains = norm_back(x_ref[at], rows, gain_ref[...])
                    in_grad[at] = mg_ref[at] + back
                    if c < PARTS:
                        mine[...] = vec_ref[...]
                    mine[0:16] = mine[0:16] + gains.reshape(16, 128)
                    if c == CUTS - 1:
                        swap = to_core(mine, theirs, vs, vr)
                        swap.start()
                else:
                    out[at] = (m_ref[at] + rows).astype(BF)
        if t == CUTS + 2 * lag:
            swap.wait()
            chips[h] = mine[...] + theirs[...]
            for k in range(1, H):
                sent[k] = to_chip(
                    chips.at[h], chips.at[h], ws.at[k], wr.at[k], lax.rem(h + k, H)
                )
                sent[k].start()
        queue.run(PACE[1])
    queue.run(len(queue.jobs))
    for k in range(1, H):
        sent[k].wait()
    acc = chips[0, 0:40]
    for chip in range(1, H):
        acc = acc + chips[chip, 0:40]
    totals[0:40] = acc
    for chip in range(H):
        totals[40 + chip : 41 + chip] = chips[chip, 40:41]
    first.finish()
    glu.finish()
    giver.finish()


def close_segment(
    part, glu, entries, middle_grad, middle, gain, vector, grads, units, collective_id
):
    rows, cols = entries.shape
    depth = grads[0].shape[0] // (2 * H)
    back = lambda width: jax.ShapeDtypeStruct((depth, width), BF)
    wide = (4, 2, 2, rows, cols)
    return pl.pallas_call(
        functools.partial(close_kernel, units // 128),
        out_shape=[
            jax.ShapeDtypeStruct((rows, cols), F32),
            jax.ShapeDtypeStruct((rows, cols), BF),
            jax.ShapeDtypeStruct((56, 128), F32),
        ]
        + [back(cols)] * 4
        + [back(units)] * 3,
        in_specs=[VSPEC] * 12,
        out_specs=[VSPEC] * 10,
        scratch_shapes=scatter_scratch(rows, cols)
        + scatter_scratch(rows, cols)
        + [VMEM((p.shape[0] // 2, p.shape[1]), BF) for p in grads]
        + [VMEM((48, 128), F32), VMEM((48, 128), F32), VMEM((H, 48, 128), F32)]
        + [DMA, DMA, DMA((H,)), DMA((H,))]
        + bulk_sems(7),
        compiler_params=comm_params(collective_id),
    )(
        part.reshape(wide),
        glu.reshape(wide),
        entries,
        middle_grad,
        middle,
        gain[None],
        vector,
        *grads,
    )


def mm(left, right, at_left, at_right):
    return lax.dot_general(
        left.astype(BF),
        right.astype(BF),
        (((at_left,), (at_right,)), ((), ())),
        preferred_element_type=F32,
    )


def tri_sum(rows, reverse=False):
    r = lax.broadcasted_iota(jnp.int32, (SPAN, SPAN), 0)
    c = lax.broadcasted_iota(jnp.int32, (SPAN, SPAN), 1)
    picked = jnp.where((r <= c) if reverse else (r >= c), 1.0, 0.0).astype(BF)
    high = rows.astype(BF)
    rest = rows - high.astype(F32)
    middle = rest.astype(BF)
    low = rest - middle.astype(F32)
    return mm(picked, high, 1, 0) + mm(picked, middle, 1, 0) + mm(picked, low, 1, 0)


def span_gates(lin_ref, gap_ref, at):
    q_lin, f_lin, values = lin_ref[at, 0:128], lin_ref[at, 128:256], lin_ref[at, 256:384]
    s = jax.nn.sigmoid(q_lin)
    key = jnp.exp(gap_ref[...]) * jax.nn.sigmoid(-f_lin)
    return q_lin, f_lin, values, s, key


def span_masks(dcol_ref, drow_ref, marks_ref, c, at):
    r = lax.broadcasted_iota(jnp.int32, (SPAN, SPAN), 0)
    k = lax.broadcasted_iota(jnp.int32, (SPAN, SPAN), 1)
    dcol, drow = dcol_ref[at], drow_ref[c : c + 1]
    before, end = marks_ref[0, c], marks_ref[1, c]
    same = jnp.where(jnp.logical_and(dcol == drow, r >= k), 1.0, 0.0)
    carried = jnp.where(dcol == before, 1.0, 0.0)
    keep = jnp.where(dcol == end, 1.0, 0.0)
    whole = jnp.where(end == before, 1.0, 0.0)
    return same, carried, keep, whole


def spans(extent):
    return [(c, pl.ds(c * SPAN, SPAN)) for c in range(extent // SPAN)]


def mix_kernel(
    lin_ref, gap_ref, gain_ref, dcol_ref, drow_ref, marks_ref,
    mixed_ref, states_ref, head_ref, cum_ref, out_ref, in_ref, send, recv,
):
    greet([], core=True)
    extent = lin_ref.shape[0]
    steps = spans(extent)
    state = jnp.zeros((SPAN, SPAN), F32)
    for c, at in steps:
        q_lin, f_lin, values, s, key = span_gates(lin_ref, gap_ref, at)
        same, carried, keep, whole = span_masks(dcol_ref, drow_ref, marks_ref, c, at)
        cum = tri_sum(jnp.log1p(-key))
        cum_ref[at] = cum
        end = cum[SPAN - 1 : SPAN]
        fresh = mm(values, jnp.exp(end - cum) * key * keep, 0, 0)
        states_ref[c] = fresh
        state = state * (jnp.exp(end) * whole) + fresh
    out_ref[...] = state
    copy = to_core(out_ref, in_ref, send, recv)
    copy.start()
    copy.wait()
    state = in_ref[...] * lax.axis_index("seq").astype(F32)
    for c, at in steps:
        q_lin, f_lin, values, s, key = span_gates(lin_ref, gap_ref, at)
        same, carried, keep, whole = span_masks(dcol_ref, drow_ref, marks_ref, c, at)
        cum = cum_ref[at]
        end = cum[SPAN - 1 : SPAN]
        fresh = states_ref[c]
        states_ref[c] = state
        decayed = q_lin * s * jnp.exp(cum)
        scores = mm(decayed, key * jnp.exp(-cum), 1, 1) * same
        mixed = mm(scores, values, 1, 0) + carried * mm(decayed, state, 1, 1)
        mixed_ref[at] = mixed
        factor = lax.rsqrt(jnp.mean(mixed * mixed, axis=-1, keepdims=True) + EPS)
        head_ref[at] = (mixed * factor * gain_ref[...]).astype(BF)
        state = state * (jnp.exp(end) * whole) + fresh


def mix_forward(lin, gap_row, gain_row, dcol, drow, marks, collective_id):
    extent = lin.shape[0]
    tile = jax.ShapeDtypeStruct((extent, SPAN), F32)
    return pl.pallas_call(
        mix_kernel,
        out_shape=[
            tile,
            jax.ShapeDtypeStruct((extent // SPAN, SPAN, SPAN), F32),
            jax.ShapeDtypeStruct((extent, SPAN), BF),
            tile,
        ],
        in_specs=[VSPEC] * 5 + [SSPEC],
        out_specs=[VSPEC] * 4,
        scratch_shapes=[VMEM((SPAN, SPAN), F32), VMEM((SPAN, SPAN), F32), DMA, DMA],
        compiler_params=comm_params(collective_id),
    )(lin, gap_row, gain_row, dcol, drow, marks)


def unmix_kernel(
    lin_ref, gap_ref, gain_ref, dcol_ref, drow_ref, marks_ref, mixed_ref, states_ref, cum_ref, dhead_ref,
    dlin_ref, gapg_ref, groupg_ref, do_ref, back_ref, out_ref, in_ref, send, recv,
):
    greet([], core=True)
    extent = lin_ref.shape[0]
    steps = spans(extent)
    group = jnp.zeros((1, SPAN), F32)
    adjoint = jnp.zeros((SPAN, SPAN), F32)
    for c, at in reversed(steps):
        mixed, dy = mixed_ref[at], dhead_ref[at]
        factor = lax.rsqrt(jnp.mean(mixed * mixed, axis=-1, keepdims=True) + EPS)
        normal = mixed * factor
        group = group + jnp.sum(dy * normal, axis=0, keepdims=True)
        scaled = dy * gain_ref[...]
        d_mixed = factor * (scaled - normal * jnp.mean(scaled * normal, axis=-1, keepdims=True))
        do_ref[at] = d_mixed
        q_lin, f_lin, values, s, key = span_gates(lin_ref, gap_ref, at)
        same, carried, keep, whole = span_masks(dcol_ref, drow_ref, marks_ref, c, at)
        cum = cum_ref[at]
        back = mm(d_mixed, carried * (q_lin * s * jnp.exp(cum)), 0, 0)
        back_ref[c] = back
        adjoint = adjoint * (jnp.exp(cum[SPAN - 1 : SPAN]) * whole) + back
    groupg_ref[...] = group
    out_ref[...] = adjoint
    copy = to_core(out_ref, in_ref, send, recv)
    copy.start()
    copy.wait()
    adjoint = in_ref[...] * (1 - lax.axis_index("seq")).astype(F32)
    gap = jnp.zeros((1, SPAN), F32)
    for c, at in reversed(steps):
        q_lin, f_lin, values, s, key = span_gates(lin_ref, gap_ref, at)
        same, carried, keep, whole = span_masks(dcol_ref, drow_ref, marks_ref, c, at)
        cum, d_mixed, state = cum_ref[at], do_ref[at], states_ref[c]
        grow, shrink = jnp.exp(-cum), jnp.exp(cum)
        end = cum[SPAN - 1 : SPAN]
        decayed, grown = q_lin * s * shrink, key * grow
        rest = jnp.exp(end - cum) * keep
        tail, through = rest * key, jnp.exp(end) * whole
        scores = mm(decayed, grown, 1, 1) * same
        d_scores = mm(d_mixed, values, 1, 1) * same
        d_values = mm(scores, d_mixed, 0, 0) + mm(tail, adjoint, 1, 1)
        d_decayed = mm(d_scores, grown, 1, 0) + carried * mm(d_mixed, state, 1, 0)
        d_grown = mm(d_scores, decayed, 0, 0)
        d_tail = mm(values, adjoint, 1, 0)
        held = tail * d_tail
        d_cum = decayed * d_decayed - grown * d_grown - held
        d_end = jnp.sum(held, axis=0, keepdims=True) + through * jnp.sum(
            state * adjoint, axis=0, keepdims=True
        )
        d_log = tri_sum(d_cum, reverse=True) + d_end
        d_key = d_grown * grow + d_tail * rest - d_log / (1.0 - key)
        scaled = d_key * key
        gap = gap + jnp.sum(scaled, axis=0, keepdims=True)
        dlin_ref[at, 0:128] = (d_decayed * shrink * s * (1.0 + q_lin * (1.0 - s))).astype(BF)
        dlin_ref[at, 128:256] = (-scaled * jax.nn.sigmoid(f_lin)).astype(BF)
        dlin_ref[at, 256:384] = d_values.astype(BF)
        adjoint = adjoint * through + back_ref[c]
    gapg_ref[...] = gap


def mix_backward(lin, gap_row, gain_row, dcol, drow, marks, mixed, states, cum, d_head, collective_id):
    extent = lin.shape[0]
    row = jax.ShapeDtypeStruct((1, SPAN), F32)
    return pl.pallas_call(
        unmix_kernel,
        out_shape=[jax.ShapeDtypeStruct(lin.shape, BF), row, row],
        in_specs=[VSPEC] * 5 + [SSPEC] + [VSPEC] * 4,
        out_specs=[VSPEC] * 3,
        scratch_shapes=[
            VMEM((extent, SPAN), F32),
            VMEM((extent // SPAN, SPAN, SPAN), F32),
            VMEM((SPAN, SPAN), F32),
            VMEM((SPAN, SPAN), F32),
            DMA,
            DMA,
        ],
        compiler_params=comm_params(collective_id),
    )(lin, gap_row, gain_row, dcol, drow, marks, mixed, states, cum, d_head)


def fast_body(
    inputs,
    cotangent,
    lengths,
    first_gain,
    q_weight,
    f_weight,
    i_weight,
    o_weight,
    group_gain,
    gap_log,
    second_gain,
    gate_weight,
    up_weight,
    down_weight,
):
    rows, model = inputs.shape[1:]
    units = gate_weight.shape[1]
    head_id, block_id = lax.axis_index("hid"), lax.axis_index("seq")
    block_len = H * rows
    entries = inputs[0].astype(F32)
    cot_low = cotangent[0]
    positions = block_id * block_len + lax.iota(jnp.int32, block_len)
    documents = doc_ids(lengths, positions)
    before = doc_ids(lengths, jnp.reshape(block_id * block_len - 1, (1,)))
    drow = documents.reshape(block_len // SPAN, SPAN)
    ends = drow[:, -1]
    marks = jnp.stack([jnp.concatenate([before, ends[:-1]]), ends])
    gap_row = lax.dynamic_slice_in_dim(gap_log, head_id * SPAN, SPAN)[None]
    gain_row = group_gain[None]
    aids = (gap_row, gain_row, documents[:, None], drow, marks)

    first_low = normed(entries, first_gain).astype(BF)
    first_rows, cot_rows, qfi_block, o_block, gate_block, up_block, down_block = open_segment(
        first_low,
        cot_low,
        (q_weight, f_weight, i_weight, o_weight, gate_weight, up_weight, down_weight),
        1,
    )
    lin = jnp.dot(first_rows, qfi_block, preferred_element_type=F32)
    mixed, states, head_low, cum = mix_forward(lin, *aids, 2)
    middle, second_rows = forward_segment(
        times_t(head_low, o_block).astype(BF), entries, second_gain, 3
    )
    gate_lin = jnp.dot(second_rows, gate_block, preferred_element_type=F32)
    up_lin = jnp.dot(second_rows, up_block, preferred_element_type=F32)
    gate_sig = jax.nn.sigmoid(gate_lin)
    hidden = (gate_lin * gate_sig * up_lin).astype(BF)
    hidden_grad = jnp.dot(cot_rows, down_block, preferred_element_type=F32)
    gate_low = (hidden_grad * up_lin * gate_sig * (1.0 + gate_lin * (1.0 - gate_sig))).astype(BF)
    up_low = (hidden_grad * gate_lin * gate_sig).astype(BF)
    second_sum = (times_t(gate_low, gate_block) + times_t(up_low, up_block)).astype(BF)
    middle_grad, mix_rows, second_part = backward_segment(
        second_sum, middle, cot_low, second_gain, 4
    )
    d_head = jnp.dot(mix_rows, o_block, preferred_element_type=F32)
    d_lin, gap_part, group_part = mix_backward(lin, *aids, mixed, states, cum, d_head, 5)
    vector = jnp.concatenate(
        [
            jnp.zeros((16, 128), F32),
            second_part.reshape(16, 128),
            group_part,
            jnp.zeros((7, 128), F32),
            gap_part,
            jnp.zeros((7, 128), F32),
        ]
    )
    input_grad, output, totals, q_grad, f_grad, i_grad, o_grad, gate_grad, up_grad, down_grad = (
        close_segment(
            times_t(d_lin, qfi_block).astype(BF),
            times_t(hidden, down_block).astype(BF),
            entries,
            middle_grad,
            middle,
            first_gain,
            vector,
            (
                outer_sum(first_rows, d_lin).astype(BF),
                outer_sum(mix_rows, head_low).astype(BF),
                outer_sum(second_rows, gate_low).astype(BF),
                outer_sum(second_rows, up_low).astype(BF),
                outer_sum(cot_rows, hidden).astype(BF),
            ),
            units,
            6,
        )
    )
    return (
        output[None],
        input_grad[None],
        totals[0:16].reshape(model),
        q_grad.astype(F32),
        f_grad.astype(F32),
        i_grad.astype(F32),
        o_grad.astype(F32),
        totals[32],
        totals[40:56].reshape(model),
        totals[16:32].reshape(model),
        gate_grad.astype(F32),
        up_grad.astype(F32),
        down_grad.astype(F32),
    )


def solution(mesh):
    placed = (
        P("seq", "hid", None),
        P("seq", "hid", None),
        P(),
        P(),
        P(("seq", "hid"), None),
        P(("seq", "hid"), None),
        P(("seq", "hid"), None),
        P(("seq", "hid"), None),
        P(),
        P(),
        P(),
        P(("seq", "hid"), None),
        P(("seq", "hid"), None),
        P(("seq", "hid"), None),
    )
    body = fast_body if mesh.shape["hid"] == H else wide_body
    return jax.shard_map(
        body,
        mesh=mesh,
        in_specs=placed,
        out_specs=(
            P("seq", "hid", None),
            P("seq", "hid", None),
            P(),
            P(("seq", "hid"), None),
            P(("seq", "hid"), None),
            P(("seq", "hid"), None),
            P(("seq", "hid"), None),
            P(),
            P(),
            P(),
            P(("seq", "hid"), None),
            P(("seq", "hid"), None),
            P(("seq", "hid"), None),
        ),
        check_vma=False,
    )
```

```python
import functools

import jax
import jax.numpy as jnp
from jax import lax
from jax.experimental import pallas as pl
from jax.experimental.pallas import tpu as pltpu
from jax.sharding import PartitionSpec as P

H = 16
SPAN = 128


EPS = 1e-06
HIGH_PRECISION = lax.Precision.HIGHEST


def from_behind(block, axis, distance):
    devices = range(lax.axis_size(axis))
    route = [(i - distance, i) for i in devices if i - distance in devices]
    return lax.ppermute(block, axis, route)


def normed(entries, gain_vec):
    factor = lax.rsqrt(jnp.mean(entries * entries, axis=-1, keepdims=True) + EPS)
    return entries * factor * gain_vec


def gates(q_part, f_part, gap_piece):
    key_gate = jnp.exp(gap_piece) * jax.nn.sigmoid(-f_part)
    return (jax.nn.silu(q_part), key_gate, jnp.log1p(-key_gate))


def doc_starts(lengths):
    count = lengths.shape[0]
    earlier = lax.broadcasted_iota(jnp.int32, (count, count), 0) > lax.broadcasted_iota(
        jnp.int32, (count, count), 1
    )
    return jnp.sum(jnp.where(earlier, lengths[None, :], 0), axis=1)


def running_sum(rows):
    extent = rows.shape[-2]
    lower = (
        lax.broadcasted_iota(jnp.int32, (extent, extent), 0)
        >= lax.broadcasted_iota(jnp.int32, (extent, extent), 1)
    ).astype(jnp.float32)
    return jnp.einsum("ts,...sk->...tk", lower, rows, precision=HIGH_PRECISION)


def doc_ids(lengths, positions):
    starts = doc_starts(lengths)
    covered = (starts[None, :] <= positions[:, None]).astype(jnp.int32)
    return jnp.sum(covered, axis=1) - 1


def span_step(memory_state, pieces):
    queries, key_gate, value_rows, log_decay, documents, before = pieces
    cumulative = running_sum(log_decay)
    query_decayed = queries * jnp.exp(cumulative)
    k_grown = key_gate * jnp.exp(-cumulative)
    extent = documents.shape[0]
    row_ids = lax.broadcasted_iota(jnp.int32, (extent, extent), 0)
    col_ids = lax.broadcasted_iota(jnp.int32, (extent, extent), 1)
    same_doc = jnp.logical_and(documents[:, None] == documents[None, :], row_ids >= col_ids).astype(
        jnp.float32
    )
    scores = (
        jnp.einsum("hck,hsk->hcs", query_decayed, k_grown, precision=HIGH_PRECISION)
        * same_doc[None]
    )
    within_block = jnp.einsum("hcs,hsv->hcv", scores, value_rows, precision=HIGH_PRECISION)
    carried_state = (documents == before).astype(jnp.float32)[None, :, None]
    output_rows = within_block + carried_state * jnp.einsum(
        "awn,ani->awi", query_decayed, memory_state, precision=HIGH_PRECISION
    )
    last_cum = cumulative[:, -1:, :]
    keep_mask = (documents == documents[-1]).astype(jnp.float32)[None, :, None]
    tail_key_rows = jnp.exp(last_cum - cumulative) * key_gate * keep_mask
    whole_block = (documents[-1] == before).astype(jnp.float32)
    fresh_state = jnp.einsum("wfx,wfg->wxg", tail_key_rows, value_rows, precision=HIGH_PRECISION)
    memory_state = jnp.exp(last_cum[:, 0, :])[:, :, None] * whole_block * memory_state + fresh_state
    return (memory_state, output_rows)


def recur(queries, key_gate, value_rows, log_decay, documents, before, memory_state):
    head_count, extent, columns = queries.shape
    span_count = extent // SPAN

    def by_span(tensor):
        return jnp.swapaxes(tensor.reshape(head_count, span_count, SPAN, tensor.shape[-1]), 0, 1)

    doc_rows = documents.reshape(span_count, SPAN)
    befores = jnp.concatenate([jnp.reshape(before, (1,)), doc_rows[:-1, -1]])
    memory_state, span_out = lax.scan(
        jax.checkpoint(span_step),
        memory_state,
        (
            by_span(queries),
            by_span(key_gate),
            by_span(value_rows),
            by_span(log_decay),
            doc_rows,
            befores,
        ),
    )
    return (
        jnp.swapaxes(span_out, 0, 1).reshape(head_count, extent, value_rows.shape[-1]),
        memory_state,
    )


def spread_cols(weight, copies):
    row_count = weight.shape[0]
    shaped = weight.reshape(row_count, 1, H, weight.shape[1] // H)
    return jnp.broadcast_to(shaped, (row_count, copies, H, shaped.shape[3])).reshape(
        row_count, copies * weight.shape[1]
    )


def fold_copies(received, copies):
    row_count = received.shape[0]
    return jnp.sum(received.reshape(row_count, copies, received.shape[1] // copies), axis=1)


def fan_rows(local_rows):
    blocks_here, row_count, columns = local_rows.shape
    return jnp.broadcast_to(local_rows[:, None], (blocks_here, H, row_count, columns)).reshape(
        blocks_here * H * row_count, columns
    )


def sum_heads(received, blocks_here):
    total_rows, columns = received.shape
    return jnp.sum(
        received.reshape(blocks_here, H, total_rows // (blocks_here * H), columns), axis=1
    )


def times_t(left_mat, right_mat):
    return lax.dot_general(
        left_mat, right_mat, (((1,), (1,)), ((), ())), preferred_element_type=jnp.float32
    )


def outer_sum(left_mat, right_mat):
    return lax.dot_general(
        left_mat, right_mat, (((0,), (0,)), ((), ())), preferred_element_type=jnp.float32
    )


def outer_high(left_mat, right_mat):
    return lax.dot_general(
        left_mat,
        right_mat,
        (((0,), (0,)), ((), ())),
        precision=HIGH_PRECISION,
        preferred_element_type=jnp.float32,
    )


def wide_body(
    inputs,
    cotangent,
    lengths,
    first_gain,
    q_weight,
    f_weight,
    i_weight,
    o_weight,
    group_gain,
    gap_log,
    second_gain,
    gate_weight,
    up_weight,
    down_weight,
):
    hid_size = lax.axis_size("hid")
    per_seq = hid_size // H
    block_total = lax.axis_size("seq") * per_seq
    hid_place = lax.axis_index("hid")
    head_id = hid_place % H
    block_id = lax.axis_index("seq") * per_seq + hid_place // H
    model = inputs.shape[2]
    head_width = model // H
    block_len = hid_size * inputs.shape[1]
    entries = inputs.astype(jnp.float32)
    q_block, f_block, i_block, o_block, gate_block, up_block, down_block = (
        lax.all_to_all(
            spread_cols(q_weight, block_total),
            ("seq", "hid"),
            split_axis=1,
            concat_axis=0,
            tiled=True,
        ),
        lax.all_to_all(
            spread_cols(f_weight, block_total),
            ("seq", "hid"),
            split_axis=1,
            concat_axis=0,
            tiled=True,
        ),
        lax.all_to_all(
            spread_cols(i_weight, block_total),
            ("seq", "hid"),
            split_axis=1,
            concat_axis=0,
            tiled=True,
        ),
        lax.all_to_all(
            spread_cols(o_weight, block_total),
            ("seq", "hid"),
            split_axis=1,
            concat_axis=0,
            tiled=True,
        ),
        lax.all_to_all(
            spread_cols(gate_weight, block_total),
            ("seq", "hid"),
            split_axis=1,
            concat_axis=0,
            tiled=True,
        ),
        lax.all_to_all(
            spread_cols(up_weight, block_total),
            ("seq", "hid"),
            split_axis=1,
            concat_axis=0,
            tiled=True,
        ),
        lax.all_to_all(
            spread_cols(down_weight, block_total),
            ("seq", "hid"),
            split_axis=1,
            concat_axis=0,
            tiled=True,
        ),
    )
    positions = block_id * block_len + lax.iota(jnp.int32, block_len)
    documents = doc_ids(lengths, positions)
    before = doc_ids(lengths, jnp.reshape(block_id * block_len - 1, (1,)))[0]
    first_norm, first_back = jax.vjp(normed, entries, first_gain)
    first_low = first_norm.astype(jnp.bfloat16)
    first_rows = lax.all_to_all(fan_rows(first_low), "hid", split_axis=0, concat_axis=0, tiled=True)
    q_lin = jnp.dot(first_rows, q_block, preferred_element_type=jnp.float32)
    f_lin = jnp.dot(first_rows, f_block, preferred_element_type=jnp.float32)
    i_lin = jnp.dot(first_rows, i_block, preferred_element_type=jnp.float32)
    gap_part = lax.dynamic_slice_in_dim(gap_log, head_id * head_width, head_width)
    queries, key_gate, log_decay = gates(q_lin, f_lin, gap_part)
    cumulative = running_sum(log_decay)
    last_cum = cumulative[-1]
    tail_key_rows = (
        jnp.exp(last_cum[None, :] - cumulative)
        * key_gate
        * (documents == documents[-1]).astype(jnp.float32)[:, None]
    )
    local_state = outer_high(tail_key_rows, i_lin)
    decay = jnp.exp(last_cum) * (documents[-1] == before).astype(jnp.float32)
    state_in = jnp.zeros_like(local_state)
    for number in range(block_total - 1):
        state_out = decay[:, None] * state_in + local_state
        state_in = from_behind(state_out.astype(jnp.bfloat16), ("seq", "hid"), H).astype(
            state_out.dtype
        )

    def core(q_part, f_part, i_part, gap_piece):
        queries_in, keys_in, logs_in = gates(q_part, f_part, gap_piece)
        mixed_all, memory_state = recur(
            queries_in[None],
            keys_in[None],
            i_part[None],
            logs_in[None],
            documents,
            before,
            state_in[None],
        )
        return (mixed_all[0], memory_state[0])

    (mixed_out, _), core_back = jax.vjp(core, q_lin, f_lin, i_lin, gap_part)
    head_normed, norm_back = jax.vjp(normed, mixed_out, group_gain)
    head_low = head_normed.astype(jnp.bfloat16)
    mix_out = sum_heads(
        lax.all_to_all(
            times_t(head_low, o_block).astype(jnp.bfloat16),
            "hid",
            split_axis=0,
            concat_axis=0,
            tiled=True,
        ).astype(jnp.float32),
        per_seq,
    )
    middle = entries + mix_out
    second_norm, second_back = jax.vjp(normed, middle, second_gain)
    second_low = second_norm.astype(jnp.bfloat16)
    second_rows, cot_rows = (
        lax.all_to_all(fan_rows(second_low), "hid", split_axis=0, concat_axis=0, tiled=True),
        lax.all_to_all(fan_rows(cotangent), "hid", split_axis=0, concat_axis=0, tiled=True),
    )
    gate_lin = jnp.dot(second_rows, gate_block, preferred_element_type=jnp.float32)
    up_lin = jnp.dot(second_rows, up_block, preferred_element_type=jnp.float32)
    hidden = (jax.nn.silu(gate_lin) * up_lin).astype(jnp.bfloat16)
    glu_out = sum_heads(
        lax.all_to_all(
            times_t(hidden, down_block).astype(jnp.bfloat16),
            "hid",
            split_axis=0,
            concat_axis=0,
            tiled=True,
        ).astype(jnp.float32),
        per_seq,
    )
    output = (middle + glu_out).astype(jnp.bfloat16)
    down_part = outer_sum(cot_rows, hidden)
    hidden_grad = jnp.dot(cot_rows, down_block, preferred_element_type=jnp.float32)
    gate_sig = jax.nn.sigmoid(gate_lin)
    gate_low = (hidden_grad * up_lin * gate_sig * (1.0 + gate_lin * (1.0 - gate_sig))).astype(
        jnp.bfloat16
    )
    up_low = (hidden_grad * gate_lin * gate_sig).astype(jnp.bfloat16)
    gate_part = outer_sum(second_rows, gate_low)
    up_part = outer_sum(second_rows, up_low)
    second_sum = lax.all_to_all(
        (times_t(gate_low, gate_block) + times_t(up_low, up_block)).astype(jnp.bfloat16),
        "hid",
        split_axis=0,
        concat_axis=0,
        tiled=True,
    ).astype(jnp.float32)
    middle_part, second_part = second_back(sum_heads(second_sum, per_seq))
    middle_grad = cotangent.astype(jnp.float32) + middle_part
    mix_grad = middle_grad.astype(jnp.bfloat16)
    mix_rows = lax.all_to_all(fan_rows(mix_grad), "hid", split_axis=0, concat_axis=0, tiled=True)
    normed_grad = jnp.dot(mix_rows, o_block, preferred_element_type=jnp.float32)
    o_part = outer_sum(mix_rows, head_low)
    mixed_grad, group_part = norm_back(normed_grad)
    carried_state = (documents == before).astype(jnp.float32)[:, None]
    grad_local = outer_high(queries * jnp.exp(cumulative) * carried_state, mixed_grad)
    state_grad = jnp.zeros_like(grad_local)
    for number in range(block_total - 1):
        grad_in = decay[:, None] * state_grad + grad_local
        state_grad = from_behind(grad_in.astype(jnp.bfloat16), ("seq", "hid"), -H).astype(
            grad_in.dtype
        )
    q_grad_lin, f_grad_lin, i_grad_lin, gap_piece_grad = core_back((mixed_grad, state_grad))
    q_low = q_grad_lin.astype(jnp.bfloat16)
    f_low = f_grad_lin.astype(jnp.bfloat16)
    i_low = i_grad_lin.astype(jnp.bfloat16)
    q_part = outer_sum(first_rows, q_low)
    f_part = outer_sum(first_rows, f_low)
    i_part = outer_sum(first_rows, i_low)
    first_sum = lax.all_to_all(
        (times_t(q_low, q_block) + times_t(f_low, f_block) + times_t(i_low, i_block)).astype(
            jnp.bfloat16
        ),
        "hid",
        split_axis=0,
        concat_axis=0,
        tiled=True,
    ).astype(jnp.float32)
    entry_part, first_part = first_back(sum_heads(first_sum, per_seq))
    input_grad = middle_grad + entry_part
    q_back, f_back, i_back, o_back, gate_back, up_back, down_back = (
        lax.all_to_all(
            q_part.astype(jnp.bfloat16), ("seq", "hid"), split_axis=0, concat_axis=1, tiled=True
        ).astype(q_part.dtype),
        lax.all_to_all(
            f_part.astype(jnp.bfloat16), ("seq", "hid"), split_axis=0, concat_axis=1, tiled=True
        ).astype(f_part.dtype),
        lax.all_to_all(
            i_part.astype(jnp.bfloat16), ("seq", "hid"), split_axis=0, concat_axis=1, tiled=True
        ).astype(i_part.dtype),
        lax.all_to_all(
            o_part.astype(jnp.bfloat16), ("seq", "hid"), split_axis=0, concat_axis=1, tiled=True
        ).astype(o_part.dtype),
        lax.all_to_all(
            gate_part.astype(jnp.bfloat16), ("seq", "hid"), split_axis=0, concat_axis=1, tiled=True
        ).astype(gate_part.dtype),
        lax.all_to_all(
            up_part.astype(jnp.bfloat16), ("seq", "hid"), split_axis=0, concat_axis=1, tiled=True
        ).astype(up_part.dtype),
        lax.all_to_all(
            down_part.astype(jnp.bfloat16), ("seq", "hid"), split_axis=0, concat_axis=1, tiled=True
        ).astype(down_part.dtype),
    )
    o_grad = fold_copies(o_back, block_total)
    head_pick = (lax.iota(jnp.int32, H) == head_id).astype(jnp.float32)
    gap_full = (head_pick[:, None] * gap_piece_grad[None, :]).reshape(model)
    first_grad, second_grad, group_grad, gap_grad = lax.psum(
        (first_part, second_part, group_part, gap_full), ("seq", "hid")
    )
    return (
        output,
        input_grad,
        first_grad,
        fold_copies(q_back, block_total),
        fold_copies(f_back, block_total),
        fold_copies(i_back, block_total),
        o_grad,
        group_grad,
        gap_grad,
        second_grad,
        fold_copies(gate_back, block_total),
        fold_copies(up_back, block_total),
        fold_copies(down_back, block_total),
    )


F32 = jnp.float32
BF = jnp.bfloat16
MESH = pl.DeviceIdType.MESH
DMA = pltpu.SemaphoreType.DMA
VMEM = pltpu.VMEM
PIECES = 3
PARTS = 4
CUTS = PIECES * PARTS
AHEAD = (4, 4, 4, 4, 4, 4)
PACE = (4, 6, 2, 2, 2, 2, 5)
VSPEC = pl.BlockSpec(memory_space=pltpu.VMEM)
ASPEC = pl.BlockSpec(memory_space=pl.ANY)
SSPEC = pl.BlockSpec(memory_space=pltpu.SMEM)


def place():
    h = lax.axis_index("hid")
    return h, h // 4, lax.rem(h // 2, 2), lax.rem(h, 2)


def partners():
    h, z, y, x = place()
    column = [lax.rem(z + k, 4) * 4 + lax.rem(h, 4) for k in (1, 2, 3)]
    return column, h + 2 - 4 * y, h + 1 - 2 * x


def greet(chips, core=False):
    gate = pltpu.get_barrier_semaphore()
    for chip in chips:
        pl.semaphore_signal(gate, inc=1, device_id={"hid": chip}, device_id_type=MESH)
    if core:
        other = 1 - lax.axis_index("seq")
        pl.semaphore_signal(gate, inc=1, device_id={"seq": other}, device_id_type=MESH)
    pl.semaphore_wait(gate, len(chips) + int(core))


def to_chip(src, dst, send, recv, chip):
    return pltpu.make_async_remote_copy(
        src_ref=src,
        dst_ref=dst,
        send_sem=send,
        recv_sem=recv,
        device_id={"hid": chip},
        device_id_type=MESH,
    )


def to_core(src, dst, send, recv):
    return pltpu.make_async_remote_copy(
        src_ref=src,
        dst_ref=dst,
        send_sem=send,
        recv_sem=recv,
        device_id={"seq": 1 - lax.axis_index("seq")},
        device_id_type=MESH,
    )


def comm_params(collective_id):
    return pltpu.CompilerParams(
        collective_id=collective_id, has_side_effects=True, vmem_limit_bytes=62 << 20
    )


class Cuts:
    def cut(self, c):
        i, j = c // PARTS, c % PARTS
        rows, cols = self.ref.shape[3] // PIECES, self.ref.shape[4] // PARTS
        return pl.ds(i * rows, rows), pl.ds(j * cols, cols), j % 2


class Gather(Cuts):
    def __init__(self, ref, sems):
        self.ref, self.sems = ref, sems
        self.one, self.two, self.three = {}, {}, {}

    def start(self, c):
        h, z, y, x = place()
        column, py, px = partners()
        a, b, j = self.cut(c)
        ref = self.ref.at[z, y, x, a, b]
        for k in range(3):
            self.one[c, k] = to_chip(
                ref, ref, self.sems[0].at[c, k], self.sems[1].at[c, k], column[k]
            )
            self.one[c, k].start()

    def second(self, c):
        h, z, y, x = place()
        column, py, px = partners()
        a, b, j = self.cut(c)
        for k in range(3):
            self.one[c, k].wait_recv()
        ref = self.ref.at[:, y, x, a, b]
        self.two[c] = to_chip(ref, ref, self.sems[2].at[c], self.sems[3].at[c], py if j else px)
        self.two[c].start()

    def third(self, c):
        h, z, y, x = place()
        column, py, px = partners()
        a, b, j = self.cut(c)
        self.two[c].wait_recv()
        ref = self.ref.at[:, :, x, a, b] if j else self.ref.at[:, y, :, a, b]
        self.three[c] = to_chip(ref, ref, self.sems[4].at[c], self.sems[5].at[c], px if j else py)
        self.three[c].start()

    def finish(self):
        for c in self.three:
            self.three[c].wait_recv()
        for c in self.three:
            for k in range(3):
                self.one[c, k].wait_send()
            self.two[c].wait_send()
            self.three[c].wait_send()


def gather_sems():
    n = CUTS
    return [DMA((n, 3)), DMA((n, 3)), DMA((n,)), DMA((n,)), DMA((n,)), DMA((n,))]


class Scatter(Cuts):
    def __init__(self, ref, bufs, sems):
        self.ref, self.bufs, self.sems = ref, bufs, sems
        self.one, self.two, self.three = {}, {}, {}

    def start(self, c):
        h, z, y, x = place()
        column, py, px = partners()
        a, b, j = self.cut(c)
        src = self.ref.at[:, :, 1 - x, a, b] if j else self.ref.at[:, 1 - y, :, a, b]
        self.one[c] = to_chip(
            src, self.bufs[0].at[c], self.sems[0].at[c], self.sems[1].at[c], px if j else py
        )
        self.one[c].start()

    def second(self, c):
        h, z, y, x = place()
        column, py, px = partners()
        b1, t1, b2 = self.bufs[:3]
        a, b, j = self.cut(c)
        q = y if j else x
        self.one[c].wait_recv()
        theirs = self.ref[:, 1 - q, x, a, b] if j else self.ref[:, y, 1 - q, a, b]
        b1[c, :, 1 - q] = (theirs.astype(F32) + b1[c, :, 1 - q].astype(F32)).astype(BF)
        self.two[c] = to_chip(
            b1.at[c, :, 1 - q], b2.at[c], self.sems[2].at[c], self.sems[3].at[c], py if j else px
        )
        self.two[c].start()
        mine = self.ref[:, q, x, a, b] if j else self.ref[:, y, q, a, b]
        t1[c] = mine.astype(F32) + b1[c, :, q].astype(F32)

    def third(self, c):
        h, z, y, x = place()
        column, py, px = partners()
        b1, t1, b2, t2, b3 = self.bufs
        self.two[c].wait_recv()
        t2[c] = t1[c, z] + b2[c, z].astype(F32)
        b2[c] = (t1[c] + b2[c].astype(F32)).astype(BF)
        for k in range(3):
            self.three[c, k] = to_chip(
                b2.at[c, lax.rem(z + k + 1, 4)],
                b3.at[c, k],
                self.sems[4].at[c, k],
                self.sems[5].at[c, k],
                column[k],
            )
            self.three[c, k].start()

    def last(self, c):
        h, z, y, x = place()
        b3, t2 = self.bufs[4], self.bufs[3]
        for k in range(3):
            self.three[c, k].wait_recv()
        return t2[c] + b3[c, 0].astype(F32) + b3[c, 1].astype(F32) + b3[c, 2].astype(F32)

    def finish(self):
        for c in self.one:
            self.one[c].wait_send()
            self.two[c].wait_send()
            for k in range(3):
                self.three[c, k].wait_send()


def scatter_bufs(rows, cols):
    n, r, w = CUTS, rows // PIECES, cols // PARTS
    return [
        VMEM((n, 4, 2, r, w), BF),
        VMEM((n, 4, r, w), F32),
        VMEM((n, 4, r, w), BF),
        VMEM((n, r, w), F32),
        VMEM((n, 3, r, w), BF),
    ]


def scatter_sems():
    n = CUTS
    return [DMA((n,)), DMA((n,)), DMA((n,)), DMA((n,)), DMA((n, 3)), DMA((n, 3))]


def all_chips():
    h = lax.axis_index("hid")
    return [lax.rem(h + k, H) for k in range(1, H)]


class Queue:
    def __init__(self, *lists):
        size = max([len(jobs) for jobs in lists] + [1])
        placed = [
            (place * size / len(jobs), n, job)
            for n, jobs in enumerate(lists)
            for place, job in enumerate(jobs)
        ]
        self.jobs = [job for _, _, job in sorted(placed, key=lambda entry: entry[:2])]

    def run(self, number):
        for job in self.jobs[:number]:
            job()
        self.jobs = self.jobs[number:]

    def drain(self):
        self.run(len(self.jobs))


def unit_span(tiles, h):
    first = (tiles * h) // H
    return first, (tiles * (h + 1)) // H - first


def lanes(tile, count):
    return pl.ds(pl.multiple_of(tile * 128, 128), count * 128)


class Bulk:
    def __init__(self, items, tiles, depth, sems):
        self.items, self.tiles, self.depth = items, tiles, depth
        self.ss, self.rs, self.ls, self.xs, self.xr = sems
        self.least = tiles // H

    def sized(self, n, chip, act):
        if not self.items[n][3]:
            act(chip, 1)
            return
        first, count = unit_span(self.tiles, chip)
        if self.tiles % H == 0:
            act(first, self.least)
            return
        for number in (self.least, self.least + 1):
            pl.when(count == number)(functools.partial(act, first, number))

    def ours(self, view):
        half = H * self.depth
        return pl.ds(pl.multiple_of(view * half, half), half)

    def row(self, core, chip):
        return pl.ds(pl.multiple_of((core * H + chip) * self.depth, self.depth), self.depth)


class Fetch(Bulk):
    def copy(self, n, k, chip, first, count):
        h, b = lax.axis_index("hid"), lax.axis_index("seq")
        src, dst, at, _ = self.items[n]
        return to_chip(
            src.at[:, lanes(first, count)],
            dst.at[self.row(b, h), lanes(at, count)],
            self.ss.at[n, k],
            self.rs.at[n, k],
            chip,
        )

    def own(self, n, first, count):
        h, b = lax.axis_index("hid"), lax.axis_index("seq")
        src, dst, at, _ = self.items[n]
        return pltpu.make_async_copy(
            src.at[:, lanes(first, count)], dst.at[self.row(b, h), lanes(at, count)], self.ls.at[n]
        )

    def job(self, n, k):
        def run():
            chip = lax.rem(lax.axis_index("hid") + k, H)
            self.sized(
                n, chip, lambda first, count: self.copy(n, k, chip, first, count).start()
            )

        return run

    def jobs(self):
        return [self.job(n, k) for n in range(len(self.items)) for k in range(1, H)]

    def start_own(self):
        h = lax.axis_index("hid")
        for n, (_, dst, _, split) in enumerate(self.items):
            self.sized(n, h, lambda first, count: self.own(n, first, count).start())
            if split and self.tiles % H:

                @pl.when(unit_span(self.tiles, h)[1] == self.least)
                def _():
                    dst[:, self.least * 128 :] = jnp.zeros((dst.shape[0], 128), BF)

    def swap(self, n, tile, count, slot):
        b = lax.axis_index("seq")
        view = self.items[n][1].at[self.ours(b), lanes(tile, count)]
        return to_core(view, view, self.xs.at[n, slot], self.xr.at[n, slot])

    def each_swap(self, n, act):
        at, split = self.items[n][2:]
        act(self.swap(n, at, self.least if split else 1, 0))
        if split and self.tiles % H:

            @pl.when(unit_span(self.tiles, lax.axis_index("hid"))[1] > self.least)
            def _():
                act(self.swap(n, self.least, 1, 1))

    def arrive(self, n):
        h = lax.axis_index("hid")
        self.sized(n, h, lambda first, count: self.own(n, first, count).wait())
        for k in range(1, H):
            self.sized(
                n, h, lambda first, count: self.copy(n, k, h, first, count).wait_recv()
            )
        self.each_swap(n, lambda copy: copy.start())

    def settle(self, ns):
        for n in ns:
            self.each_swap(n, lambda copy: copy.wait())

    def finish(self):
        for n in range(len(self.items)):
            for k in range(1, H):
                chip = lax.rem(lax.axis_index("hid") + k, H)
                self.sized(
                    n, chip, lambda first, count: self.copy(n, k, chip, first, count).wait_send()
                )


class Return(Bulk):
    def __init__(self, items, parts, tiles, depth, sems):
        super().__init__(items, tiles, depth, sems)
        self.parts = parts

    def swap(self, p):
        part, total, _ = self.parts[p]
        return to_core(
            part.at[self.ours(1 - lax.axis_index("seq"))], total, self.xs.at[p, 0], self.xr.at[p, 0]
        )

    def add(self, p):
        def run():
            part, total, _ = self.parts[p]
            b = lax.axis_index("seq")
            self.swap(p).wait()
            half, step = total.shape[0], 128

            @pl.loop(0, half // step)
            def _(t):
                at = pl.ds(pl.multiple_of(t * step, step), step)
                own = pl.ds(pl.multiple_of(b * half + t * step, step), step)
                total[at] = (total[at].astype(F32) + part[own].astype(F32)).astype(BF)

            for n in self.parts[p][2]:
                h = lax.axis_index("hid")
                self.sized(n, h, lambda first, count: self.own(n, first, count).start())

        return run

    def copy(self, n, k, chip, first, count):
        dst, src, at, _ = self.items[n]
        return to_chip(
            src.at[self.row(0, chip), lanes(at, count)],
            dst.at[:, lanes(first, count)],
            self.ss.at[n, k],
            self.rs.at[n, k],
            chip,
        )

    def own(self, n, first, count):
        dst, src, at, _ = self.items[n]
        return pltpu.make_async_copy(
            src.at[self.row(0, lax.axis_index("hid")), lanes(at, count)],
            dst.at[:, lanes(first, count)],
            self.ls.at[n],
        )

    def job(self, n, k):
        def run():
            h = lax.axis_index("hid")
            chip = lax.rem(h + k, H)
            self.sized(n, h, lambda first, count: self.copy(n, k, chip, first, count).start())

        return run

    def jobs(self, p):
        return [self.add(p)] + [self.job(n, k) for n in self.parts[p][2] for k in range(1, H)]

    def finish(self):
        h = lax.axis_index("hid")
        for n in range(len(self.items)):
            self.sized(n, h, lambda first, count: self.own(n, first, count).wait())
            for k in range(1, H):
                chip, source = lax.rem(h + k, H), lax.rem(h + H - k, H)
                self.sized(
                    n, source, lambda first, count: self.copy(n, k, chip, first, count).wait_recv()
                )
                self.sized(
                    n, h, lambda first, count: self.copy(n, k, chip, first, count).wait_send()
                )


def bulk_sems(n):
    return [DMA((n, H)), DMA((n, H)), DMA((n,)), DMA((n, 2)), DMA((n, 2))]


def split_refs(refs, *counts):
    groups, at = [], 0
    for count in counts:
        groups.append(refs[at : at + count])
        at += count
    assert at == len(refs)
    return groups


def row_norm(rows):
    return lax.rsqrt(jnp.mean(rows * rows, axis=-1, keepdims=True) + EPS)


def gather_jobs(gather, ahead):
    lag = PARTS

    def step(t):
        def run():
            if t == 0:
                for c in range(ahead):
                    gather.start(c)
            if t < CUTS:
                gather.second(t)
                if t + ahead < CUTS:
                    gather.start(t + ahead)
            if t >= lag:
                gather.third(t - lag)

        return run

    return [step(t) for t in range(CUTS + lag)]


def scatter_jobs(scatter, ahead, rows_done):
    lag, held = PARTS, []

    def step(t):
        def run():
            if t == 0:
                for c in range(ahead):
                    scatter.start(c)
            if t < CUTS:
                scatter.second(t)
                if t + ahead < CUTS:
                    scatter.start(t + ahead)
            if 0 <= t - lag // 2 < CUTS:
                scatter.third(t - lag // 2)
            c = t - lag - lag // 2
            if c >= 0:
                held.append(scatter.last(c))
                if len(held) == PARTS:
                    rows_done(c // PARTS, jnp.concatenate(held, axis=1))
                    held.clear()

        return run

    return [step(t) for t in range(CUTS + lag + lag // 2)]


def turn_jobs(scatter, gather, ahead, rows_done):
    lag = PARTS

    def write(i, rows):
        rows_done(i, rows)
        if i == PIECES - 1:
            scatter.finish()
        for c in range(i * PARTS, (i + 1) * PARTS):
            gather.start(c)

    first = scatter_jobs(scatter, ahead, write)

    def step(t):
        def run():
            if t < len(first):
                first[t]()
            c = t - 2 * lag - lag // 2 - (PARTS - 1)
            if 0 <= c < CUTS:
                gather.second(c)
            if 0 <= c - lag < CUTS:
                gather.third(c - lag)

        return run

    return [step(t) for t in range(CUTS + 3 * lag + lag // 2 + PARTS - 1)]


def norm_back(rows, grad, gain):
    factor = row_norm(rows)
    normal = rows * factor
    scaled = grad * gain
    back = factor * (scaled - normal * jnp.mean(scaled * normal, axis=-1, keepdims=True))
    return back, jnp.sum(grad * normal, axis=0, keepdims=True)


def row_blocks(ref):
    size = 2 * ref.shape[1] * ref.shape[2] * ref.shape[3]
    return [(pl.ds(2 * n, 2), pl.ds(n * size, size)) for n in range(ref.shape[0] // 2)]


def merged(rows):
    return rows.reshape(-1, rows.shape[-1])


def doc_tile(lengths_ref, start, shape, dim):
    positions = start + lax.broadcasted_iota(jnp.int32, shape, dim)
    documents = jnp.full(shape, -1, jnp.int32)
    begin = jnp.int32(0)
    for n in range(lengths_ref.shape[0]):
        documents = documents + jnp.where(positions >= begin, 1, 0)
        begin = begin + lengths_ref[n]
    return documents


def layer_kernel(tiles, *refs):
    (
        (x_ref, c_ref, lengths, first_gain, second_gain, gain_ref, gap_all),
        weights,
        (out, in_grad, totals, *homes),
        (first, cot, second, mix, part, glu_part),
        (wqfi, wo, wg, wu, wd),
        (entry, middle, mid, dcol, drow, gap_ref),
        (lin, mixed, states, head, cum, d_head, d_lin, d_mixed, backs),
        (hidden, gate_low, up_low),
        (gqfi, go, gg, gu, gd),
        (tqfi, to, tg, tu, td),
        main_bufs,
        glu_bufs,
        gather_sets,
        scatter_sets,
        (f_out, f_in, b_out, b_in, fs, fr, bs, br, ls),
        (mine, theirs, chips, vs, vr, ws, wr),
        bulk_sets,
    ) = split_refs(refs, 7, 7, 10, 6, 5, 6, 9, 3, 5, 5, 5, 5, 24, 24, 9, 7, 20)
    q, f, i, o, g, u, d = weights
    hq, hf, hi, ho, hg, hu, hd = homes
    h, z, y, x = place()
    core = lax.axis_index("seq")
    depth, size = q.shape[0], x_ref.shape[1] // PIECES
    extent = lin.shape[0]
    mixer_in = Fetch(
        [(q, wqfi, 0, False), (f, wqfi, 1, False), (i, wqfi, 2, False), (o, wo, 0, False)],
        H,
        depth,
        bulk_sets[0:5],
    )
    units_in = Fetch(
        [(g, wg, 0, True), (u, wu, 0, True), (d, wd, 0, True)], tiles, depth, bulk_sets[5:10]
    )
    units_out = Return(
        [(hd, td, 0, True), (hg, tg, 0, True), (hu, tu, 0, True)],
        [(gd, td, (0,)), (gg, tg, (1,)), (gu, tu, (2,))],
        tiles,
        depth,
        bulk_sets[10:15],
    )
    mixer_out = Return(
        [(ho, to, 0, False), (hq, tqfi, 0, False), (hf, tqfi, 1, False), (hi, tqfi, 2, False)],
        [(go, to, (0,)), (gqfi, tqfi, (1, 2, 3))],
        H,
        depth,
        bulk_sets[15:20],
    )
    gathers = [
        Gather(ref, gather_sets[6 * n : 6 * n + 6])
        for n, ref in enumerate((first, cot, second, mix))
    ]
    scatters = [
        Scatter(ref, bufs, scatter_sets[6 * n : 6 * n + 6])
        for n, (ref, bufs) in enumerate(
            ((part, main_bufs), (part, main_bufs), (part, main_bufs), (glu_part, glu_bufs))
        )
    ]

    own = pltpu.make_async_copy(c_ref.at[0], cot.at[z, y, x], ls)
    own.start()
    mixer_in.start_own()
    for n in range(PIECES):
        at = pl.ds(n * size, size)
        rows = x_ref[0, at].astype(F32)
        entry[at] = rows
        first[z, y, x, at] = (rows * row_norm(rows) * first_gain[...]).astype(BF)
    greet(all_chips(), core=True)
    own.wait()

    def documents():
        gap_ref[...] = gap_all[pl.ds(h, 1)]
        base = core * extent
        for c, at in spans(extent):
            dcol[at] = doc_tile(lengths, base + c * SPAN, (SPAN, SPAN), 0)
            drow[8 * c : 8 * c + 8] = doc_tile(lengths, base + c * SPAN, (8, SPAN), 1)
        drow[8 * len(spans(extent)) :] = doc_tile(lengths, base - 1, (8, SPAN), 0)
        mine[...] = jnp.zeros_like(mine)
        units_in.start_own()

    mixer_jobs = mixer_in.jobs()
    queue = Queue([documents] + mixer_jobs[: 3 * (H - 1)])
    for job in gather_jobs(gathers[0], AHEAD[0]):
        job()
        queue.run(PACE[0])
    queue.drain()
    unit_jobs = units_in.jobs()
    queue = Queue(mixer_jobs[3 * (H - 1) :])
    queue.jobs += Queue(unit_jobs, gather_jobs(gathers[1], AHEAD[1])).jobs
    queue.run(max(PACE[1], H - 1))
    for n in range(3):
        mixer_in.arrive(n)
    gathers[0].finish()
    mixer_in.settle((0, 1, 2))

    for n, at in row_blocks(first):
        lin[at] = jnp.dot(merged(first[n]), wqfi[...], preferred_element_type=F32)
        queue.run(PACE[2])
    blocks = (lin, gap_ref, gain_ref, dcol, drow)
    mix_forward(blocks, mixed, states, head, cum, (f_out, f_in, fs, fr), lambda: queue.run(PACE[2]))
    mixer_in.arrive(3)
    mixer_in.settle((3,))
    for n, at in row_blocks(part):
        part[n] = times_t(head[at], wo[...]).astype(BF).reshape((2,) + part.shape[1:])

    def middle_rows(n, total):
        at = pl.ds(n * size, size)
        rows = entry[at] + total
        middle[at] = rows
        second[z, y, x, at] = (rows * row_norm(rows) * second_gain[...]).astype(BF)

    for job in turn_jobs(scatters[0], gathers[2], AHEAD[2], middle_rows):
        job()
        queue.run(PACE[3])
    queue.drain()
    for n in range(3):
        units_in.arrive(n)
    gathers[1].finish()
    gathers[2].finish()
    mixer_in.finish()
    units_in.settle((0, 1, 2))
    units_in.finish()

    for n, at in row_blocks(second):
        rows = merged(second[n])
        gate_lin = jnp.dot(rows, wg[...], preferred_element_type=F32)
        up_lin = jnp.dot(rows, wu[...], preferred_element_type=F32)
        d_hidden = jnp.dot(merged(cot[n]), wd[...], preferred_element_type=F32)
        s = jax.nn.sigmoid(gate_lin)
        silu = gate_lin * s
        hidden[at] = (silu * up_lin).astype(BF)
        gate_low[at] = (d_hidden * up_lin * s * (1.0 + gate_lin * (1.0 - s))).astype(BF)
        up_low[at] = (d_hidden * silu).astype(BF)
        total = times_t(gate_low[at], wg[...]) + times_t(up_low[at], wu[...])
        part[n] = total.astype(BF).reshape((2,) + part.shape[1:])

    def grad_rows(n, total):
        at = pl.ds(n * size, size)
        back, gains = norm_back(middle[at], total, second_gain[...])
        mine[16:32] = mine[16:32] + gains.reshape(16, 128)
        rows = c_ref[0, at].astype(F32) + back
        mid[at] = rows
        mix[z, y, x, at] = rows.astype(BF)

    def out_rows(n, total):
        at = pl.ds(n * size, size)
        out[0, at] = (middle[at] + total).astype(BF)

    def outer(dst, rows, cols, giver, p):
        width = 512

        def piece(start):
            def run():
                at = pl.ds(start, width)
                dst[at] = outer_sum(merged(rows[:, :, :, :, at]), cols[...]).astype(BF)

            return run

        return [piece(start) for start in range(0, rows.shape[4], width)] + [
            lambda: giver.swap(p).start()
        ]

    def glu_block(n, at):
        def run():
            rows = times_t(hidden[at], wd[...]).astype(BF)
            glu_part[n] = rows.reshape((2,) + glu_part.shape[1:])

        return run

    queue = Queue(outer(gd, cot, hidden, units_out, 0))
    queue.jobs += [glu_block(n, at) for n, at in row_blocks(glu_part)]
    queue.jobs += outer(gg, second, gate_low, units_out, 1)
    queue.jobs += Queue(
        units_out.jobs(0) + outer(gu, second, up_low, units_out, 2) + units_out.jobs(1) + units_out.jobs(2),
        scatter_jobs(scatters[3], AHEAD[4], out_rows),
    ).jobs
    for job in turn_jobs(scatters[1], gathers[3], AHEAD[3], grad_rows):
        job()
        queue.run(PACE[4])
    gathers[3].finish()

    queue.jobs = outer(go, mix, head, mixer_out, 0) + queue.jobs
    for n, at in row_blocks(mix):
        d_head[at] = jnp.dot(merged(mix[n]), wo[...], preferred_element_type=F32)
        queue.run(PACE[5])
    group, gap = mix_backward(
        blocks, mixed, states, cum, d_head, d_lin, d_mixed, backs, (b_out, b_in, bs, br),
        lambda: queue.run(PACE[5]),
    )
    mine[32:33] = group
    mine[40:41] = gap
    for n, at in row_blocks(part):
        part[n] = times_t(d_lin[at], wqfi[...]).astype(BF).reshape((2,) + part.shape[1:])
    sent = {}

    def in_rows(n, total):
        at = pl.ds(n * size, size)
        back, gains = norm_back(entry[at], total, first_gain[...])
        in_grad[0, at] = mid[at] + back
        mine[0:16] = mine[0:16] + gains.reshape(16, 128)
        if n == PIECES - 1:
            swap = to_core(mine, theirs, vs, vr)
            swap.start()
            swap.wait()
            chips[h] = mine[...] + theirs[...]
            for k in range(1, H):
                sent[k] = to_chip(
                    chips.at[h], chips.at[h], ws.at[k], wr.at[k], lax.rem(h + k, H)
                )
                sent[k].start()

    queue = Queue(
        queue.jobs, outer(gqfi, first, d_lin, mixer_out, 1) + mixer_out.jobs(0) + mixer_out.jobs(1)
    )
    for job in scatter_jobs(scatters[2], AHEAD[5], in_rows):
        job()
        queue.run(PACE[6])
    queue.drain()
    for k in range(1, H):
        sent[k].wait()
    acc = chips[0, 0:40]
    for chip in range(1, H):
        acc = acc + chips[chip, 0:40]
    totals[0:40] = acc
    for chip in range(H):
        totals[40 + chip : 41 + chip] = chips[chip, 40:41]
    scatters[2].finish()
    scatters[3].finish()
    units_out.finish()
    mixer_out.finish()


def layer(inputs, cotangent, lengths, first_gain, second_gain, group_gain, gap_log, weights):
    _, rows, cols = inputs.shape
    depth, units = weights[-1].shape
    extent, count = H * rows, 2 * H * depth
    tiles = units // 128
    wide = -(-tiles // H) * 128
    home = lambda width: jax.ShapeDtypeStruct((depth, width), BF)
    full = VMEM((4, 2, 2, rows, cols), BF)
    local = VMEM((rows, cols), F32)
    tile = VMEM((extent, SPAN), F32)
    square = VMEM((SPAN, SPAN), F32)
    squares = VMEM((extent // SPAN, SPAN, SPAN), F32)
    widths = (384, 128, wide, wide, wide)
    return pl.pallas_call(
        functools.partial(layer_kernel, tiles),
        out_shape=[
            jax.ShapeDtypeStruct((1, rows, cols), BF),
            jax.ShapeDtypeStruct((1, rows, cols), F32),
            jax.ShapeDtypeStruct((56, 128), F32),
        ]
        + [home(cols)] * 4
        + [home(units)] * 3,
        in_specs=[VSPEC] * 2 + [SSPEC] + [VSPEC] * 4 + [ASPEC] * 7,
        out_specs=[VSPEC] * 3 + [ASPEC] * 7,
        scratch_shapes=[full] * 6
        + [VMEM((count, width), BF) for width in widths]
        + [local, local, local, VMEM((extent, SPAN), jnp.int32)]
        + [VMEM((8 * (extent // SPAN) + 8, SPAN), jnp.int32), VMEM((1, SPAN), F32)]
        + [VMEM((extent, 384), F32), tile, squares, VMEM((extent, SPAN), BF), tile]
        + [tile, VMEM((extent, 384), BF), tile, squares]
        + [VMEM((extent, wide), BF)] * 3
        + [VMEM((count, width), BF) for width in widths]
        + [VMEM((count // 2, width), BF) for width in widths]
        + scatter_bufs(rows, cols)
        + scatter_bufs(rows, cols)
        + gather_sems() * 4
        + scatter_sems() * 4
        + [square] * 4
        + [DMA] * 5
        + [VMEM((48, 128), F32), VMEM((48, 128), F32), VMEM((H, 48, 128), F32)]
        + [DMA, DMA, DMA((H,)), DMA((H,))]
        + bulk_sems(4)
        + bulk_sems(3)
        + bulk_sems(3)
        + bulk_sems(4),
        compiler_params=comm_params(1),
    )(
        inputs,
        cotangent,
        lengths,
        first_gain[None],
        second_gain[None],
        group_gain[None],
        gap_log.reshape(H, SPAN),
        *weights,
    )


def mm(left, right, at_left, at_right):
    return lax.dot_general(
        left.astype(BF),
        right.astype(BF),
        (((at_left,), (at_right,)), ((), ())),
        preferred_element_type=F32,
    )


def tri_sum(rows, reverse=False):
    r = lax.broadcasted_iota(jnp.int32, (SPAN, SPAN), 0)
    c = lax.broadcasted_iota(jnp.int32, (SPAN, SPAN), 1)
    picked = jnp.where((r <= c) if reverse else (r >= c), 1.0, 0.0).astype(BF)
    high = rows.astype(BF)
    rest = rows - high.astype(F32)
    middle = rest.astype(BF)
    low = rest - middle.astype(F32)
    return mm(picked, high, 1, 0) + mm(picked, middle, 1, 0) + mm(picked, low, 1, 0)


def span_gates(lin_ref, gap_ref, at):
    q_lin, f_lin, values = lin_ref[at, 0:128], lin_ref[at, 128:256], lin_ref[at, 256:384]
    s = jax.nn.sigmoid(q_lin)
    key = jnp.exp(gap_ref[...]) * jax.nn.sigmoid(-f_lin)
    return q_lin, f_lin, values, s, key


def span_masks(dcol_ref, drow_ref, c, at):
    r = lax.broadcasted_iota(jnp.int32, (SPAN, SPAN), 0)
    k = lax.broadcasted_iota(jnp.int32, (SPAN, SPAN), 1)
    dcol, drow = dcol_ref[at], drow_ref[8 * c : 8 * c + 1]
    last = (c + 1) * SPAN - 1
    end = dcol_ref[last : last + 1]
    if c:
        before = dcol_ref[c * SPAN - 1 : c * SPAN]
    else:
        count = drow_ref.shape[0]
        before = drow_ref[count - 8 : count - 7]
    same = jnp.where(jnp.logical_and(dcol == drow, r >= k), 1.0, 0.0)
    carried = jnp.where(dcol == before, 1.0, 0.0)
    keep = jnp.where(dcol == end, 1.0, 0.0)
    whole = jnp.where(end == before, 1.0, 0.0)
    return same, carried, keep, whole


def spans(extent):
    return [(c, pl.ds(c * SPAN, SPAN)) for c in range(extent // SPAN)]


def mix_forward(blocks, mixed_ref, states_ref, head_ref, cum_ref, handover, between):
    out_ref, in_ref, send, recv = handover
    lin_ref, gap_ref, gain_ref, dcol_ref, drow_ref = blocks
    steps = spans(lin_ref.shape[0])
    state = jnp.zeros((SPAN, SPAN), F32)
    for c, at in steps:
        q_lin, f_lin, values, s, key = span_gates(lin_ref, gap_ref, at)
        same, carried, keep, whole = span_masks(dcol_ref, drow_ref, c, at)
        cum = tri_sum(jnp.log1p(-key))
        cum_ref[at] = cum
        end = cum[SPAN - 1 : SPAN]
        fresh = mm(values, jnp.exp(end - cum) * key * keep, 0, 0)
        states_ref[c] = fresh
        state = state * (jnp.exp(end) * whole) + fresh
    out_ref[...] = state
    copy = to_core(out_ref, in_ref, send, recv)
    copy.start()
    between()
    copy.wait()
    state = in_ref[...] * lax.axis_index("seq").astype(F32)
    for c, at in steps:
        q_lin, f_lin, values, s, key = span_gates(lin_ref, gap_ref, at)
        same, carried, keep, whole = span_masks(dcol_ref, drow_ref, c, at)
        cum = cum_ref[at]
        end = cum[SPAN - 1 : SPAN]
        fresh = states_ref[c]
        states_ref[c] = state
        decayed = q_lin * s * jnp.exp(cum)
        scores = mm(decayed, key * jnp.exp(-cum), 1, 1) * same
        mixed = mm(scores, values, 1, 0) + carried * mm(decayed, state, 1, 1)
        mixed_ref[at] = mixed
        head_ref[at] = (mixed * row_norm(mixed) * gain_ref[...]).astype(BF)
        state = state * (jnp.exp(end) * whole) + fresh
        if c % 2:
            between()


def mix_backward(
    blocks, mixed_ref, states_ref, cum_ref, dhead_ref, dlin_ref, do_ref, back_ref, handover, between
):
    out_ref, in_ref, send, recv = handover
    lin_ref, gap_ref, gain_ref, dcol_ref, drow_ref = blocks
    steps = spans(lin_ref.shape[0])
    group = jnp.zeros((1, SPAN), F32)
    adjoint = jnp.zeros((SPAN, SPAN), F32)
    for c, at in reversed(steps):
        d_mixed, gains = norm_back(mixed_ref[at], dhead_ref[at], gain_ref[...])
        group = group + gains
        do_ref[at] = d_mixed
        q_lin, f_lin, values, s, key = span_gates(lin_ref, gap_ref, at)
        same, carried, keep, whole = span_masks(dcol_ref, drow_ref, c, at)
        cum = cum_ref[at]
        back = mm(d_mixed, carried * (q_lin * s * jnp.exp(cum)), 0, 0)
        back_ref[c] = back
        adjoint = adjoint * (jnp.exp(cum[SPAN - 1 : SPAN]) * whole) + back
    out_ref[...] = adjoint
    copy = to_core(out_ref, in_ref, send, recv)
    copy.start()
    between()
    copy.wait()
    adjoint = in_ref[...] * (1 - lax.axis_index("seq")).astype(F32)
    gap = jnp.zeros((1, SPAN), F32)
    for c, at in reversed(steps):
        q_lin, f_lin, values, s, key = span_gates(lin_ref, gap_ref, at)
        same, carried, keep, whole = span_masks(dcol_ref, drow_ref, c, at)
        cum, d_mixed, state = cum_ref[at], do_ref[at], states_ref[c]
        grow, shrink = jnp.exp(-cum), jnp.exp(cum)
        end = cum[SPAN - 1 : SPAN]
        decayed, grown = q_lin * s * shrink, key * grow
        rest = jnp.exp(end - cum) * keep
        tail, through = rest * key, jnp.exp(end) * whole
        scores = mm(decayed, grown, 1, 1) * same
        d_scores = mm(d_mixed, values, 1, 1) * same
        d_values = mm(scores, d_mixed, 0, 0) + mm(tail, adjoint, 1, 1)
        d_decayed = mm(d_scores, grown, 1, 0) + carried * mm(d_mixed, state, 1, 0)
        d_grown = mm(d_scores, decayed, 0, 0)
        d_tail = mm(values, adjoint, 1, 0)
        held = tail * d_tail
        d_cum = decayed * d_decayed - grown * d_grown - held
        d_end = jnp.sum(held, axis=0, keepdims=True) + through * jnp.sum(
            state * adjoint, axis=0, keepdims=True
        )
        d_log = tri_sum(d_cum, reverse=True) + d_end
        d_key = d_grown * grow + d_tail * rest - d_log / (1.0 - key)
        scaled = d_key * key
        gap = gap + jnp.sum(scaled, axis=0, keepdims=True)
        dlin_ref[at, 0:128] = (d_decayed * shrink * s * (1.0 + q_lin * (1.0 - s))).astype(BF)
        dlin_ref[at, 128:256] = (-scaled * jax.nn.sigmoid(f_lin)).astype(BF)
        dlin_ref[at, 256:384] = d_values.astype(BF)
        adjoint = adjoint * through + back_ref[c]
        if c % 2:
            between()
    return group, gap


def fast_body(
    inputs,
    cotangent,
    lengths,
    first_gain,
    q_weight,
    f_weight,
    i_weight,
    o_weight,
    group_gain,
    gap_log,
    second_gain,
    gate_weight,
    up_weight,
    down_weight,
):
    model = inputs.shape[2]
    output, input_grad, totals, *grads = layer(
        inputs,
        cotangent,
        lengths,
        first_gain,
        second_gain,
        group_gain,
        gap_log,
        (q_weight, f_weight, i_weight, o_weight, gate_weight, up_weight, down_weight),
    )
    q_grad, f_grad, i_grad, o_grad, gate_grad, up_grad, down_grad = (
        grad.astype(F32) for grad in grads
    )
    return (
        output,
        input_grad,
        totals[0:16].reshape(model),
        q_grad,
        f_grad,
        i_grad,
        o_grad,
        totals[32],
        totals[40:56].reshape(model),
        totals[16:32].reshape(model),
        gate_grad,
        up_grad,
        down_grad,
    )


def solution(mesh):
    placed = (
        P("seq", "hid", None),
        P("seq", "hid", None),
        P(),
        P(),
        P(("seq", "hid"), None),
        P(("seq", "hid"), None),
        P(("seq", "hid"), None),
        P(("seq", "hid"), None),
        P(),
        P(),
        P(),
        P(("seq", "hid"), None),
        P(("seq", "hid"), None),
        P(("seq", "hid"), None),
    )
    body = fast_body if mesh.shape["hid"] == H else wide_body
    return jax.shard_map(
        body,
        mesh=mesh,
        in_specs=placed,
        out_specs=(
            P("seq", "hid", None),
            P("seq", "hid", None),
            P(),
            P(("seq", "hid"), None),
            P(("seq", "hid"), None),
            P(("seq", "hid"), None),
            P(("seq", "hid"), None),
            P(),
            P(),
            P(),
            P(("seq", "hid"), None),
            P(("seq", "hid"), None),
            P(("seq", "hid"), None),
        ),
        check_vma=False,
    )
```

```python
import functools

import jax
import jax.numpy as jnp
from jax import lax
from jax.experimental import pallas as pl
from jax.experimental.pallas import tpu as pltpu
from jax.sharding import PartitionSpec as P

H = 16
SPAN = 128


EPS = 1e-06
HIGH_PRECISION = lax.Precision.HIGHEST


def from_behind(block, axis, distance):
    devices = range(lax.axis_size(axis))
    route = [(i - distance, i) for i in devices if i - distance in devices]
    return lax.ppermute(block, axis, route)


def normed(entries, gain_vec):
    factor = lax.rsqrt(jnp.mean(entries * entries, axis=-1, keepdims=True) + EPS)
    return entries * factor * gain_vec


def gates(q_part, f_part, gap_piece):
    key_gate = jnp.exp(gap_piece) * jax.nn.sigmoid(-f_part)
    return (jax.nn.silu(q_part), key_gate, jnp.log1p(-key_gate))


def doc_starts(lengths):
    count = lengths.shape[0]
    earlier = lax.broadcasted_iota(jnp.int32, (count, count), 0) > lax.broadcasted_iota(
        jnp.int32, (count, count), 1
    )
    return jnp.sum(jnp.where(earlier, lengths[None, :], 0), axis=1)


def running_sum(rows):
    extent = rows.shape[-2]
    lower = (
        lax.broadcasted_iota(jnp.int32, (extent, extent), 0)
        >= lax.broadcasted_iota(jnp.int32, (extent, extent), 1)
    ).astype(jnp.float32)
    return jnp.einsum("ts,...sk->...tk", lower, rows, precision=HIGH_PRECISION)


def doc_ids(lengths, positions):
    starts = doc_starts(lengths)
    covered = (starts[None, :] <= positions[:, None]).astype(jnp.int32)
    return jnp.sum(covered, axis=1) - 1


def span_step(memory_state, pieces):
    queries, key_gate, value_rows, log_decay, documents, before = pieces
    cumulative = running_sum(log_decay)
    query_decayed = queries * jnp.exp(cumulative)
    k_grown = key_gate * jnp.exp(-cumulative)
    extent = documents.shape[0]
    row_ids = lax.broadcasted_iota(jnp.int32, (extent, extent), 0)
    col_ids = lax.broadcasted_iota(jnp.int32, (extent, extent), 1)
    same_doc = jnp.logical_and(documents[:, None] == documents[None, :], row_ids >= col_ids).astype(
        jnp.float32
    )
    scores = (
        jnp.einsum("hck,hsk->hcs", query_decayed, k_grown, precision=HIGH_PRECISION)
        * same_doc[None]
    )
    within_block = jnp.einsum("hcs,hsv->hcv", scores, value_rows, precision=HIGH_PRECISION)
    carried_state = (documents == before).astype(jnp.float32)[None, :, None]
    output_rows = within_block + carried_state * jnp.einsum(
        "awn,ani->awi", query_decayed, memory_state, precision=HIGH_PRECISION
    )
    last_cum = cumulative[:, -1:, :]
    keep_mask = (documents == documents[-1]).astype(jnp.float32)[None, :, None]
    tail_key_rows = jnp.exp(last_cum - cumulative) * key_gate * keep_mask
    whole_block = (documents[-1] == before).astype(jnp.float32)
    fresh_state = jnp.einsum("wfx,wfg->wxg", tail_key_rows, value_rows, precision=HIGH_PRECISION)
    memory_state = jnp.exp(last_cum[:, 0, :])[:, :, None] * whole_block * memory_state + fresh_state
    return (memory_state, output_rows)


def recur(queries, key_gate, value_rows, log_decay, documents, before, memory_state):
    head_count, extent, columns = queries.shape
    span_count = extent // SPAN

    def by_span(tensor):
        return jnp.swapaxes(tensor.reshape(head_count, span_count, SPAN, tensor.shape[-1]), 0, 1)

    doc_rows = documents.reshape(span_count, SPAN)
    befores = jnp.concatenate([jnp.reshape(before, (1,)), doc_rows[:-1, -1]])
    memory_state, span_out = lax.scan(
        jax.checkpoint(span_step),
        memory_state,
        (
            by_span(queries),
            by_span(key_gate),
            by_span(value_rows),
            by_span(log_decay),
            doc_rows,
            befores,
        ),
    )
    return (
        jnp.swapaxes(span_out, 0, 1).reshape(head_count, extent, value_rows.shape[-1]),
        memory_state,
    )


def spread_cols(weight, copies):
    row_count = weight.shape[0]
    shaped = weight.reshape(row_count, 1, H, weight.shape[1] // H)
    return jnp.broadcast_to(shaped, (row_count, copies, H, shaped.shape[3])).reshape(
        row_count, copies * weight.shape[1]
    )


def fold_copies(received, copies):
    row_count = received.shape[0]
    return jnp.sum(received.reshape(row_count, copies, received.shape[1] // copies), axis=1)


def fan_rows(local_rows):
    blocks_here, row_count, columns = local_rows.shape
    return jnp.broadcast_to(local_rows[:, None], (blocks_here, H, row_count, columns)).reshape(
        blocks_here * H * row_count, columns
    )


def sum_heads(received, blocks_here):
    total_rows, columns = received.shape
    return jnp.sum(
        received.reshape(blocks_here, H, total_rows // (blocks_here * H), columns), axis=1
    )


def times_t(left_mat, right_mat):
    return lax.dot_general(
        left_mat, right_mat, (((1,), (1,)), ((), ())), preferred_element_type=jnp.float32
    )


def outer_sum(left_mat, right_mat):
    return lax.dot_general(
        left_mat, right_mat, (((0,), (0,)), ((), ())), preferred_element_type=jnp.float32
    )


def outer_high(left_mat, right_mat):
    return lax.dot_general(
        left_mat,
        right_mat,
        (((0,), (0,)), ((), ())),
        precision=HIGH_PRECISION,
        preferred_element_type=jnp.float32,
    )


def wide_body(
    inputs,
    cotangent,
    lengths,
    first_gain,
    q_weight,
    f_weight,
    i_weight,
    o_weight,
    group_gain,
    gap_log,
    second_gain,
    gate_weight,
    up_weight,
    down_weight,
):
    hid_size = lax.axis_size("hid")
    per_seq = hid_size // H
    block_total = lax.axis_size("seq") * per_seq
    hid_place = lax.axis_index("hid")
    head_id = hid_place % H
    block_id = lax.axis_index("seq") * per_seq + hid_place // H
    model = inputs.shape[2]
    head_width = model // H
    block_len = hid_size * inputs.shape[1]
    entries = inputs.astype(jnp.float32)
    q_block, f_block, i_block, o_block, gate_block, up_block, down_block = (
        lax.all_to_all(
            spread_cols(q_weight, block_total),
            ("seq", "hid"),
            split_axis=1,
            concat_axis=0,
            tiled=True,
        ),
        lax.all_to_all(
            spread_cols(f_weight, block_total),
            ("seq", "hid"),
            split_axis=1,
            concat_axis=0,
            tiled=True,
        ),
        lax.all_to_all(
            spread_cols(i_weight, block_total),
            ("seq", "hid"),
            split_axis=1,
            concat_axis=0,
            tiled=True,
        ),
        lax.all_to_all(
            spread_cols(o_weight, block_total),
            ("seq", "hid"),
            split_axis=1,
            concat_axis=0,
            tiled=True,
        ),
        lax.all_to_all(
            spread_cols(gate_weight, block_total),
            ("seq", "hid"),
            split_axis=1,
            concat_axis=0,
            tiled=True,
        ),
        lax.all_to_all(
            spread_cols(up_weight, block_total),
            ("seq", "hid"),
            split_axis=1,
            concat_axis=0,
            tiled=True,
        ),
        lax.all_to_all(
            spread_cols(down_weight, block_total),
            ("seq", "hid"),
            split_axis=1,
            concat_axis=0,
            tiled=True,
        ),
    )
    positions = block_id * block_len + lax.iota(jnp.int32, block_len)
    documents = doc_ids(lengths, positions)
    before = doc_ids(lengths, jnp.reshape(block_id * block_len - 1, (1,)))[0]
    first_norm, first_back = jax.vjp(normed, entries, first_gain)
    first_low = first_norm.astype(jnp.bfloat16)
    first_rows = lax.all_to_all(fan_rows(first_low), "hid", split_axis=0, concat_axis=0, tiled=True)
    q_lin = jnp.dot(first_rows, q_block, preferred_element_type=jnp.float32)
    f_lin = jnp.dot(first_rows, f_block, preferred_element_type=jnp.float32)
    i_lin = jnp.dot(first_rows, i_block, preferred_element_type=jnp.float32)
    gap_part = lax.dynamic_slice_in_dim(gap_log, head_id * head_width, head_width)
    queries, key_gate, log_decay = gates(q_lin, f_lin, gap_part)
    cumulative = running_sum(log_decay)
    last_cum = cumulative[-1]
    tail_key_rows = (
        jnp.exp(last_cum[None, :] - cumulative)
        * key_gate
        * (documents == documents[-1]).astype(jnp.float32)[:, None]
    )
    local_state = outer_high(tail_key_rows, i_lin)
    decay = jnp.exp(last_cum) * (documents[-1] == before).astype(jnp.float32)
    state_in = jnp.zeros_like(local_state)
    for number in range(block_total - 1):
        state_out = decay[:, None] * state_in + local_state
        state_in = from_behind(state_out.astype(jnp.bfloat16), ("seq", "hid"), H).astype(
            state_out.dtype
        )

    def core(q_part, f_part, i_part, gap_piece):
        queries_in, keys_in, logs_in = gates(q_part, f_part, gap_piece)
        mixed_all, memory_state = recur(
            queries_in[None],
            keys_in[None],
            i_part[None],
            logs_in[None],
            documents,
            before,
            state_in[None],
        )
        return (mixed_all[0], memory_state[0])

    (mixed_out, _), core_back = jax.vjp(core, q_lin, f_lin, i_lin, gap_part)
    head_normed, norm_back = jax.vjp(normed, mixed_out, group_gain)
    head_low = head_normed.astype(jnp.bfloat16)
    mix_out = sum_heads(
        lax.all_to_all(
            times_t(head_low, o_block).astype(jnp.bfloat16),
            "hid",
            split_axis=0,
            concat_axis=0,
            tiled=True,
        ).astype(jnp.float32),
        per_seq,
    )
    middle = entries + mix_out
    second_norm, second_back = jax.vjp(normed, middle, second_gain)
    second_low = second_norm.astype(jnp.bfloat16)
    second_rows, cot_rows = (
        lax.all_to_all(fan_rows(second_low), "hid", split_axis=0, concat_axis=0, tiled=True),
        lax.all_to_all(fan_rows(cotangent), "hid", split_axis=0, concat_axis=0, tiled=True),
    )
    gate_lin = jnp.dot(second_rows, gate_block, preferred_element_type=jnp.float32)
    up_lin = jnp.dot(second_rows, up_block, preferred_element_type=jnp.float32)
    hidden = (jax.nn.silu(gate_lin) * up_lin).astype(jnp.bfloat16)
    glu_out = sum_heads(
        lax.all_to_all(
            times_t(hidden, down_block).astype(jnp.bfloat16),
            "hid",
            split_axis=0,
            concat_axis=0,
            tiled=True,
        ).astype(jnp.float32),
        per_seq,
    )
    output = (middle + glu_out).astype(jnp.bfloat16)
    down_part = outer_sum(cot_rows, hidden)
    hidden_grad = jnp.dot(cot_rows, down_block, preferred_element_type=jnp.float32)
    gate_sig = jax.nn.sigmoid(gate_lin)
    gate_low = (hidden_grad * up_lin * gate_sig * (1.0 + gate_lin * (1.0 - gate_sig))).astype(
        jnp.bfloat16
    )
    up_low = (hidden_grad * gate_lin * gate_sig).astype(jnp.bfloat16)
    gate_part = outer_sum(second_rows, gate_low)
    up_part = outer_sum(second_rows, up_low)
    second_sum = lax.all_to_all(
        (times_t(gate_low, gate_block) + times_t(up_low, up_block)).astype(jnp.bfloat16),
        "hid",
        split_axis=0,
        concat_axis=0,
        tiled=True,
    ).astype(jnp.float32)
    middle_part, second_part = second_back(sum_heads(second_sum, per_seq))
    middle_grad = cotangent.astype(jnp.float32) + middle_part
    mix_grad = middle_grad.astype(jnp.bfloat16)
    mix_rows = lax.all_to_all(fan_rows(mix_grad), "hid", split_axis=0, concat_axis=0, tiled=True)
    normed_grad = jnp.dot(mix_rows, o_block, preferred_element_type=jnp.float32)
    o_part = outer_sum(mix_rows, head_low)
    mixed_grad, group_part = norm_back(normed_grad)
    carried_state = (documents == before).astype(jnp.float32)[:, None]
    grad_local = outer_high(queries * jnp.exp(cumulative) * carried_state, mixed_grad)
    state_grad = jnp.zeros_like(grad_local)
    for number in range(block_total - 1):
        grad_in = decay[:, None] * state_grad + grad_local
        state_grad = from_behind(grad_in.astype(jnp.bfloat16), ("seq", "hid"), -H).astype(
            grad_in.dtype
        )
    q_grad_lin, f_grad_lin, i_grad_lin, gap_piece_grad = core_back((mixed_grad, state_grad))
    q_low = q_grad_lin.astype(jnp.bfloat16)
    f_low = f_grad_lin.astype(jnp.bfloat16)
    i_low = i_grad_lin.astype(jnp.bfloat16)
    q_part = outer_sum(first_rows, q_low)
    f_part = outer_sum(first_rows, f_low)
    i_part = outer_sum(first_rows, i_low)
    first_sum = lax.all_to_all(
        (times_t(q_low, q_block) + times_t(f_low, f_block) + times_t(i_low, i_block)).astype(
            jnp.bfloat16
        ),
        "hid",
        split_axis=0,
        concat_axis=0,
        tiled=True,
    ).astype(jnp.float32)
    entry_part, first_part = first_back(sum_heads(first_sum, per_seq))
    input_grad = middle_grad + entry_part
    q_back, f_back, i_back, o_back, gate_back, up_back, down_back = (
        lax.all_to_all(
            q_part.astype(jnp.bfloat16), ("seq", "hid"), split_axis=0, concat_axis=1, tiled=True
        ).astype(q_part.dtype),
        lax.all_to_all(
            f_part.astype(jnp.bfloat16), ("seq", "hid"), split_axis=0, concat_axis=1, tiled=True
        ).astype(f_part.dtype),
        lax.all_to_all(
            i_part.astype(jnp.bfloat16), ("seq", "hid"), split_axis=0, concat_axis=1, tiled=True
        ).astype(i_part.dtype),
        lax.all_to_all(
            o_part.astype(jnp.bfloat16), ("seq", "hid"), split_axis=0, concat_axis=1, tiled=True
        ).astype(o_part.dtype),
        lax.all_to_all(
            gate_part.astype(jnp.bfloat16), ("seq", "hid"), split_axis=0, concat_axis=1, tiled=True
        ).astype(gate_part.dtype),
        lax.all_to_all(
            up_part.astype(jnp.bfloat16), ("seq", "hid"), split_axis=0, concat_axis=1, tiled=True
        ).astype(up_part.dtype),
        lax.all_to_all(
            down_part.astype(jnp.bfloat16), ("seq", "hid"), split_axis=0, concat_axis=1, tiled=True
        ).astype(down_part.dtype),
    )
    o_grad = fold_copies(o_back, block_total)
    head_pick = (lax.iota(jnp.int32, H) == head_id).astype(jnp.float32)
    gap_full = (head_pick[:, None] * gap_piece_grad[None, :]).reshape(model)
    first_grad, second_grad, group_grad, gap_grad = lax.psum(
        (first_part, second_part, group_part, gap_full), ("seq", "hid")
    )
    return (
        output,
        input_grad,
        first_grad,
        fold_copies(q_back, block_total),
        fold_copies(f_back, block_total),
        fold_copies(i_back, block_total),
        o_grad,
        group_grad,
        gap_grad,
        second_grad,
        fold_copies(gate_back, block_total),
        fold_copies(up_back, block_total),
        fold_copies(down_back, block_total),
    )


F32 = jnp.float32
BF = jnp.bfloat16
MESH = pl.DeviceIdType.MESH
DMA = pltpu.SemaphoreType.DMA
VMEM = pltpu.VMEM
PIECES = 3
PARTS = 4
CUTS = PIECES * PARTS
AHEAD = (4, 4, 4, 4, 4, 4)
PACE = (4, 8)
TIMES = ((4, 5), (-1, 1), (12, 4), (0, 2), (8, 1), (0, 8))
VSPEC = pl.BlockSpec(memory_space=pltpu.VMEM)
ASPEC = pl.BlockSpec(memory_space=pl.ANY)
SSPEC = pl.BlockSpec(memory_space=pltpu.SMEM)


def place():
    h = lax.axis_index("hid")
    return h, h // 4, lax.rem(h // 2, 2), lax.rem(h, 2)


def partners():
    h, z, y, x = place()
    column = [lax.rem(z + k, 4) * 4 + lax.rem(h, 4) for k in (1, 2, 3)]
    return column, h + 2 - 4 * y, h + 1 - 2 * x


def greet(chips, core=False):
    gate = pltpu.get_barrier_semaphore()
    for chip in chips:
        pl.semaphore_signal(gate, inc=1, device_id={"hid": chip}, device_id_type=MESH)
    if core:
        other = 1 - lax.axis_index("seq")
        pl.semaphore_signal(gate, inc=1, device_id={"seq": other}, device_id_type=MESH)
    pl.semaphore_wait(gate, len(chips) + int(core))


def to_chip(src, dst, send, recv, chip):
    return pltpu.make_async_remote_copy(
        src_ref=src,
        dst_ref=dst,
        send_sem=send,
        recv_sem=recv,
        device_id={"hid": chip},
        device_id_type=MESH,
    )


def to_core(src, dst, send, recv):
    return pltpu.make_async_remote_copy(
        src_ref=src,
        dst_ref=dst,
        send_sem=send,
        recv_sem=recv,
        device_id={"seq": 1 - lax.axis_index("seq")},
        device_id_type=MESH,
    )


def comm_params(collective_id):
    return pltpu.CompilerParams(
        collective_id=collective_id, has_side_effects=True, vmem_limit_bytes=62 << 20
    )


class Cuts:
    def cut(self, c):
        i, j = c // PARTS, c % PARTS
        rows, cols = self.ref.shape[3] // PIECES, self.ref.shape[4] // PARTS
        return pl.ds(i * rows, rows), pl.ds(j * cols, cols), j % 2


class Gather(Cuts):
    def __init__(self, ref, sems):
        self.ref = ref
        self.s1, self.s2, self.s3, self.r1, self.r2, self.r3 = sems

    def start(self, c):
        h, z, y, x = place()
        column, py, px = partners()
        a, b, j = self.cut(c)
        ref = self.ref.at[z, y, x, a, b]
        for k in range(3):
            to_chip(ref, ref, self.s1, self.r1.at[c], column[k]).start()

    def second(self, c):
        h, z, y, x = place()
        column, py, px = partners()
        a, b, j = self.cut(c)
        three = self.ref.at[0:3, y, x, a, b]
        to_chip(three, three, self.s1, self.r1.at[c], px).wait_recv()
        ref = self.ref.at[:, y, x, a, b]
        to_chip(ref, ref, self.s2, self.r2.at[c], py if j else px).start()

    def third(self, c):
        h, z, y, x = place()
        column, py, px = partners()
        a, b, j = self.cut(c)
        got = self.ref.at[:, y, x, a, b]
        to_chip(got, got, self.s2, self.r2.at[c], px).wait_recv()
        ref = self.ref.at[:, :, x, a, b] if j else self.ref.at[:, y, :, a, b]
        to_chip(ref, ref, self.s3, self.r3, px if j else py).start()

    def finish(self):
        h, z, y, x = place()
        half, quarter, three = self.ref.at[:, 0], self.ref.at[:, 0, 0], self.ref.at[0:3, 0, 0]
        to_chip(half, half, self.s3, self.r3, x).wait_recv()
        for ref, sem in ((three, self.s1), (quarter, self.s2), (half, self.s3)):
            to_chip(ref, ref, sem, self.r3, x).wait_send()


def gather_sems():
    return [DMA, DMA, DMA, DMA((CUTS,)), DMA((CUTS,)), DMA]


class Scatter(Cuts):
    def __init__(self, ref, bufs, sems):
        self.ref, self.bufs = ref, bufs
        self.s1, self.s2, self.s3, self.r1, self.r2, self.r3 = sems

    def start(self, c):
        h, z, y, x = place()
        column, py, px = partners()
        a, b, j = self.cut(c)
        src = self.ref.at[:, :, 1 - x, a, b] if j else self.ref.at[:, 1 - y, :, a, b]
        to_chip(src, self.bufs[0].at[c], self.s1, self.r1.at[c], px if j else py).start()

    def second(self, c):
        h, z, y, x = place()
        column, py, px = partners()
        b1, t1, b2 = self.bufs[:3]
        a, b, j = self.cut(c)
        q = y if j else x
        to_chip(b1.at[c], b1.at[c], self.s1, self.r1.at[c], px).wait_recv()
        theirs = self.ref[:, 1 - q, x, a, b] if j else self.ref[:, y, 1 - q, a, b]
        b1[c, :, 1 - q] = (theirs.astype(F32) + b1[c, :, 1 - q].astype(F32)).astype(BF)
        to_chip(b1.at[c, :, 1 - q], b2.at[c], self.s2, self.r2.at[c], py if j else px).start()
        mine = self.ref[:, q, x, a, b] if j else self.ref[:, y, q, a, b]
        t1[c] = mine.astype(F32) + b1[c, :, q].astype(F32)

    def third(self, c):
        h, z, y, x = place()
        column, py, px = partners()
        b1, t1, b2, t2, b3 = self.bufs
        to_chip(b2.at[c], b2.at[c], self.s2, self.r2.at[c], px).wait_recv()
        t2[c] = t1[c, z] + b2[c, z].astype(F32)
        b2[c] = (t1[c] + b2[c].astype(F32)).astype(BF)
        for k in range(3):
            to_chip(
                b2.at[c, lax.rem(z + k + 1, 4)], b3.at[c, k], self.s3, self.r3.at[c], column[k]
            ).start()

    def last(self, c):
        h, z, y, x = place()
        b3, t2 = self.bufs[4], self.bufs[3]
        to_chip(b3.at[c], b3.at[c], self.s3, self.r3.at[c], x).wait_recv()
        return t2[c] + b3[c, 0].astype(F32) + b3[c, 1].astype(F32) + b3[c, 2].astype(F32)

    def finish(self):
        h, z, y, x = place()
        whole = self.bufs[0].at[:], self.bufs[2].at[:], self.bufs[4].at[:]
        for ref, sem in zip(whole, (self.s1, self.s2, self.s3)):
            to_chip(ref, ref, sem, self.r1.at[0], x).wait_send()


def scatter_bufs(rows, cols):
    n, r, w = CUTS, rows // PIECES, cols // PARTS
    return [
        VMEM((n, 4, 2, r, w), BF),
        VMEM((n, 4, r, w), F32),
        VMEM((n, 4, r, w), BF),
        VMEM((n, r, w), F32),
        VMEM((n, 3, r, w), BF),
    ]


def scatter_sems():
    return [DMA, DMA, DMA, DMA((CUTS,)), DMA((CUTS,)), DMA((CUTS,))]


def all_chips():
    h = lax.axis_index("hid")
    return [lax.rem(h + k, H) for k in range(1, H)]


class Plan:
    def __init__(self, *entries):
        self.entries = [[list(jobs), start, pace] for jobs, start, pace in entries]

    def step(self, t):
        for entry in self.entries:
            jobs, start, pace = entry
            if t >= start:
                for job in jobs[:pace]:
                    job()
                entry[0] = jobs[pace:]

    def rest(self):
        for entry in self.entries:
            for job in entry[0]:
                job()
            entry[0] = []

    def left(self, n):
        jobs, self.entries[n][0] = self.entries[n][0], []
        return jobs

    def during(self, jobs):
        for t, job in enumerate(jobs):
            job()
            self.step(t)


def unit_span(tiles, h):
    first = (tiles * h) // H
    return first, (tiles * (h + 1)) // H - first


def lanes(tile, count):
    return pl.ds(pl.multiple_of(tile * 128, 128), count * 128)


class Bulk:
    def __init__(self, items, tiles, depth, sems):
        self.items, self.tiles, self.depth = items, tiles, depth
        self.ss, self.rs, self.ls, self.xs, self.xr = sems
        self.least = tiles // H

    def sized(self, n, chip, act):
        if not self.items[n][3]:
            act(chip, 1)
            return
        first, count = unit_span(self.tiles, chip)
        if self.tiles % H == 0:
            act(first, self.least)
            return
        for number in (self.least, self.least + 1):
            pl.when(count == number)(functools.partial(act, first, number))

    def ours(self, view):
        half = H * self.depth
        return pl.ds(pl.multiple_of(view * half, half), half)

    def row(self, core, chip):
        return pl.ds(pl.multiple_of((core * H + chip) * self.depth, self.depth), self.depth)


class Fetch(Bulk):
    def copy(self, n, k, chip, first, count):
        h, b = lax.axis_index("hid"), lax.axis_index("seq")
        src, dst, at, _ = self.items[n]
        return to_chip(
            src.at[:, lanes(first, count)],
            dst.at[self.row(b, h), lanes(at, count)],
            self.ss.at[n],
            self.rs.at[n],
            chip,
        )

    def own(self, n, first, count):
        h, b = lax.axis_index("hid"), lax.axis_index("seq")
        src, dst, at, _ = self.items[n]
        return pltpu.make_async_copy(
            src.at[:, lanes(first, count)], dst.at[self.row(b, h), lanes(at, count)], self.ls.at[n]
        )

    def job(self, n, k):
        def run():
            chip = lax.rem(lax.axis_index("hid") + k, H)
            self.sized(
                n, chip, lambda first, count: self.copy(n, k, chip, first, count).start()
            )

        return run

    def jobs(self):
        return [self.job(n, k) for n in range(len(self.items)) for k in range(1, H)]

    def start_own(self):
        h = lax.axis_index("hid")
        for n, (_, dst, _, split) in enumerate(self.items):
            self.sized(n, h, lambda first, count: self.own(n, first, count).start())
            if split and self.tiles % H:

                @pl.when(unit_span(self.tiles, h)[1] == self.least)
                def _():
                    dst[:, self.least * 128 :] = jnp.zeros((dst.shape[0], 128), BF)

    def swap(self, n, tile, count, slot):
        b = lax.axis_index("seq")
        view = self.items[n][1].at[self.ours(b), lanes(tile, count)]
        return to_core(view, view, self.xs.at[n, slot], self.xr.at[n, slot])

    def each_swap(self, n, act):
        at, split = self.items[n][2:]
        act(self.swap(n, at, self.least if split else 1, 0))
        if split and self.tiles % H:

            @pl.when(unit_span(self.tiles, lax.axis_index("hid"))[1] > self.least)
            def _():
                act(self.swap(n, self.least, 1, 1))

    def arrive(self, n):
        h = lax.axis_index("hid")
        self.sized(n, h, lambda first, count: self.own(n, first, count).wait())
        self.sized(n, h, lambda first, count: self.rest(n, count).wait_recv())
        self.each_swap(n, lambda copy: copy.start())

    def settle(self, ns):
        for n in ns:
            self.each_swap(n, lambda copy: copy.wait())

    def finish(self):
        h = lax.axis_index("hid")
        for n in range(len(self.items)):
            self.sized(n, h, lambda first, count: self.rest(n, count).wait_send())

    def rest(self, n, count):
        src, dst, at, split = self.items[n]
        others = self.tiles - count if split else H - 1
        return to_chip(
            src.at[:, lanes(0, others)],
            dst.at[pl.ds(0, (H - 1) * self.depth), lanes(at, count)],
            self.ss.at[n],
            self.rs.at[n],
            lax.axis_index("hid"),
        )


class Return(Bulk):
    def __init__(self, items, parts, tiles, depth, sems):
        super().__init__(items, tiles, depth, sems)
        self.parts = parts

    def swap(self, p):
        part, total, _ = self.parts[p]
        return to_core(
            part.at[self.ours(1 - lax.axis_index("seq"))], total, self.xs.at[p, 0], self.xr.at[p, 0]
        )

    def add(self, p):
        def run():
            part, total, _ = self.parts[p]
            b = lax.axis_index("seq")
            self.swap(p).wait()
            half, step = total.shape[0], 128

            @pl.loop(0, half // step)
            def _(t):
                at = pl.ds(pl.multiple_of(t * step, step), step)
                own = pl.ds(pl.multiple_of(b * half + t * step, step), step)
                total[at] = (total[at].astype(F32) + part[own].astype(F32)).astype(BF)

            for n in self.parts[p][2]:
                h = lax.axis_index("hid")
                self.sized(n, h, lambda first, count: self.own(n, first, count).start())

        return run

    def copy(self, n, k, chip, first, count):
        dst, src, at, _ = self.items[n]
        return to_chip(
            src.at[self.row(0, chip), lanes(at, count)],
            dst.at[:, lanes(first, count)],
            self.ss.at[n],
            self.rs.at[n],
            chip,
        )

    def own(self, n, first, count):
        dst, src, at, _ = self.items[n]
        return pltpu.make_async_copy(
            src.at[self.row(0, lax.axis_index("hid")), lanes(at, count)],
            dst.at[:, lanes(first, count)],
            self.ls.at[n],
        )

    def job(self, n, k):
        def run():
            h = lax.axis_index("hid")
            chip = lax.rem(h + k, H)
            self.sized(n, h, lambda first, count: self.copy(n, k, chip, first, count).start())

        return run

    def jobs(self, p):
        return [self.add(p)] + [self.job(n, k) for n in self.parts[p][2] for k in range(1, H)]

    def finish(self):
        h = lax.axis_index("hid")
        for n in range(len(self.items)):
            self.sized(n, h, lambda first, count: self.own(n, first, count).wait())
            self.sized(n, h, lambda first, count: self.rest(n, count).wait())

    def rest(self, n, count):
        dst, src, at, split = self.items[n]
        others = self.tiles - count if split else H - 1
        return to_chip(
            src.at[pl.ds(0, (H - 1) * self.depth), lanes(at, count)],
            dst.at[:, lanes(0, others)],
            self.ss.at[n],
            self.rs.at[n],
            lax.axis_index("hid"),
        )


def bulk_sems(n):
    return [DMA((n,)), DMA((n,)), DMA((n,)), DMA((n, 2)), DMA((n, 2))]


def split_refs(refs, *counts):
    groups, at = [], 0
    for count in counts:
        groups.append(refs[at : at + count])
        at += count
    assert at == len(refs)
    return groups


def row_norm(rows):
    return lax.rsqrt(jnp.mean(rows * rows, axis=-1, keepdims=True) + EPS)


def gather_jobs(gather, ahead):
    lag = PARTS

    def step(t):
        def run():
            if t == 0:
                for c in range(ahead):
                    gather.start(c)
            if t < CUTS:
                gather.second(t)
                if t + ahead < CUTS:
                    gather.start(t + ahead)
            if t >= lag:
                gather.third(t - lag)

        return run

    return [step(t) for t in range(CUTS + lag)]


def scatter_jobs(scatter, ahead, rows_done, meanwhile=()):
    lag, held = PARTS, []

    def step(t):
        def run():
            if t == 0:
                for c in range(ahead):
                    scatter.start(c)
                for job in meanwhile:
                    job()
            if t < CUTS:
                scatter.second(t)
                if t + ahead < CUTS:
                    scatter.start(t + ahead)
            if 0 <= t - lag // 2 < CUTS:
                scatter.third(t - lag // 2)
            c = t - lag - lag // 2
            if c >= 0:
                held.append(scatter.last(c))
                if len(held) == PARTS:
                    rows_done(c // PARTS, jnp.concatenate(held, axis=1))
                    held.clear()

        return run

    return [step(t) for t in range(CUTS + lag + lag // 2)]


def turn_jobs(scatter, gather, ahead, rows_done, meanwhile=()):
    lag = PARTS

    def write(i, rows):
        rows_done(i, rows)
        if i == PIECES - 1:
            scatter.finish()
        for c in range(i * PARTS, (i + 1) * PARTS):
            gather.start(c)

    first = scatter_jobs(scatter, ahead, write, meanwhile)

    def step(t):
        def run():
            if t < len(first):
                first[t]()
            c = t - 2 * lag - lag // 2 - (PARTS - 1)
            if 0 <= c < CUTS:
                gather.second(c)
            if 0 <= c - lag < CUTS:
                gather.third(c - lag)

        return run

    return [step(t) for t in range(CUTS + 3 * lag + lag // 2 + PARTS - 1)]


def norm_back(rows, grad, gain):
    factor = row_norm(rows)
    normal = rows * factor
    scaled = grad * gain
    back = factor * (scaled - normal * jnp.mean(scaled * normal, axis=-1, keepdims=True))
    return back, jnp.sum(grad * normal, axis=0, keepdims=True)


def row_blocks(ref):
    size = 2 * ref.shape[1] * ref.shape[2] * ref.shape[3]
    return [(pl.ds(2 * n, 2), pl.ds(n * size, size)) for n in range(ref.shape[0] // 2)]


def merged(rows):
    return rows.reshape(-1, rows.shape[-1])


def doc_tile(lengths_ref, start, shape, dim):
    positions = start + lax.broadcasted_iota(jnp.int32, shape, dim)
    documents = jnp.full(shape, -1, jnp.int32)
    begin = jnp.int32(0)
    for n in range(lengths_ref.shape[0]):
        documents = documents + jnp.where(positions >= begin, 1, 0)
        begin = begin + lengths_ref[n]
    return documents


def layer_kernel(tiles, *refs):
    (
        (x_ref, c_ref, lengths, first_gain, second_gain, gain_ref, gap_all),
        weights,
        (out, in_grad, totals, *homes),
        (first, cot, second, mix, part, glu_part),
        (wqfi, wo, wg, wu, wd),
        (entry, middle, mid, dcol, drow, gap_ref),
        (lin, mixed, states, head, cum, d_head, d_lin, d_mixed, backs),
        (hidden, gate_low, up_low),
        (gqfi, go, gg, gu, gd),
        (tqfi, to, tg, tu, td),
        main_bufs,
        glu_bufs,
        gather_sets,
        scatter_sets,
        (f_out, f_in, b_out, b_in, fs, fr, bs, br, ls),
        (mine, theirs, chips, vs, vr, ws, wr),
        bulk_sets,
    ) = split_refs(refs, 7, 7, 10, 6, 5, 6, 9, 3, 5, 5, 5, 5, 24, 24, 9, 7, 20)
    q, f, i, o, g, u, d = weights
    hq, hf, hi, ho, hg, hu, hd = homes
    h, z, y, x = place()
    core = lax.axis_index("seq")
    depth, size = q.shape[0], x_ref.shape[1] // PIECES
    extent = lin.shape[0]
    mixer_in = Fetch(
        [(q, wqfi, 0, False), (f, wqfi, 1, False), (i, wqfi, 2, False), (o, wo, 0, False)],
        H,
        depth,
        bulk_sets[0:5],
    )
    units_in = Fetch(
        [(g, wg, 0, True), (u, wu, 0, True), (d, wd, 0, True)], tiles, depth, bulk_sets[5:10]
    )
    units_out = Return(
        [(hd, td, 0, True), (hg, tg, 0, True), (hu, tu, 0, True)],
        [(gd, td, (0,)), (gg, tg, (1,)), (gu, tu, (2,))],
        tiles,
        depth,
        bulk_sets[10:15],
    )
    mixer_out = Return(
        [(ho, to, 0, False), (hq, tqfi, 0, False), (hf, tqfi, 1, False), (hi, tqfi, 2, False)],
        [(go, to, (0,)), (gqfi, tqfi, (1, 2, 3))],
        H,
        depth,
        bulk_sets[15:20],
    )
    gathers = [
        Gather(ref, gather_sets[6 * n : 6 * n + 6])
        for n, ref in enumerate((first, cot, second, mix))
    ]
    scatters = [
        Scatter(ref, bufs, scatter_sets[6 * n : 6 * n + 6])
        for n, (ref, bufs) in enumerate(
            ((part, main_bufs), (part, main_bufs), (part, main_bufs), (glu_part, glu_bufs))
        )
    ]

    own = pltpu.make_async_copy(c_ref.at[0], cot.at[z, y, x], ls)
    own.start()
    mixer_in.start_own()
    for n in range(PIECES):
        at = pl.ds(n * size, size)
        rows = x_ref[0, at].astype(F32)
        entry[at] = rows
        first[z, y, x, at] = (rows * row_norm(rows) * first_gain[...]).astype(BF)
    greet(all_chips(), core=True)
    own.wait()

    def documents():
        gap_ref[...] = gap_all[pl.ds(h, 1)]
        base = core * extent
        for c, at in spans(extent):
            dcol[at] = doc_tile(lengths, base + c * SPAN, (SPAN, SPAN), 0)
            drow[8 * c : 8 * c + 8] = doc_tile(lengths, base + c * SPAN, (8, SPAN), 1)
        drow[8 * len(spans(extent)) :] = doc_tile(lengths, base - 1, (8, SPAN), 0)
        mine[...] = jnp.zeros_like(mine)
        units_in.start_own()

    mixer_jobs = mixer_in.jobs()
    plan = Plan(([documents], 0, 1), (mixer_jobs[: 3 * (H - 1)], *TIMES[0]))
    plan.during(gather_jobs(gathers[0], AHEAD[0]))
    plan.rest()
    for job in mixer_jobs[3 * (H - 1) :]:
        job()
    for n in range(3):
        mixer_in.arrive(n)
    gathers[0].finish()
    mixer_in.settle((0, 1, 2))
    plan = Plan((gather_jobs(gathers[1], AHEAD[1]), *TIMES[1]), (units_in.jobs(), *TIMES[2]))

    for n, at in row_blocks(first):
        lin[at] = jnp.dot(merged(first[n]), wqfi[...], preferred_element_type=F32)
        plan.step(-1)
    blocks = (lin, gap_ref, gain_ref, dcol, drow)
    mix_forward(blocks, mixed, states, head, cum, (f_out, f_in, fs, fr), lambda: plan.step(-1))
    mixer_in.arrive(3)
    mixer_in.settle((3,))
    for n, at in row_blocks(part):
        part[n] = times_t(head[at], wo[...]).astype(BF).reshape((2,) + part.shape[1:])
        plan.step(-1)

    def middle_rows(n, total):
        at = pl.ds(n * size, size)
        rows = entry[at] + total
        middle[at] = rows
        second[z, y, x, at] = (rows * row_norm(rows) * second_gain[...]).astype(BF)

    plan.during(turn_jobs(scatters[0], gathers[2], AHEAD[2], middle_rows))
    plan.rest()
    for n in range(3):
        units_in.arrive(n)
    gathers[1].finish()
    gathers[2].finish()
    mixer_in.finish()
    units_in.settle((0, 1, 2))
    units_in.finish()

    for n, at in row_blocks(second):
        rows = merged(second[n])
        gate_lin = jnp.dot(rows, wg[...], preferred_element_type=F32)
        up_lin = jnp.dot(rows, wu[...], preferred_element_type=F32)
        d_hidden = jnp.dot(merged(cot[n]), wd[...], preferred_element_type=F32)
        s = jax.nn.sigmoid(gate_lin)
        silu = gate_lin * s
        hidden[at] = (silu * up_lin).astype(BF)
        gate_low[at] = (d_hidden * up_lin * s * (1.0 + gate_lin * (1.0 - s))).astype(BF)
        up_low[at] = (d_hidden * silu).astype(BF)
        total = times_t(gate_low[at], wg[...]) + times_t(up_low[at], wu[...])
        part[n] = total.astype(BF).reshape((2,) + part.shape[1:])

    def grad_rows(n, total):
        at = pl.ds(n * size, size)
        back, gains = norm_back(middle[at], total, second_gain[...])
        mine[16:32] = mine[16:32] + gains.reshape(16, 128)
        rows = c_ref[0, at].astype(F32) + back
        mid[at] = rows
        mix[z, y, x, at] = rows.astype(BF)

    def out_rows(n, total):
        at = pl.ds(n * size, size)
        out[0, at] = (middle[at] + total).astype(BF)

    def outer(dst, rows, cols, giver, p):
        width = 512

        def piece(start):
            def run():
                at = pl.ds(start, width)
                dst[at] = outer_sum(merged(rows[:, :, :, :, at]), cols[...]).astype(BF)

            return run

        return [piece(start) for start in range(0, rows.shape[4], width)] + [
            lambda: giver.swap(p).start()
        ]

    def glu_block(n, at):
        def run():
            rows = times_t(hidden[at], wd[...]).astype(BF)
            glu_part[n] = rows.reshape((2,) + glu_part.shape[1:])

        return run

    returns = outer(gg, second, gate_low, units_out, 1) + units_out.jobs(0)
    returns += outer(gu, second, up_low, units_out, 2) + units_out.jobs(1) + units_out.jobs(2)
    outward = [glu_block(n, at) for n, at in row_blocks(glu_part)]
    outward += scatter_jobs(scatters[3], AHEAD[4], out_rows)
    plan = Plan((returns, *TIMES[3]), (outward, *TIMES[4]))
    plan.during(
        turn_jobs(
            scatters[1], gathers[3], AHEAD[3], grad_rows, outer(gd, cot, hidden, units_out, 0)
        )
    )
    gathers[3].finish()

    kept = plan.left(0), plan.left(1)
    plan = Plan((outer(go, mix, head, mixer_out, 0), 0, 2), (kept[0], 0, PACE[0]), (kept[1], 0, 1))
    for n, at in row_blocks(mix):
        d_head[at] = jnp.dot(merged(mix[n]), wo[...], preferred_element_type=F32)
        plan.step(0)
    group, gap = mix_backward(
        blocks, mixed, states, cum, d_head, d_lin, d_mixed, backs, (b_out, b_in, bs, br),
        lambda: plan.step(0),
    )
    mine[32:33] = group
    mine[40:41] = gap
    for n, at in row_blocks(part):
        part[n] = times_t(d_lin[at], wqfi[...]).astype(BF).reshape((2,) + part.shape[1:])

    def in_rows(n, total):
        at = pl.ds(n * size, size)
        back, gains = norm_back(entry[at], total, first_gain[...])
        in_grad[0, at] = mid[at] + back
        mine[0:16] = mine[0:16] + gains.reshape(16, 128)
        if n == PIECES - 1:
            swap = to_core(mine, theirs, vs, vr)
            swap.start()
            swap.wait()
            chips[h] = mine[...] + theirs[...]
            for k in range(1, H):
                to_chip(chips.at[h], chips.at[h], ws, wr, lax.rem(h + k, H)).start()

    for job in plan.left(0):
        job()
    kept = plan.left(1), plan.left(2)
    plan = Plan(
        (kept[0], 0, PACE[1]), (mixer_out.jobs(0) + mixer_out.jobs(1), *TIMES[5]), (kept[1], 0, 1)
    )
    plan.during(
        scatter_jobs(
            scatters[2], AHEAD[5], in_rows, outer(gqfi, first, d_lin, mixer_out, 1)
        )
    )
    plan.rest()
    others = chips.at[0 : H - 1]
    to_chip(others, others, ws, wr, h).wait()
    acc = chips[0, 0:40]
    for chip in range(1, H):
        acc = acc + chips[chip, 0:40]
    totals[0:40] = acc
    for chip in range(H):
        totals[40 + chip : 41 + chip] = chips[chip, 40:41]
    scatters[2].finish()
    scatters[3].finish()
    units_out.finish()
    mixer_out.finish()


def layer(inputs, cotangent, lengths, first_gain, second_gain, group_gain, gap_log, weights):
    _, rows, cols = inputs.shape
    depth, units = weights[-1].shape
    extent, count = H * rows, 2 * H * depth
    tiles = units // 128
    wide = -(-tiles // H) * 128
    home = lambda width: jax.ShapeDtypeStruct((depth, width), BF)
    full = VMEM((4, 2, 2, rows, cols), BF)
    local = VMEM((rows, cols), F32)
    tile = VMEM((extent, SPAN), F32)
    square = VMEM((SPAN, SPAN), F32)
    squares = VMEM((extent // SPAN, SPAN, SPAN), F32)
    widths = (384, 128, wide, wide, wide)
    return pl.pallas_call(
        functools.partial(layer_kernel, tiles),
        out_shape=[
            jax.ShapeDtypeStruct((1, rows, cols), BF),
            jax.ShapeDtypeStruct((1, rows, cols), F32),
            jax.ShapeDtypeStruct((56, 128), F32),
        ]
        + [home(cols)] * 4
        + [home(units)] * 3,
        in_specs=[VSPEC] * 2 + [SSPEC] + [VSPEC] * 4 + [ASPEC] * 7,
        out_specs=[VSPEC] * 3 + [ASPEC] * 7,
        scratch_shapes=[full] * 6
        + [VMEM((count, width), BF) for width in widths]
        + [local, local, local, VMEM((extent, SPAN), jnp.int32)]
        + [VMEM((8 * (extent // SPAN) + 8, SPAN), jnp.int32), VMEM((1, SPAN), F32)]
        + [VMEM((extent, 384), F32), tile, squares, VMEM((extent, SPAN), BF), tile]
        + [tile, VMEM((extent, 384), BF), tile, squares]
        + [VMEM((extent, wide), BF)] * 3
        + [VMEM((count, width), BF) for width in widths]
        + [VMEM((count // 2, width), BF) for width in widths]
        + scatter_bufs(rows, cols)
        + scatter_bufs(rows, cols)
        + gather_sems() * 4
        + scatter_sems() * 4
        + [square] * 4
        + [DMA] * 5
        + [VMEM((48, 128), F32), VMEM((48, 128), F32), VMEM((H, 48, 128), F32)]
        + [DMA, DMA, DMA, DMA]
        + bulk_sems(4)
        + bulk_sems(3)
        + bulk_sems(3)
        + bulk_sems(4),
        compiler_params=comm_params(1),
    )(
        inputs,
        cotangent,
        lengths,
        first_gain[None],
        second_gain[None],
        group_gain[None],
        gap_log.reshape(H, SPAN),
        *weights,
    )


def mm(left, right, at_left, at_right):
    return lax.dot_general(
        left.astype(BF),
        right.astype(BF),
        (((at_left,), (at_right,)), ((), ())),
        preferred_element_type=F32,
    )


def tri_sum(rows, reverse=False):
    r = lax.broadcasted_iota(jnp.int32, (SPAN, SPAN), 0)
    c = lax.broadcasted_iota(jnp.int32, (SPAN, SPAN), 1)
    picked = jnp.where((r <= c) if reverse else (r >= c), 1.0, 0.0).astype(BF)
    high = rows.astype(BF)
    rest = rows - high.astype(F32)
    middle = rest.astype(BF)
    low = rest - middle.astype(F32)
    return mm(picked, high, 1, 0) + mm(picked, middle, 1, 0) + mm(picked, low, 1, 0)


def span_gates(lin_ref, gap_ref, at):
    q_lin, f_lin, values = lin_ref[at, 0:128], lin_ref[at, 128:256], lin_ref[at, 256:384]
    s = jax.nn.sigmoid(q_lin)
    key = jnp.exp(gap_ref[...]) * jax.nn.sigmoid(-f_lin)
    return q_lin, f_lin, values, s, key


def span_masks(dcol_ref, drow_ref, c, at):
    r = lax.broadcasted_iota(jnp.int32, (SPAN, SPAN), 0)
    k = lax.broadcasted_iota(jnp.int32, (SPAN, SPAN), 1)
    dcol, drow = dcol_ref[at], drow_ref[8 * c : 8 * c + 1]
    last = (c + 1) * SPAN - 1
    end = dcol_ref[last : last + 1]
    if c:
        before = dcol_ref[c * SPAN - 1 : c * SPAN]
    else:
        count = drow_ref.shape[0]
        before = drow_ref[count - 8 : count - 7]
    same = jnp.where(jnp.logical_and(dcol == drow, r >= k), 1.0, 0.0)
    carried = jnp.where(dcol == before, 1.0, 0.0)
    keep = jnp.where(dcol == end, 1.0, 0.0)
    whole = jnp.where(end == before, 1.0, 0.0)
    return same, carried, keep, whole


def spans(extent):
    return [(c, pl.ds(c * SPAN, SPAN)) for c in range(extent // SPAN)]


def mix_forward(blocks, mixed_ref, states_ref, head_ref, cum_ref, handover, between):
    out_ref, in_ref, send, recv = handover
    lin_ref, gap_ref, gain_ref, dcol_ref, drow_ref = blocks
    steps = spans(lin_ref.shape[0])
    state = jnp.zeros((SPAN, SPAN), F32)
    for c, at in steps:
        q_lin, f_lin, values, s, key = span_gates(lin_ref, gap_ref, at)
        same, carried, keep, whole = span_masks(dcol_ref, drow_ref, c, at)
        cum = tri_sum(jnp.log1p(-key))
        cum_ref[at] = cum
        end = cum[SPAN - 1 : SPAN]
        fresh = mm(values, jnp.exp(end - cum) * key * keep, 0, 0)
        states_ref[c] = fresh
        state = state * (jnp.exp(end) * whole) + fresh
    out_ref[...] = state
    copy = to_core(out_ref, in_ref, send, recv)
    copy.start()
    between()
    copy.wait()
    state = in_ref[...] * lax.axis_index("seq").astype(F32)
    for c, at in steps:
        q_lin, f_lin, values, s, key = span_gates(lin_ref, gap_ref, at)
        same, carried, keep, whole = span_masks(dcol_ref, drow_ref, c, at)
        cum = cum_ref[at]
        end = cum[SPAN - 1 : SPAN]
        fresh = states_ref[c]
        states_ref[c] = state
        decayed = q_lin * s * jnp.exp(cum)
        scores = mm(decayed, key * jnp.exp(-cum), 1, 1) * same
        mixed = mm(scores, values, 1, 0) + carried * mm(decayed, state, 1, 1)
        mixed_ref[at] = mixed
        head_ref[at] = (mixed * row_norm(mixed) * gain_ref[...]).astype(BF)
        state = state * (jnp.exp(end) * whole) + fresh
        if c % 2:
            between()


def mix_backward(
    blocks, mixed_ref, states_ref, cum_ref, dhead_ref, dlin_ref, do_ref, back_ref, handover, between
):
    out_ref, in_ref, send, recv = handover
    lin_ref, gap_ref, gain_ref, dcol_ref, drow_ref = blocks
    steps = spans(lin_ref.shape[0])
    group = jnp.zeros((1, SPAN), F32)
    adjoint = jnp.zeros((SPAN, SPAN), F32)
    for c, at in reversed(steps):
        d_mixed, gains = norm_back(mixed_ref[at], dhead_ref[at], gain_ref[...])
        group = group + gains
        do_ref[at] = d_mixed
        q_lin, f_lin, values, s, key = span_gates(lin_ref, gap_ref, at)
        same, carried, keep, whole = span_masks(dcol_ref, drow_ref, c, at)
        cum = cum_ref[at]
        back = mm(d_mixed, carried * (q_lin * s * jnp.exp(cum)), 0, 0)
        back_ref[c] = back
        adjoint = adjoint * (jnp.exp(cum[SPAN - 1 : SPAN]) * whole) + back
    out_ref[...] = adjoint
    copy = to_core(out_ref, in_ref, send, recv)
    copy.start()
    between()
    copy.wait()
    adjoint = in_ref[...] * (1 - lax.axis_index("seq")).astype(F32)
    gap = jnp.zeros((1, SPAN), F32)
    for c, at in reversed(steps):
        q_lin, f_lin, values, s, key = span_gates(lin_ref, gap_ref, at)
        same, carried, keep, whole = span_masks(dcol_ref, drow_ref, c, at)
        cum, d_mixed, state = cum_ref[at], do_ref[at], states_ref[c]
        grow, shrink = jnp.exp(-cum), jnp.exp(cum)
        end = cum[SPAN - 1 : SPAN]
        decayed, grown = q_lin * s * shrink, key * grow
        rest = jnp.exp(end - cum) * keep
        tail, through = rest * key, jnp.exp(end) * whole
        scores = mm(decayed, grown, 1, 1) * same
        d_scores = mm(d_mixed, values, 1, 1) * same
        d_values = mm(scores, d_mixed, 0, 0) + mm(tail, adjoint, 1, 1)
        d_decayed = mm(d_scores, grown, 1, 0) + carried * mm(d_mixed, state, 1, 0)
        d_grown = mm(d_scores, decayed, 0, 0)
        d_tail = mm(values, adjoint, 1, 0)
        held = tail * d_tail
        d_cum = decayed * d_decayed - grown * d_grown - held
        d_end = jnp.sum(held, axis=0, keepdims=True) + through * jnp.sum(
            state * adjoint, axis=0, keepdims=True
        )
        d_log = tri_sum(d_cum, reverse=True) + d_end
        d_key = d_grown * grow + d_tail * rest - d_log / (1.0 - key)
        scaled = d_key * key
        gap = gap + jnp.sum(scaled, axis=0, keepdims=True)
        dlin_ref[at, 0:128] = (d_decayed * shrink * s * (1.0 + q_lin * (1.0 - s))).astype(BF)
        dlin_ref[at, 128:256] = (-scaled * jax.nn.sigmoid(f_lin)).astype(BF)
        dlin_ref[at, 256:384] = d_values.astype(BF)
        adjoint = adjoint * through + back_ref[c]
        if c % 2:
            between()
    return group, gap


def fast_body(
    inputs,
    cotangent,
    lengths,
    first_gain,
    q_weight,
    f_weight,
    i_weight,
    o_weight,
    group_gain,
    gap_log,
    second_gain,
    gate_weight,
    up_weight,
    down_weight,
):
    model = inputs.shape[2]
    output, input_grad, totals, *grads = layer(
        inputs,
        cotangent,
        lengths,
        first_gain,
        second_gain,
        group_gain,
        gap_log,
        (q_weight, f_weight, i_weight, o_weight, gate_weight, up_weight, down_weight),
    )
    q_grad, f_grad, i_grad, o_grad, gate_grad, up_grad, down_grad = (
        grad.astype(F32) for grad in grads
    )
    return (
        output,
        input_grad,
        totals[0:16].reshape(model),
        q_grad,
        f_grad,
        i_grad,
        o_grad,
        totals[32],
        totals[40:56].reshape(model),
        totals[16:32].reshape(model),
        gate_grad,
        up_grad,
        down_grad,
    )


def solution(mesh):
    placed = (
        P("seq", "hid", None),
        P("seq", "hid", None),
        P(),
        P(),
        P(("seq", "hid"), None),
        P(("seq", "hid"), None),
        P(("seq", "hid"), None),
        P(("seq", "hid"), None),
        P(),
        P(),
        P(),
        P(("seq", "hid"), None),
        P(("seq", "hid"), None),
        P(("seq", "hid"), None),
    )
    body = fast_body if mesh.shape["hid"] == H else wide_body
    return jax.shard_map(
        body,
        mesh=mesh,
        in_specs=placed,
        out_specs=(
            P("seq", "hid", None),
            P("seq", "hid", None),
            P(),
            P(("seq", "hid"), None),
            P(("seq", "hid"), None),
            P(("seq", "hid"), None),
            P(("seq", "hid"), None),
            P(),
            P(),
            P(),
            P(("seq", "hid"), None),
            P(("seq", "hid"), None),
            P(("seq", "hid"), None),
        ),
        check_vma=False,
    )
```

```python
import functools

import jax
import jax.numpy as jnp
from jax import lax
from jax.experimental import pallas as pl
from jax.experimental.pallas import tpu as pltpu
from jax.sharding import PartitionSpec as P

H = 16
SPAN = 128


EPS = 1e-06
HIGH_PRECISION = lax.Precision.HIGHEST


def from_behind(block, axis, distance):
    devices = range(lax.axis_size(axis))
    route = [(i - distance, i) for i in devices if i - distance in devices]
    return lax.ppermute(block, axis, route)


def normed(entries, gain_vec):
    factor = lax.rsqrt(jnp.mean(entries * entries, axis=-1, keepdims=True) + EPS)
    return entries * factor * gain_vec


def gates(q_part, f_part, gap_piece):
    key_gate = jnp.exp(gap_piece) * jax.nn.sigmoid(-f_part)
    return (jax.nn.silu(q_part), key_gate, jnp.log1p(-key_gate))


def doc_starts(lengths):
    count = lengths.shape[0]
    earlier = lax.broadcasted_iota(jnp.int32, (count, count), 0) > lax.broadcasted_iota(
        jnp.int32, (count, count), 1
    )
    return jnp.sum(jnp.where(earlier, lengths[None, :], 0), axis=1)


def running_sum(rows):
    extent = rows.shape[-2]
    lower = (
        lax.broadcasted_iota(jnp.int32, (extent, extent), 0)
        >= lax.broadcasted_iota(jnp.int32, (extent, extent), 1)
    ).astype(jnp.float32)
    return jnp.einsum("ts,...sk->...tk", lower, rows, precision=HIGH_PRECISION)


def doc_ids(lengths, positions):
    starts = doc_starts(lengths)
    covered = (starts[None, :] <= positions[:, None]).astype(jnp.int32)
    return jnp.sum(covered, axis=1) - 1


def span_step(memory_state, pieces):
    queries, key_gate, value_rows, log_decay, documents, before = pieces
    cumulative = running_sum(log_decay)
    query_decayed = queries * jnp.exp(cumulative)
    k_grown = key_gate * jnp.exp(-cumulative)
    extent = documents.shape[0]
    row_ids = lax.broadcasted_iota(jnp.int32, (extent, extent), 0)
    col_ids = lax.broadcasted_iota(jnp.int32, (extent, extent), 1)
    same_doc = jnp.logical_and(documents[:, None] == documents[None, :], row_ids >= col_ids).astype(
        jnp.float32
    )
    scores = (
        jnp.einsum("hck,hsk->hcs", query_decayed, k_grown, precision=HIGH_PRECISION)
        * same_doc[None]
    )
    within_block = jnp.einsum("hcs,hsv->hcv", scores, value_rows, precision=HIGH_PRECISION)
    carried_state = (documents == before).astype(jnp.float32)[None, :, None]
    output_rows = within_block + carried_state * jnp.einsum(
        "awn,ani->awi", query_decayed, memory_state, precision=HIGH_PRECISION
    )
    last_cum = cumulative[:, -1:, :]
    keep_mask = (documents == documents[-1]).astype(jnp.float32)[None, :, None]
    tail_key_rows = jnp.exp(last_cum - cumulative) * key_gate * keep_mask
    whole_block = (documents[-1] == before).astype(jnp.float32)
    fresh_state = jnp.einsum("wfx,wfg->wxg", tail_key_rows, value_rows, precision=HIGH_PRECISION)
    memory_state = jnp.exp(last_cum[:, 0, :])[:, :, None] * whole_block * memory_state + fresh_state
    return (memory_state, output_rows)


def recur(queries, key_gate, value_rows, log_decay, documents, before, memory_state):
    head_count, extent, columns = queries.shape
    span_count = extent // SPAN

    def by_span(tensor):
        return jnp.swapaxes(tensor.reshape(head_count, span_count, SPAN, tensor.shape[-1]), 0, 1)

    doc_rows = documents.reshape(span_count, SPAN)
    befores = jnp.concatenate([jnp.reshape(before, (1,)), doc_rows[:-1, -1]])
    memory_state, span_out = lax.scan(
        jax.checkpoint(span_step),
        memory_state,
        (
            by_span(queries),
            by_span(key_gate),
            by_span(value_rows),
            by_span(log_decay),
            doc_rows,
            befores,
        ),
    )
    return (
        jnp.swapaxes(span_out, 0, 1).reshape(head_count, extent, value_rows.shape[-1]),
        memory_state,
    )


def spread_cols(weight, copies):
    row_count = weight.shape[0]
    shaped = weight.reshape(row_count, 1, H, weight.shape[1] // H)
    return jnp.broadcast_to(shaped, (row_count, copies, H, shaped.shape[3])).reshape(
        row_count, copies * weight.shape[1]
    )


def fold_copies(received, copies):
    row_count = received.shape[0]
    return jnp.sum(received.reshape(row_count, copies, received.shape[1] // copies), axis=1)


def fan_rows(local_rows):
    blocks_here, row_count, columns = local_rows.shape
    return jnp.broadcast_to(local_rows[:, None], (blocks_here, H, row_count, columns)).reshape(
        blocks_here * H * row_count, columns
    )


def sum_heads(received, blocks_here):
    total_rows, columns = received.shape
    return jnp.sum(
        received.reshape(blocks_here, H, total_rows // (blocks_here * H), columns), axis=1
    )


def times_t(left_mat, right_mat):
    return lax.dot_general(
        left_mat, right_mat, (((1,), (1,)), ((), ())), preferred_element_type=jnp.float32
    )


def outer_sum(left_mat, right_mat):
    return lax.dot_general(
        left_mat, right_mat, (((0,), (0,)), ((), ())), preferred_element_type=jnp.float32
    )


def outer_high(left_mat, right_mat):
    return lax.dot_general(
        left_mat,
        right_mat,
        (((0,), (0,)), ((), ())),
        precision=HIGH_PRECISION,
        preferred_element_type=jnp.float32,
    )


def wide_body(
    inputs,
    cotangent,
    lengths,
    first_gain,
    q_weight,
    f_weight,
    i_weight,
    o_weight,
    group_gain,
    gap_log,
    second_gain,
    gate_weight,
    up_weight,
    down_weight,
):
    hid_size = lax.axis_size("hid")
    per_seq = hid_size // H
    block_total = lax.axis_size("seq") * per_seq
    hid_place = lax.axis_index("hid")
    head_id = hid_place % H
    block_id = lax.axis_index("seq") * per_seq + hid_place // H
    model = inputs.shape[2]
    head_width = model // H
    block_len = hid_size * inputs.shape[1]
    entries = inputs.astype(jnp.float32)
    q_block, f_block, i_block, o_block, gate_block, up_block, down_block = (
        lax.all_to_all(
            spread_cols(q_weight, block_total),
            ("seq", "hid"),
            split_axis=1,
            concat_axis=0,
            tiled=True,
        ),
        lax.all_to_all(
            spread_cols(f_weight, block_total),
            ("seq", "hid"),
            split_axis=1,
            concat_axis=0,
            tiled=True,
        ),
        lax.all_to_all(
            spread_cols(i_weight, block_total),
            ("seq", "hid"),
            split_axis=1,
            concat_axis=0,
            tiled=True,
        ),
        lax.all_to_all(
            spread_cols(o_weight, block_total),
            ("seq", "hid"),
            split_axis=1,
            concat_axis=0,
            tiled=True,
        ),
        lax.all_to_all(
            spread_cols(gate_weight, block_total),
            ("seq", "hid"),
            split_axis=1,
            concat_axis=0,
            tiled=True,
        ),
        lax.all_to_all(
            spread_cols(up_weight, block_total),
            ("seq", "hid"),
            split_axis=1,
            concat_axis=0,
            tiled=True,
        ),
        lax.all_to_all(
            spread_cols(down_weight, block_total),
            ("seq", "hid"),
            split_axis=1,
            concat_axis=0,
            tiled=True,
        ),
    )
    positions = block_id * block_len + lax.iota(jnp.int32, block_len)
    documents = doc_ids(lengths, positions)
    before = doc_ids(lengths, jnp.reshape(block_id * block_len - 1, (1,)))[0]
    first_norm, first_back = jax.vjp(normed, entries, first_gain)
    first_low = first_norm.astype(jnp.bfloat16)
    first_rows = lax.all_to_all(fan_rows(first_low), "hid", split_axis=0, concat_axis=0, tiled=True)
    q_lin = jnp.dot(first_rows, q_block, preferred_element_type=jnp.float32)
    f_lin = jnp.dot(first_rows, f_block, preferred_element_type=jnp.float32)
    i_lin = jnp.dot(first_rows, i_block, preferred_element_type=jnp.float32)
    gap_part = lax.dynamic_slice_in_dim(gap_log, head_id * head_width, head_width)
    queries, key_gate, log_decay = gates(q_lin, f_lin, gap_part)
    cumulative = running_sum(log_decay)
    last_cum = cumulative[-1]
    tail_key_rows = (
        jnp.exp(last_cum[None, :] - cumulative)
        * key_gate
        * (documents == documents[-1]).astype(jnp.float32)[:, None]
    )
    local_state = outer_high(tail_key_rows, i_lin)
    decay = jnp.exp(last_cum) * (documents[-1] == before).astype(jnp.float32)
    state_in = jnp.zeros_like(local_state)
    for number in range(block_total - 1):
        state_out = decay[:, None] * state_in + local_state
        state_in = from_behind(state_out.astype(jnp.bfloat16), ("seq", "hid"), H).astype(
            state_out.dtype
        )

    def core(q_part, f_part, i_part, gap_piece):
        queries_in, keys_in, logs_in = gates(q_part, f_part, gap_piece)
        mixed_all, memory_state = recur(
            queries_in[None],
            keys_in[None],
            i_part[None],
            logs_in[None],
            documents,
            before,
            state_in[None],
        )
        return (mixed_all[0], memory_state[0])

    (mixed_out, _), core_back = jax.vjp(core, q_lin, f_lin, i_lin, gap_part)
    head_normed, norm_back = jax.vjp(normed, mixed_out, group_gain)
    head_low = head_normed.astype(jnp.bfloat16)
    mix_out = sum_heads(
        lax.all_to_all(
            times_t(head_low, o_block).astype(jnp.bfloat16),
            "hid",
            split_axis=0,
            concat_axis=0,
            tiled=True,
        ).astype(jnp.float32),
        per_seq,
    )
    middle = entries + mix_out
    second_norm, second_back = jax.vjp(normed, middle, second_gain)
    second_low = second_norm.astype(jnp.bfloat16)
    second_rows, cot_rows = (
        lax.all_to_all(fan_rows(second_low), "hid", split_axis=0, concat_axis=0, tiled=True),
        lax.all_to_all(fan_rows(cotangent), "hid", split_axis=0, concat_axis=0, tiled=True),
    )
    gate_lin = jnp.dot(second_rows, gate_block, preferred_element_type=jnp.float32)
    up_lin = jnp.dot(second_rows, up_block, preferred_element_type=jnp.float32)
    hidden = (jax.nn.silu(gate_lin) * up_lin).astype(jnp.bfloat16)
    glu_out = sum_heads(
        lax.all_to_all(
            times_t(hidden, down_block).astype(jnp.bfloat16),
            "hid",
            split_axis=0,
            concat_axis=0,
            tiled=True,
        ).astype(jnp.float32),
        per_seq,
    )
    output = (middle + glu_out).astype(jnp.bfloat16)
    down_part = outer_sum(cot_rows, hidden)
    hidden_grad = jnp.dot(cot_rows, down_block, preferred_element_type=jnp.float32)
    gate_sig = jax.nn.sigmoid(gate_lin)
    gate_low = (hidden_grad * up_lin * gate_sig * (1.0 + gate_lin * (1.0 - gate_sig))).astype(
        jnp.bfloat16
    )
    up_low = (hidden_grad * gate_lin * gate_sig).astype(jnp.bfloat16)
    gate_part = outer_sum(second_rows, gate_low)
    up_part = outer_sum(second_rows, up_low)
    second_sum = lax.all_to_all(
        (times_t(gate_low, gate_block) + times_t(up_low, up_block)).astype(jnp.bfloat16),
        "hid",
        split_axis=0,
        concat_axis=0,
        tiled=True,
    ).astype(jnp.float32)
    middle_part, second_part = second_back(sum_heads(second_sum, per_seq))
    middle_grad = cotangent.astype(jnp.float32) + middle_part
    mix_grad = middle_grad.astype(jnp.bfloat16)
    mix_rows = lax.all_to_all(fan_rows(mix_grad), "hid", split_axis=0, concat_axis=0, tiled=True)
    normed_grad = jnp.dot(mix_rows, o_block, preferred_element_type=jnp.float32)
    o_part = outer_sum(mix_rows, head_low)
    mixed_grad, group_part = norm_back(normed_grad)
    carried_state = (documents == before).astype(jnp.float32)[:, None]
    grad_local = outer_high(queries * jnp.exp(cumulative) * carried_state, mixed_grad)
    state_grad = jnp.zeros_like(grad_local)
    for number in range(block_total - 1):
        grad_in = decay[:, None] * state_grad + grad_local
        state_grad = from_behind(grad_in.astype(jnp.bfloat16), ("seq", "hid"), -H).astype(
            grad_in.dtype
        )
    q_grad_lin, f_grad_lin, i_grad_lin, gap_piece_grad = core_back((mixed_grad, state_grad))
    q_low = q_grad_lin.astype(jnp.bfloat16)
    f_low = f_grad_lin.astype(jnp.bfloat16)
    i_low = i_grad_lin.astype(jnp.bfloat16)
    q_part = outer_sum(first_rows, q_low)
    f_part = outer_sum(first_rows, f_low)
    i_part = outer_sum(first_rows, i_low)
    first_sum = lax.all_to_all(
        (times_t(q_low, q_block) + times_t(f_low, f_block) + times_t(i_low, i_block)).astype(
            jnp.bfloat16
        ),
        "hid",
        split_axis=0,
        concat_axis=0,
        tiled=True,
    ).astype(jnp.float32)
    entry_part, first_part = first_back(sum_heads(first_sum, per_seq))
    input_grad = middle_grad + entry_part
    q_back, f_back, i_back, o_back, gate_back, up_back, down_back = (
        lax.all_to_all(
            q_part.astype(jnp.bfloat16), ("seq", "hid"), split_axis=0, concat_axis=1, tiled=True
        ).astype(q_part.dtype),
        lax.all_to_all(
            f_part.astype(jnp.bfloat16), ("seq", "hid"), split_axis=0, concat_axis=1, tiled=True
        ).astype(f_part.dtype),
        lax.all_to_all(
            i_part.astype(jnp.bfloat16), ("seq", "hid"), split_axis=0, concat_axis=1, tiled=True
        ).astype(i_part.dtype),
        lax.all_to_all(
            o_part.astype(jnp.bfloat16), ("seq", "hid"), split_axis=0, concat_axis=1, tiled=True
        ).astype(o_part.dtype),
        lax.all_to_all(
            gate_part.astype(jnp.bfloat16), ("seq", "hid"), split_axis=0, concat_axis=1, tiled=True
        ).astype(gate_part.dtype),
        lax.all_to_all(
            up_part.astype(jnp.bfloat16), ("seq", "hid"), split_axis=0, concat_axis=1, tiled=True
        ).astype(up_part.dtype),
        lax.all_to_all(
            down_part.astype(jnp.bfloat16), ("seq", "hid"), split_axis=0, concat_axis=1, tiled=True
        ).astype(down_part.dtype),
    )
    o_grad = fold_copies(o_back, block_total)
    head_pick = (lax.iota(jnp.int32, H) == head_id).astype(jnp.float32)
    gap_full = (head_pick[:, None] * gap_piece_grad[None, :]).reshape(model)
    first_grad, second_grad, group_grad, gap_grad = lax.psum(
        (first_part, second_part, group_part, gap_full), ("seq", "hid")
    )
    return (
        output,
        input_grad,
        first_grad,
        fold_copies(q_back, block_total),
        fold_copies(f_back, block_total),
        fold_copies(i_back, block_total),
        o_grad,
        group_grad,
        gap_grad,
        second_grad,
        fold_copies(gate_back, block_total),
        fold_copies(up_back, block_total),
        fold_copies(down_back, block_total),
    )


F32 = jnp.float32
BF = jnp.bfloat16
MESH = pl.DeviceIdType.MESH
DMA = pltpu.SemaphoreType.DMA
VMEM = pltpu.VMEM
PIECES = 3
PARTS = 4
CUTS = PIECES * PARTS
AHEAD = (4, 4, 4, 4, 4, 4)
PACE = (4, 8)
TIMES = ((4, 5), (-1, 1), (16, 6), (6, 2), (8, 1), (0, 8))
VSPEC = pl.BlockSpec(memory_space=pltpu.VMEM)
ASPEC = pl.BlockSpec(memory_space=pl.ANY)
SSPEC = pl.BlockSpec(memory_space=pltpu.SMEM)


def place():
    h = lax.axis_index("hid")
    return h, h // 4, lax.rem(h // 2, 2), lax.rem(h, 2)


def partners():
    h, z, y, x = place()
    column = [lax.rem(z + k, 4) * 4 + lax.rem(h, 4) for k in (1, 2, 3)]
    return column, h + 2 - 4 * y, h + 1 - 2 * x


def greet(chips, core=False):
    gate = pltpu.get_barrier_semaphore()
    for chip in chips:
        pl.semaphore_signal(gate, inc=1, device_id={"hid": chip}, device_id_type=MESH)
    if core:
        other = 1 - lax.axis_index("seq")
        pl.semaphore_signal(gate, inc=1, device_id={"seq": other}, device_id_type=MESH)
    pl.semaphore_wait(gate, len(chips) + int(core))


def to_chip(src, dst, send, recv, chip):
    return pltpu.make_async_remote_copy(
        src_ref=src,
        dst_ref=dst,
        send_sem=send,
        recv_sem=recv,
        device_id={"hid": chip},
        device_id_type=MESH,
    )


def to_core(src, dst, send, recv):
    return pltpu.make_async_remote_copy(
        src_ref=src,
        dst_ref=dst,
        send_sem=send,
        recv_sem=recv,
        device_id={"seq": 1 - lax.axis_index("seq")},
        device_id_type=MESH,
    )


def comm_params(collective_id):
    return pltpu.CompilerParams(
        collective_id=collective_id, has_side_effects=True, vmem_limit_bytes=62 << 20
    )


class Cuts:
    def cut(self, c):
        i, j = c // PARTS, c % PARTS
        rows, cols = self.ref.shape[3] // PIECES, self.ref.shape[4] // PARTS
        return pl.ds(i * rows, rows), pl.ds(j * cols, cols), j % 2


class Gather(Cuts):
    def __init__(self, ref, sems):
        self.ref = ref
        self.s1, self.s2, self.s3, self.r1, self.r2, self.r3 = sems

    def start(self, c):
        h, z, y, x = place()
        column, py, px = partners()
        a, b, j = self.cut(c)
        ref = self.ref.at[z, y, x, a, b]
        for k in range(3):
            to_chip(ref, ref, self.s1, self.r1.at[c], column[k]).start()

    def second(self, c):
        h, z, y, x = place()
        column, py, px = partners()
        a, b, j = self.cut(c)
        three = self.ref.at[0:3, y, x, a, b]
        to_chip(three, three, self.s1, self.r1.at[c], px).wait_recv()
        ref = self.ref.at[:, y, x, a, b]
        to_chip(ref, ref, self.s2, self.r2.at[c], py if j else px).start()

    def third(self, c):
        h, z, y, x = place()
        column, py, px = partners()
        a, b, j = self.cut(c)
        got = self.ref.at[:, y, x, a, b]
        to_chip(got, got, self.s2, self.r2.at[c], px).wait_recv()
        ref = self.ref.at[:, :, x, a, b] if j else self.ref.at[:, y, :, a, b]
        to_chip(ref, ref, self.s3, self.r3, px if j else py).start()

    def finish(self):
        h, z, y, x = place()
        half, quarter, three = self.ref.at[:, 0], self.ref.at[:, 0, 0], self.ref.at[0:3, 0, 0]
        to_chip(half, half, self.s3, self.r3, x).wait_recv()
        for ref, sem in ((three, self.s1), (quarter, self.s2), (half, self.s3)):
            to_chip(ref, ref, sem, self.r3, x).wait_send()


def gather_sems():
    return [DMA, DMA, DMA, DMA((CUTS,)), DMA((CUTS,)), DMA]


class Scatter(Cuts):
    def __init__(self, ref, bufs, sems):
        self.ref, self.bufs = ref, bufs
        self.s1, self.s2, self.s3, self.r1, self.r2, self.r3 = sems

    def start(self, c):
        h, z, y, x = place()
        column, py, px = partners()
        a, b, j = self.cut(c)
        src = self.ref.at[:, :, 1 - x, a, b] if j else self.ref.at[:, 1 - y, :, a, b]
        to_chip(src, self.bufs[0].at[c], self.s1, self.r1.at[c], px if j else py).start()

    def second(self, c):
        h, z, y, x = place()
        column, py, px = partners()
        b1, t1, b2 = self.bufs[:3]
        a, b, j = self.cut(c)
        q = y if j else x
        to_chip(b1.at[c], b1.at[c], self.s1, self.r1.at[c], px).wait_recv()
        theirs = self.ref[:, 1 - q, x, a, b] if j else self.ref[:, y, 1 - q, a, b]
        b1[c, :, 1 - q] = (theirs.astype(F32) + b1[c, :, 1 - q].astype(F32)).astype(BF)
        to_chip(b1.at[c, :, 1 - q], b2.at[c], self.s2, self.r2.at[c], py if j else px).start()
        mine = self.ref[:, q, x, a, b] if j else self.ref[:, y, q, a, b]
        t1[c] = mine.astype(F32) + b1[c, :, q].astype(F32)

    def third(self, c):
        h, z, y, x = place()
        column, py, px = partners()
        b1, t1, b2, t2, b3 = self.bufs
        to_chip(b2.at[c], b2.at[c], self.s2, self.r2.at[c], px).wait_recv()
        t2[c] = t1[c, z] + b2[c, z].astype(F32)
        b2[c] = (t1[c] + b2[c].astype(F32)).astype(BF)
        for k in range(3):
            to_chip(
                b2.at[c, lax.rem(z + k + 1, 4)], b3.at[c, k], self.s3, self.r3.at[c], column[k]
            ).start()

    def last(self, c):
        h, z, y, x = place()
        b3, t2 = self.bufs[4], self.bufs[3]
        to_chip(b3.at[c], b3.at[c], self.s3, self.r3.at[c], x).wait_recv()
        return t2[c] + b3[c, 0].astype(F32) + b3[c, 1].astype(F32) + b3[c, 2].astype(F32)

    def finish(self):
        h, z, y, x = place()
        whole = self.bufs[0].at[:], self.bufs[2].at[:], self.bufs[4].at[:]
        for ref, sem in zip(whole, (self.s1, self.s2, self.s3)):
            to_chip(ref, ref, sem, self.r1.at[0], x).wait_send()


def scatter_bufs(rows, cols):
    n, r, w = CUTS, rows // PIECES, cols // PARTS
    return [
        VMEM((n, 4, 2, r, w), BF),
        VMEM((n, 4, r, w), F32),
        VMEM((n, 4, r, w), BF),
        VMEM((n, r, w), F32),
        VMEM((n, 3, r, w), BF),
    ]


def scatter_sems():
    return [DMA, DMA, DMA, DMA((CUTS,)), DMA((CUTS,)), DMA((CUTS,))]


def all_chips():
    h = lax.axis_index("hid")
    return [lax.rem(h + k, H) for k in range(1, H)]


class Plan:
    def __init__(self, *entries):
        self.entries = [[list(jobs), start, pace] for jobs, start, pace in entries]

    def step(self, t):
        for entry in self.entries:
            jobs, start, pace = entry
            if t >= start:
                for job in jobs[:pace]:
                    job()
                entry[0] = jobs[pace:]

    def rest(self):
        for entry in self.entries:
            for job in entry[0]:
                job()
            entry[0] = []

    def left(self, n):
        jobs, self.entries[n][0] = self.entries[n][0], []
        return jobs

    def during(self, jobs):
        for t, job in enumerate(jobs):
            job()
            self.step(t)


def unit_span(tiles, h):
    first = (tiles * h) // H
    return first, (tiles * (h + 1)) // H - first


def lanes(tile, count):
    return pl.ds(pl.multiple_of(tile * 128, 128), count * 128)


class Bulk:
    def __init__(self, items, tiles, depth, sems):
        self.items, self.tiles, self.depth = items, tiles, depth
        self.ss, self.rs, self.ls, self.xs, self.xr = sems
        self.least = tiles // H

    def sized(self, n, chip, act):
        if not self.items[n][3]:
            act(chip, 1)
            return
        first, count = unit_span(self.tiles, chip)
        if self.tiles % H == 0:
            act(first, self.least)
            return
        for number in (self.least, self.least + 1):
            pl.when(count == number)(functools.partial(act, first, number))

    def ours(self, view):
        half = H * self.depth
        return pl.ds(pl.multiple_of(view * half, half), half)

    def row(self, core, chip):
        return pl.ds(pl.multiple_of((core * H + chip) * self.depth, self.depth), self.depth)


class Fetch(Bulk):
    def copy(self, n, k, chip, first, count):
        h, b = lax.axis_index("hid"), lax.axis_index("seq")
        src, dst, at, _ = self.items[n]
        return to_chip(
            src.at[:, lanes(first, count)],
            dst.at[self.row(b, h), lanes(at, count)],
            self.ss.at[n],
            self.rs.at[n],
            chip,
        )

    def own(self, n, first, count):
        h, b = lax.axis_index("hid"), lax.axis_index("seq")
        src, dst, at, _ = self.items[n]
        return pltpu.make_async_copy(
            src.at[:, lanes(first, count)], dst.at[self.row(b, h), lanes(at, count)], self.ls.at[n]
        )

    def job(self, n, k):
        def run():
            chip = lax.rem(lax.axis_index("hid") + k, H)
            self.sized(
                n, chip, lambda first, count: self.copy(n, k, chip, first, count).start()
            )

        return run

    def jobs(self):
        return [self.job(n, k) for n in range(len(self.items)) for k in range(1, H)]

    def start_own(self):
        h = lax.axis_index("hid")
        for n, (_, dst, _, split) in enumerate(self.items):
            self.sized(n, h, lambda first, count: self.own(n, first, count).start())
            if split and self.tiles % H:

                @pl.when(unit_span(self.tiles, h)[1] == self.least)
                def _():
                    dst[:, self.least * 128 :] = jnp.zeros((dst.shape[0], 128), BF)

    def swap(self, n, tile, count, slot):
        b = lax.axis_index("seq")
        view = self.items[n][1].at[self.ours(b), lanes(tile, count)]
        return to_core(view, view, self.xs.at[n, slot], self.xr.at[n, slot])

    def each_swap(self, n, act):
        at, split = self.items[n][2:]
        act(self.swap(n, at, self.least if split else 1, 0))
        if split and self.tiles % H:

            @pl.when(unit_span(self.tiles, lax.axis_index("hid"))[1] > self.least)
            def _():
                act(self.swap(n, self.least, 1, 1))

    def arrive(self, n):
        h = lax.axis_index("hid")
        self.sized(n, h, lambda first, count: self.own(n, first, count).wait())
        self.sized(n, h, lambda first, count: self.rest(n, count).wait_recv())
        self.each_swap(n, lambda copy: copy.start())

    def settle(self, ns):
        for n in ns:
            self.each_swap(n, lambda copy: copy.wait())

    def finish(self):
        h = lax.axis_index("hid")
        for n in range(len(self.items)):
            self.sized(n, h, lambda first, count: self.rest(n, count).wait_send())

    def rest(self, n, count):
        src, dst, at, split = self.items[n]
        others = self.tiles - count if split else H - 1
        return to_chip(
            src.at[:, lanes(0, others)],
            dst.at[pl.ds(0, (H - 1) * self.depth), lanes(at, count)],
            self.ss.at[n],
            self.rs.at[n],
            lax.axis_index("hid"),
        )


class Return(Bulk):
    def __init__(self, items, parts, tiles, depth, sems):
        super().__init__(items, tiles, depth, sems)
        self.parts = parts

    def swap(self, p):
        part, total, _ = self.parts[p]
        return to_core(
            part.at[self.ours(1 - lax.axis_index("seq"))], total, self.xs.at[p, 0], self.xr.at[p, 0]
        )

    def add(self, p):
        def run():
            part, total, _ = self.parts[p]
            b = lax.axis_index("seq")
            self.swap(p).wait()
            half, step = total.shape[0], 128

            @pl.loop(0, half // step)
            def _(t):
                at = pl.ds(pl.multiple_of(t * step, step), step)
                own = pl.ds(pl.multiple_of(b * half + t * step, step), step)
                total[at] = (total[at].astype(F32) + part[own].astype(F32)).astype(BF)

            for n in self.parts[p][2]:
                h = lax.axis_index("hid")
                self.sized(n, h, lambda first, count: self.own(n, first, count).start())

        return run

    def copy(self, n, k, chip, first, count):
        dst, src, at, _ = self.items[n]
        return to_chip(
            src.at[self.row(0, chip), lanes(at, count)],
            dst.at[:, lanes(first, count)],
            self.ss.at[n],
            self.rs.at[n],
            chip,
        )

    def own(self, n, first, count):
        dst, src, at, _ = self.items[n]
        return pltpu.make_async_copy(
            src.at[self.row(0, lax.axis_index("hid")), lanes(at, count)],
            dst.at[:, lanes(first, count)],
            self.ls.at[n],
        )

    def job(self, n, k):
        def run():
            h = lax.axis_index("hid")
            chip = lax.rem(h + k, H)
            self.sized(n, h, lambda first, count: self.copy(n, k, chip, first, count).start())

        return run

    def jobs(self, p):
        return [self.add(p)] + [self.job(n, k) for n in self.parts[p][2] for k in range(1, H)]

    def finish(self):
        h = lax.axis_index("hid")
        for n in range(len(self.items)):
            self.sized(n, h, lambda first, count: self.own(n, first, count).wait())
            self.sized(n, h, lambda first, count: self.rest(n, count).wait())

    def rest(self, n, count):
        dst, src, at, split = self.items[n]
        others = self.tiles - count if split else H - 1
        return to_chip(
            src.at[pl.ds(0, (H - 1) * self.depth), lanes(at, count)],
            dst.at[:, lanes(0, others)],
            self.ss.at[n],
            self.rs.at[n],
            lax.axis_index("hid"),
        )


def bulk_sems(n):
    return [DMA((n,)), DMA((n,)), DMA((n,)), DMA((n, 2)), DMA((n, 2))]


def split_refs(refs, *counts):
    groups, at = [], 0
    for count in counts:
        groups.append(refs[at : at + count])
        at += count
    assert at == len(refs)
    return groups


def row_norm(rows):
    return lax.rsqrt(jnp.mean(rows * rows, axis=-1, keepdims=True) + EPS)


def gather_jobs(gather, ahead):
    lag = PARTS

    def step(t):
        def run():
            if t == 0:
                for c in range(ahead):
                    gather.start(c)
            if t < CUTS:
                gather.second(t)
                if t + ahead < CUTS:
                    gather.start(t + ahead)
            if t >= lag:
                gather.third(t - lag)

        return run

    return [step(t) for t in range(CUTS + lag)]


def scatter_jobs(scatter, ahead, rows_done, meanwhile=()):
    lag, held = PARTS, []

    def step(t):
        def run():
            if t == 0:
                for c in range(ahead):
                    scatter.start(c)
                for job in meanwhile:
                    job()
            if t < CUTS:
                scatter.second(t)
                if t + ahead < CUTS:
                    scatter.start(t + ahead)
            if 0 <= t - lag // 2 < CUTS:
                scatter.third(t - lag // 2)
            c = t - lag - lag // 2
            if c >= 0:
                held.append(scatter.last(c))
                if len(held) == PARTS:
                    rows_done(c // PARTS, jnp.concatenate(held, axis=1))
                    held.clear()

        return run

    return [step(t) for t in range(CUTS + lag + lag // 2)]


def turn_jobs(scatter, gather, ahead, rows_done, meanwhile=()):
    lag = PARTS

    def write(i, rows):
        rows_done(i, rows)
        if i == PIECES - 1:
            scatter.finish()
        for c in range(i * PARTS, (i + 1) * PARTS):
            gather.start(c)

    first = scatter_jobs(scatter, ahead, write, meanwhile)

    def step(t):
        def run():
            if t < len(first):
                first[t]()
            c = t - 2 * lag - lag // 2 - (PARTS - 1)
            if 0 <= c < CUTS:
                gather.second(c)
            if 0 <= c - lag < CUTS:
                gather.third(c - lag)

        return run

    return [step(t) for t in range(CUTS + 3 * lag + lag // 2 + PARTS - 1)]


def norm_back(rows, grad, gain):
    factor = row_norm(rows)
    normal = rows * factor
    scaled = grad * gain
    back = factor * (scaled - normal * jnp.mean(scaled * normal, axis=-1, keepdims=True))
    return back, jnp.sum(grad * normal, axis=0, keepdims=True)


def row_blocks(ref):
    size = 2 * ref.shape[1] * ref.shape[2] * ref.shape[3]
    return [(pl.ds(2 * n, 2), pl.ds(n * size, size)) for n in range(ref.shape[0] // 2)]


def merged(rows):
    return rows.reshape(-1, rows.shape[-1])


def doc_tile(lengths_ref, start, shape, dim):
    positions = start + lax.broadcasted_iota(jnp.int32, shape, dim)
    documents = jnp.full(shape, -1, jnp.int32)
    begin = jnp.int32(0)
    for n in range(lengths_ref.shape[0]):
        documents = documents + jnp.where(positions >= begin, 1, 0)
        begin = begin + lengths_ref[n]
    return documents


def layer_kernel(tiles, *refs):
    (
        (x_ref, c_ref, lengths, first_gain, second_gain, gain_ref, gap_all),
        weights,
        (out, in_grad, totals, *homes),
        (first, cot, second, mix, part, glu_part),
        (wqfi, wo, wg, wu, wd),
        (entry, middle, mid, dcol, drow, gap_ref),
        (lin, mixed, states, head, cum, d_head, d_lin, d_mixed, backs),
        (hidden, gate_low, up_low),
        (gqfi, go, gg, gu, gd),
        (tqfi, to, tg, tu, td),
        main_bufs,
        glu_bufs,
        gather_sets,
        scatter_sets,
        (f_out, f_in, b_out, b_in, fs, fr, bs, br, ls),
        (mine, theirs, chips, vs, vr, ws, wr),
        bulk_sets,
    ) = split_refs(refs, 7, 7, 10, 6, 5, 6, 9, 3, 5, 5, 5, 5, 24, 24, 9, 7, 20)
    q, f, i, o, g, u, d = weights
    hq, hf, hi, ho, hg, hu, hd = homes
    h, z, y, x = place()
    core = lax.axis_index("seq")
    depth, size = q.shape[0], x_ref.shape[1] // PIECES
    extent = lin.shape[0]
    mixer_in = Fetch(
        [(q, wqfi, 0, False), (f, wqfi, 1, False), (i, wqfi, 2, False), (o, wo, 0, False)],
        H,
        depth,
        bulk_sets[0:5],
    )
    units_in = Fetch(
        [(g, wg, 0, True), (u, wu, 0, True), (d, wd, 0, True)], tiles, depth, bulk_sets[5:10]
    )
    units_out = Return(
        [(hd, td, 0, True), (hg, tg, 0, True), (hu, tu, 0, True)],
        [(gd, td, (0,)), (gg, tg, (1,)), (gu, tu, (2,))],
        tiles,
        depth,
        bulk_sets[10:15],
    )
    mixer_out = Return(
        [(ho, to, 0, False), (hq, tqfi, 0, False), (hf, tqfi, 1, False), (hi, tqfi, 2, False)],
        [(go, to, (0,)), (gqfi, tqfi, (1, 2, 3))],
        H,
        depth,
        bulk_sets[15:20],
    )
    gathers = [
        Gather(ref, gather_sets[6 * n : 6 * n + 6])
        for n, ref in enumerate((first, cot, second, mix))
    ]
    scatters = [
        Scatter(ref, bufs, scatter_sets[6 * n : 6 * n + 6])
        for n, (ref, bufs) in enumerate(
            ((part, main_bufs), (part, main_bufs), (part, main_bufs), (glu_part, glu_bufs))
        )
    ]

    own = pltpu.make_async_copy(c_ref.at[0], cot.at[z, y, x], ls)
    own.start()
    mixer_in.start_own()
    for n in range(PIECES):
        at = pl.ds(n * size, size)
        rows = x_ref[0, at].astype(F32)
        entry[at] = rows
        first[z, y, x, at] = (rows * row_norm(rows) * first_gain[...]).astype(BF)
    greet(all_chips(), core=True)
    own.wait()

    def documents():
        gap_ref[...] = gap_all[pl.ds(h, 1)]
        base = core * extent
        for c, at in spans(extent):
            dcol[at] = doc_tile(lengths, base + c * SPAN, (SPAN, SPAN), 0)
            drow[8 * c : 8 * c + 8] = doc_tile(lengths, base + c * SPAN, (8, SPAN), 1)
        drow[8 * len(spans(extent)) :] = doc_tile(lengths, base - 1, (8, SPAN), 0)
        mine[...] = jnp.zeros_like(mine)
        units_in.start_own()

    mixer_jobs = mixer_in.jobs()
    plan = Plan(([documents], 0, 1), (mixer_jobs[: 3 * (H - 1)], *TIMES[0]))
    plan.during(gather_jobs(gathers[0], AHEAD[0]))
    plan.rest()
    for job in mixer_jobs[3 * (H - 1) :]:
        job()
    for n in range(3):
        mixer_in.arrive(n)
    gathers[0].finish()
    mixer_in.settle((0, 1, 2))
    plan = Plan((gather_jobs(gathers[1], AHEAD[1]), *TIMES[1]), (units_in.jobs(), *TIMES[2]))

    for n, at in row_blocks(first):
        lin[at] = jnp.dot(merged(first[n]), wqfi[...], preferred_element_type=F32)
        plan.step(-1)
    blocks = (lin, gap_ref, gain_ref, dcol, drow)
    mix_forward(blocks, mixed, states, head, cum, (f_out, f_in, fs, fr), lambda: plan.step(-1))
    mixer_in.arrive(3)
    mixer_in.settle((3,))
    for n, at in row_blocks(part):
        part[n] = times_t(head[at], wo[...]).astype(BF).reshape((2,) + part.shape[1:])
        plan.step(-1)

    def middle_rows(n, total):
        at = pl.ds(n * size, size)
        rows = entry[at] + total
        middle[at] = rows
        second[z, y, x, at] = (rows * row_norm(rows) * second_gain[...]).astype(BF)

    plan.during(turn_jobs(scatters[0], gathers[2], AHEAD[2], middle_rows))
    plan.rest()
    for n in range(3):
        units_in.arrive(n)
    gathers[1].finish()
    gathers[2].finish()
    mixer_in.finish()
    units_in.settle((0, 1, 2))
    units_in.finish()

    for n, at in row_blocks(second):
        rows = merged(second[n])
        gate_lin = jnp.dot(rows, wg[...], preferred_element_type=F32)
        up_lin = jnp.dot(rows, wu[...], preferred_element_type=F32)
        d_hidden = jnp.dot(merged(cot[n]), wd[...], preferred_element_type=F32)
        s = jax.nn.sigmoid(gate_lin)
        silu = gate_lin * s
        hidden[at] = (silu * up_lin).astype(BF)
        gate_low[at] = (d_hidden * up_lin * s * (1.0 + gate_lin * (1.0 - s))).astype(BF)
        up_low[at] = (d_hidden * silu).astype(BF)
        total = times_t(gate_low[at], wg[...]) + times_t(up_low[at], wu[...])
        part[n] = total.astype(BF).reshape((2,) + part.shape[1:])

    def grad_rows(n, total):
        at = pl.ds(n * size, size)
        back, gains = norm_back(middle[at], total, second_gain[...])
        mine[16:32] = mine[16:32] + gains.reshape(16, 128)
        rows = c_ref[0, at].astype(F32) + back
        mid[at] = rows
        mix[z, y, x, at] = rows.astype(BF)

    def out_rows(n, total):
        at = pl.ds(n * size, size)
        out[0, at] = (middle[at] + total).astype(BF)

    def outer(dst, rows, cols, giver, p):
        width = 512

        def piece(start):
            def run():
                at = pl.ds(start, width)
                dst[at] = outer_sum(merged(rows[:, :, :, :, at]), cols[...]).astype(BF)

            return run

        return [piece(start) for start in range(0, rows.shape[4], width)] + [
            lambda: giver.swap(p).start()
        ]

    def glu_block(n, at):
        def run():
            rows = times_t(hidden[at], wd[...]).astype(BF)
            glu_part[n] = rows.reshape((2,) + glu_part.shape[1:])

        return run

    returns = outer(gg, second, gate_low, units_out, 1) + units_out.jobs(0)
    returns += outer(gu, second, up_low, units_out, 2) + units_out.jobs(1) + units_out.jobs(2)
    outward = [glu_block(n, at) for n, at in row_blocks(glu_part)]
    outward += scatter_jobs(scatters[3], AHEAD[4], out_rows)
    plan = Plan((returns, *TIMES[3]), (outward, *TIMES[4]))
    plan.during(
        turn_jobs(
            scatters[1], gathers[3], AHEAD[3], grad_rows, outer(gd, cot, hidden, units_out, 0)
        )
    )
    gathers[3].finish()

    kept = plan.left(0), plan.left(1)
    plan = Plan((outer(go, mix, head, mixer_out, 0), 0, 2), (kept[0], 0, PACE[0]), (kept[1], 0, 1))
    for n, at in row_blocks(mix):
        d_head[at] = jnp.dot(merged(mix[n]), wo[...], preferred_element_type=F32)
        plan.step(0)
    group, gap = mix_backward(
        blocks, mixed, states, cum, d_head, d_lin, d_mixed, backs, (b_out, b_in, bs, br),
        lambda: plan.step(0),
    )
    mine[32:33] = group
    mine[40:41] = gap
    for n, at in row_blocks(part):
        part[n] = times_t(d_lin[at], wqfi[...]).astype(BF).reshape((2,) + part.shape[1:])

    def in_rows(n, total):
        at = pl.ds(n * size, size)
        back, gains = norm_back(entry[at], total, first_gain[...])
        in_grad[0, at] = mid[at] + back
        mine[0:16] = mine[0:16] + gains.reshape(16, 128)
        if n == PIECES - 1:
            swap = to_core(mine, theirs, vs, vr)
            swap.start()
            swap.wait()
            chips[h] = mine[...] + theirs[...]
            for k in range(1, H):
                to_chip(chips.at[h], chips.at[h], ws, wr, lax.rem(h + k, H)).start()

    for job in plan.left(0):
        job()
    kept = plan.left(1), plan.left(2)
    plan = Plan(
        (kept[0], 0, PACE[1]), (mixer_out.jobs(0) + mixer_out.jobs(1), *TIMES[5]), (kept[1], 0, 1)
    )
    plan.during(
        scatter_jobs(
            scatters[2], AHEAD[5], in_rows, outer(gqfi, first, d_lin, mixer_out, 1)
        )
    )
    plan.rest()
    others = chips.at[0 : H - 1]
    to_chip(others, others, ws, wr, h).wait()
    acc = chips[0, 0:40]
    for chip in range(1, H):
        acc = acc + chips[chip, 0:40]
    totals[0:40] = acc
    for chip in range(H):
        totals[40 + chip : 41 + chip] = chips[chip, 40:41]
    scatters[2].finish()
    scatters[3].finish()
    units_out.finish()
    mixer_out.finish()


def layer(inputs, cotangent, lengths, first_gain, second_gain, group_gain, gap_log, weights):
    _, rows, cols = inputs.shape
    depth, units = weights[-1].shape
    extent, count = H * rows, 2 * H * depth
    tiles = units // 128
    wide = -(-tiles // H) * 128
    home = lambda width: jax.ShapeDtypeStruct((depth, width), BF)
    full = VMEM((4, 2, 2, rows, cols), BF)
    local = VMEM((rows, cols), F32)
    tile = VMEM((extent, SPAN), F32)
    square = VMEM((SPAN, SPAN), F32)
    squares = VMEM((extent // SPAN, SPAN, SPAN), F32)
    widths = (384, 128, wide, wide, wide)
    return pl.pallas_call(
        functools.partial(layer_kernel, tiles),
        out_shape=[
            jax.ShapeDtypeStruct((1, rows, cols), BF),
            jax.ShapeDtypeStruct((1, rows, cols), F32),
            jax.ShapeDtypeStruct((56, 128), F32),
        ]
        + [home(cols)] * 4
        + [home(units)] * 3,
        in_specs=[VSPEC] * 2 + [SSPEC] + [VSPEC] * 4 + [ASPEC] * 7,
        out_specs=[VSPEC] * 3 + [ASPEC] * 7,
        scratch_shapes=[full] * 6
        + [VMEM((count, width), BF) for width in widths]
        + [local, local, local, VMEM((extent, SPAN), jnp.int32)]
        + [VMEM((8 * (extent // SPAN) + 8, SPAN), jnp.int32), VMEM((1, SPAN), F32)]
        + [VMEM((extent, 384), F32), tile, squares, VMEM((extent, SPAN), BF), tile]
        + [tile, VMEM((extent, 384), BF), tile, squares]
        + [VMEM((extent, wide), BF)] * 3
        + [VMEM((count, width), BF) for width in widths]
        + [VMEM((count // 2, width), BF) for width in widths]
        + scatter_bufs(rows, cols)
        + scatter_bufs(rows, cols)
        + gather_sems() * 4
        + scatter_sems() * 4
        + [square] * 4
        + [DMA] * 5
        + [VMEM((48, 128), F32), VMEM((48, 128), F32), VMEM((H, 48, 128), F32)]
        + [DMA, DMA, DMA, DMA]
        + bulk_sems(4)
        + bulk_sems(3)
        + bulk_sems(3)
        + bulk_sems(4),
        compiler_params=comm_params(1),
    )(
        inputs,
        cotangent,
        lengths,
        first_gain[None],
        second_gain[None],
        group_gain[None],
        gap_log.reshape(H, SPAN),
        *weights,
    )


def product(left, right, at_left, at_right):
    return lax.dot_general(
        left, right, (((at_left,), (at_right,)), ((), ())), preferred_element_type=F32
    )


def halves(rows):
    high = rows.astype(BF)
    return high, (rows - high.astype(F32)).astype(BF)


def mm(left, right, at_left, at_right):
    left_high, left_low = halves(left)
    right_high, right_low = halves(right)
    small = product(left_high, right_low, at_left, at_right)
    small = small + product(left_low, right_high, at_left, at_right)
    return product(left_high, right_high, at_left, at_right) + small


def tri_sum(rows, reverse=False):
    r = lax.broadcasted_iota(jnp.int32, (SPAN, SPAN), 0)
    c = lax.broadcasted_iota(jnp.int32, (SPAN, SPAN), 1)
    picked = jnp.where((r <= c) if reverse else (r >= c), 1.0, 0.0).astype(BF)
    high = rows.astype(BF)
    rest = rows - high.astype(F32)
    middle, low = halves(rest)
    return product(picked, high, 1, 0) + product(picked, middle, 1, 0) + product(picked, low, 1, 0)


def span_gates(lin_ref, gap_ref, at):
    q_lin, f_lin, values = lin_ref[at, 0:128], lin_ref[at, 128:256], lin_ref[at, 256:384]
    s = jax.nn.sigmoid(q_lin)
    key = jnp.exp(gap_ref[...]) * jax.nn.sigmoid(-f_lin)
    return q_lin, f_lin, values, s, key


def span_masks(dcol_ref, drow_ref, c, at):
    r = lax.broadcasted_iota(jnp.int32, (SPAN, SPAN), 0)
    k = lax.broadcasted_iota(jnp.int32, (SPAN, SPAN), 1)
    dcol, drow = dcol_ref[at], drow_ref[8 * c : 8 * c + 1]
    last = (c + 1) * SPAN - 1
    end = dcol_ref[last : last + 1]
    if c:
        before = dcol_ref[c * SPAN - 1 : c * SPAN]
    else:
        count = drow_ref.shape[0]
        before = drow_ref[count - 8 : count - 7]
    same = jnp.where(jnp.logical_and(dcol == drow, r >= k), 1.0, 0.0)
    carried = jnp.where(dcol == before, 1.0, 0.0)
    keep = jnp.where(dcol == end, 1.0, 0.0)
    whole = jnp.where(end == before, 1.0, 0.0)
    return same, carried, keep, whole


def spans(extent):
    return [(c, pl.ds(c * SPAN, SPAN)) for c in range(extent // SPAN)]


def mix_forward(blocks, mixed_ref, states_ref, head_ref, cum_ref, handover, between):
    out_ref, in_ref, send, recv = handover
    lin_ref, gap_ref, gain_ref, dcol_ref, drow_ref = blocks
    steps = spans(lin_ref.shape[0])
    state = jnp.zeros((SPAN, SPAN), F32)
    for c, at in steps:
        q_lin, f_lin, values, s, key = span_gates(lin_ref, gap_ref, at)
        same, carried, keep, whole = span_masks(dcol_ref, drow_ref, c, at)
        cum = tri_sum(jnp.log1p(-key))
        cum_ref[at] = cum
        end = cum[SPAN - 1 : SPAN]
        fresh = mm(values, jnp.exp(end - cum) * key * keep, 0, 0)
        states_ref[c] = fresh
        state = state * (jnp.exp(end) * whole) + fresh
    out_ref[...] = state
    copy = to_core(out_ref, in_ref, send, recv)
    copy.start()
    between()
    copy.wait()
    state = in_ref[...] * lax.axis_index("seq").astype(F32)
    for c, at in steps:
        q_lin, f_lin, values, s, key = span_gates(lin_ref, gap_ref, at)
        same, carried, keep, whole = span_masks(dcol_ref, drow_ref, c, at)
        cum = cum_ref[at]
        end = cum[SPAN - 1 : SPAN]
        fresh = states_ref[c]
        states_ref[c] = state
        decayed = q_lin * s * jnp.exp(cum)
        scores = mm(decayed, key * jnp.exp(-cum), 1, 1) * same
        mixed = mm(scores, values, 1, 0) + carried * mm(decayed, state, 1, 1)
        mixed_ref[at] = mixed
        head_ref[at] = (mixed * row_norm(mixed) * gain_ref[...]).astype(BF)
        state = state * (jnp.exp(end) * whole) + fresh
        if c % 2:
            between()


def mix_backward(
    blocks, mixed_ref, states_ref, cum_ref, dhead_ref, dlin_ref, do_ref, back_ref, handover, between
):
    out_ref, in_ref, send, recv = handover
    lin_ref, gap_ref, gain_ref, dcol_ref, drow_ref = blocks
    steps = spans(lin_ref.shape[0])
    group = jnp.zeros((1, SPAN), F32)
    adjoint = jnp.zeros((SPAN, SPAN), F32)
    for c, at in reversed(steps):
        d_mixed, gains = norm_back(mixed_ref[at], dhead_ref[at], gain_ref[...])
        group = group + gains
        do_ref[at] = d_mixed
        q_lin, f_lin, values, s, key = span_gates(lin_ref, gap_ref, at)
        same, carried, keep, whole = span_masks(dcol_ref, drow_ref, c, at)
        cum = cum_ref[at]
        back = mm(d_mixed, carried * (q_lin * s * jnp.exp(cum)), 0, 0)
        back_ref[c] = back
        adjoint = adjoint * (jnp.exp(cum[SPAN - 1 : SPAN]) * whole) + back
    out_ref[...] = adjoint
    copy = to_core(out_ref, in_ref, send, recv)
    copy.start()
    between()
    copy.wait()
    adjoint = in_ref[...] * (1 - lax.axis_index("seq")).astype(F32)
    gap = jnp.zeros((1, SPAN), F32)
    for c, at in reversed(steps):
        q_lin, f_lin, values, s, key = span_gates(lin_ref, gap_ref, at)
        same, carried, keep, whole = span_masks(dcol_ref, drow_ref, c, at)
        cum, d_mixed, state = cum_ref[at], do_ref[at], states_ref[c]
        grow, shrink = jnp.exp(-cum), jnp.exp(cum)
        end = cum[SPAN - 1 : SPAN]
        decayed, grown = q_lin * s * shrink, key * grow
        rest = jnp.exp(end - cum) * keep
        tail, through = rest * key, jnp.exp(end) * whole
        scores = mm(decayed, grown, 1, 1) * same
        d_scores = mm(d_mixed, values, 1, 1) * same
        d_values = mm(scores, d_mixed, 0, 0) + mm(tail, adjoint, 1, 1)
        d_decayed = mm(d_scores, grown, 1, 0) + carried * mm(d_mixed, state, 1, 0)
        d_grown = mm(d_scores, decayed, 0, 0)
        d_tail = mm(values, adjoint, 1, 0)
        held = tail * d_tail
        d_cum = decayed * d_decayed - grown * d_grown - held
        d_end = jnp.sum(held, axis=0, keepdims=True) + through * jnp.sum(
            state * adjoint, axis=0, keepdims=True
        )
        d_log = tri_sum(d_cum, reverse=True) + d_end
        d_key = d_grown * grow + d_tail * rest - d_log / (1.0 - key)
        scaled = d_key * key
        gap = gap + jnp.sum(scaled, axis=0, keepdims=True)
        dlin_ref[at, 0:128] = (d_decayed * shrink * s * (1.0 + q_lin * (1.0 - s))).astype(BF)
        dlin_ref[at, 128:256] = (-scaled * jax.nn.sigmoid(f_lin)).astype(BF)
        dlin_ref[at, 256:384] = d_values.astype(BF)
        adjoint = adjoint * through + back_ref[c]
        if c % 2:
            between()
    return group, gap


def finish_kernel(out_ref, in_ref, totals_ref, *refs):
    out, in_grad, first, second, group, gap = refs[7:13]
    out[...] = out_ref[...]
    in_grad[...] = in_ref[...]
    first[...] = totals_ref[0:16]
    second[...] = totals_ref[16:32]
    group[...] = totals_ref[32:33]
    gap[...] = totals_ref[40:56]
    for src, dst in zip(refs[:7], refs[13:]):
        dst[...] = src[...].astype(F32)


def finish(output, input_grad, totals, grads):
    depth = grads[0].shape[0]
    rows, cols = output.shape[1:]
    steps = 4
    piece = depth // steps
    local = pl.BlockSpec((1, piece, cols), lambda n: (0, jnp.minimum(n, rows // piece - 1), 0))
    whole = lambda height: pl.BlockSpec((height, 128), lambda n: (0, 0))
    grad = [pl.BlockSpec((piece, g.shape[1]), lambda n: (n, 0)) for g in grads]
    vector = lambda height: jax.ShapeDtypeStruct((height, 128), F32)
    return pl.pallas_call(
        finish_kernel,
        grid=(steps,),
        out_shape=[
            jax.ShapeDtypeStruct(output.shape, BF),
            jax.ShapeDtypeStruct(input_grad.shape, F32),
            vector(16),
            vector(16),
            vector(1),
            vector(16),
        ]
        + [jax.ShapeDtypeStruct(g.shape, F32) for g in grads],
        in_specs=[local, local, whole(56)] + grad,
        out_specs=[local, local, whole(16), whole(16), whole(1), whole(16)] + grad,
        compiler_params=pltpu.CompilerParams(vmem_limit_bytes=62 << 20),
    )(output, input_grad, totals, *grads)


def fast_body(
    inputs,
    cotangent,
    lengths,
    first_gain,
    q_weight,
    f_weight,
    i_weight,
    o_weight,
    group_gain,
    gap_log,
    second_gain,
    gate_weight,
    up_weight,
    down_weight,
):
    model = inputs.shape[2]
    output, input_grad, totals, *grads = layer(
        inputs,
        cotangent,
        lengths,
        first_gain,
        second_gain,
        group_gain,
        gap_log,
        (q_weight, f_weight, i_weight, o_weight, gate_weight, up_weight, down_weight),
    )
    output, input_grad, first_grad, second_grad, group_grad, gap_grad, *grads = finish(
        output, input_grad, totals, grads
    )
    q_grad, f_grad, i_grad, o_grad, gate_grad, up_grad, down_grad = grads
    return (
        output,
        input_grad,
        first_grad.reshape(model),
        q_grad,
        f_grad,
        i_grad,
        o_grad,
        group_grad.reshape(SPAN),
        gap_grad.reshape(model),
        second_grad.reshape(model),
        gate_grad,
        up_grad,
        down_grad,
    )


def solution(mesh):
    placed = (
        P("seq", "hid", None),
        P("seq", "hid", None),
        P(),
        P(),
        P(("seq", "hid"), None),
        P(("seq", "hid"), None),
        P(("seq", "hid"), None),
        P(("seq", "hid"), None),
        P(),
        P(),
        P(),
        P(("seq", "hid"), None),
        P(("seq", "hid"), None),
        P(("seq", "hid"), None),
    )
    body = fast_body if mesh.shape["hid"] == H else wide_body
    return jax.shard_map(
        body,
        mesh=mesh,
        in_specs=placed,
        out_specs=(
            P("seq", "hid", None),
            P("seq", "hid", None),
            P(),
            P(("seq", "hid"), None),
            P(("seq", "hid"), None),
            P(("seq", "hid"), None),
            P(("seq", "hid"), None),
            P(),
            P(),
            P(),
            P(("seq", "hid"), None),
            P(("seq", "hid"), None),
            P(("seq", "hid"), None),
        ),
        check_vma=False,
    )
```

```python
import functools

import jax
import jax.numpy as jnp
from jax import lax
from jax.experimental import pallas as pl
from jax.experimental.pallas import tpu as pltpu
from jax.sharding import PartitionSpec as P

H = 16
SPAN = 128


EPS = 1e-06
HIGH_PRECISION = lax.Precision.HIGHEST


def from_behind(block, axis, distance):
    devices = range(lax.axis_size(axis))
    route = [(i - distance, i) for i in devices if i - distance in devices]
    return lax.ppermute(block, axis, route)


def normed(entries, gain_vec):
    factor = lax.rsqrt(jnp.mean(entries * entries, axis=-1, keepdims=True) + EPS)
    return entries * factor * gain_vec


def gates(q_part, f_part, gap_piece):
    key_gate = jnp.exp(gap_piece) * jax.nn.sigmoid(-f_part)
    return (jax.nn.silu(q_part), key_gate, jnp.log1p(-key_gate))


def doc_starts(lengths):
    count = lengths.shape[0]
    earlier = lax.broadcasted_iota(jnp.int32, (count, count), 0) > lax.broadcasted_iota(
        jnp.int32, (count, count), 1
    )
    return jnp.sum(jnp.where(earlier, lengths[None, :], 0), axis=1)


def running_sum(rows):
    extent = rows.shape[-2]
    lower = (
        lax.broadcasted_iota(jnp.int32, (extent, extent), 0)
        >= lax.broadcasted_iota(jnp.int32, (extent, extent), 1)
    ).astype(jnp.float32)
    return jnp.einsum("ts,...sk->...tk", lower, rows, precision=HIGH_PRECISION)


def doc_ids(lengths, positions):
    starts = doc_starts(lengths)
    covered = (starts[None, :] <= positions[:, None]).astype(jnp.int32)
    return jnp.sum(covered, axis=1) - 1


def span_step(memory_state, pieces):
    queries, key_gate, value_rows, log_decay, documents, before = pieces
    cumulative = running_sum(log_decay)
    query_decayed = queries * jnp.exp(cumulative)
    k_grown = key_gate * jnp.exp(-cumulative)
    extent = documents.shape[0]
    row_ids = lax.broadcasted_iota(jnp.int32, (extent, extent), 0)
    col_ids = lax.broadcasted_iota(jnp.int32, (extent, extent), 1)
    same_doc = jnp.logical_and(documents[:, None] == documents[None, :], row_ids >= col_ids).astype(
        jnp.float32
    )
    scores = (
        jnp.einsum("hck,hsk->hcs", query_decayed, k_grown, precision=HIGH_PRECISION)
        * same_doc[None]
    )
    within_block = jnp.einsum("hcs,hsv->hcv", scores, value_rows, precision=HIGH_PRECISION)
    carried_state = (documents == before).astype(jnp.float32)[None, :, None]
    output_rows = within_block + carried_state * jnp.einsum(
        "awn,ani->awi", query_decayed, memory_state, precision=HIGH_PRECISION
    )
    last_cum = cumulative[:, -1:, :]
    keep_mask = (documents == documents[-1]).astype(jnp.float32)[None, :, None]
    tail_key_rows = jnp.exp(last_cum - cumulative) * key_gate * keep_mask
    whole_block = (documents[-1] == before).astype(jnp.float32)
    fresh_state = jnp.einsum("wfx,wfg->wxg", tail_key_rows, value_rows, precision=HIGH_PRECISION)
    memory_state = jnp.exp(last_cum[:, 0, :])[:, :, None] * whole_block * memory_state + fresh_state
    return (memory_state, output_rows)


def recur(queries, key_gate, value_rows, log_decay, documents, before, memory_state):
    head_count, extent, columns = queries.shape
    span_count = extent // SPAN

    def by_span(tensor):
        return jnp.swapaxes(tensor.reshape(head_count, span_count, SPAN, tensor.shape[-1]), 0, 1)

    doc_rows = documents.reshape(span_count, SPAN)
    befores = jnp.concatenate([jnp.reshape(before, (1,)), doc_rows[:-1, -1]])
    memory_state, span_out = lax.scan(
        jax.checkpoint(span_step),
        memory_state,
        (
            by_span(queries),
            by_span(key_gate),
            by_span(value_rows),
            by_span(log_decay),
            doc_rows,
            befores,
        ),
    )
    return (
        jnp.swapaxes(span_out, 0, 1).reshape(head_count, extent, value_rows.shape[-1]),
        memory_state,
    )


def spread_cols(weight, copies):
    row_count = weight.shape[0]
    shaped = weight.reshape(row_count, 1, H, weight.shape[1] // H)
    return jnp.broadcast_to(shaped, (row_count, copies, H, shaped.shape[3])).reshape(
        row_count, copies * weight.shape[1]
    )


def fold_copies(received, copies):
    row_count = received.shape[0]
    return jnp.sum(received.reshape(row_count, copies, received.shape[1] // copies), axis=1)


def fan_rows(local_rows):
    blocks_here, row_count, columns = local_rows.shape
    return jnp.broadcast_to(local_rows[:, None], (blocks_here, H, row_count, columns)).reshape(
        blocks_here * H * row_count, columns
    )


def sum_heads(received, blocks_here):
    total_rows, columns = received.shape
    return jnp.sum(
        received.reshape(blocks_here, H, total_rows // (blocks_here * H), columns), axis=1
    )


def times_t(left_mat, right_mat):
    return lax.dot_general(
        left_mat, right_mat, (((1,), (1,)), ((), ())), preferred_element_type=jnp.float32
    )


def outer_sum(left_mat, right_mat):
    return lax.dot_general(
        left_mat, right_mat, (((0,), (0,)), ((), ())), preferred_element_type=jnp.float32
    )


def outer_high(left_mat, right_mat):
    return lax.dot_general(
        left_mat,
        right_mat,
        (((0,), (0,)), ((), ())),
        precision=HIGH_PRECISION,
        preferred_element_type=jnp.float32,
    )


def wide_body(
    inputs,
    cotangent,
    lengths,
    first_gain,
    q_weight,
    f_weight,
    i_weight,
    o_weight,
    group_gain,
    gap_log,
    second_gain,
    gate_weight,
    up_weight,
    down_weight,
):
    hid_size = lax.axis_size("hid")
    per_seq = hid_size // H
    block_total = lax.axis_size("seq") * per_seq
    hid_place = lax.axis_index("hid")
    head_id = hid_place % H
    block_id = lax.axis_index("seq") * per_seq + hid_place // H
    model = inputs.shape[2]
    head_width = model // H
    block_len = hid_size * inputs.shape[1]
    entries = inputs.astype(jnp.float32)
    q_block, f_block, i_block, o_block, gate_block, up_block, down_block = (
        lax.all_to_all(
            spread_cols(q_weight, block_total),
            ("seq", "hid"),
            split_axis=1,
            concat_axis=0,
            tiled=True,
        ),
        lax.all_to_all(
            spread_cols(f_weight, block_total),
            ("seq", "hid"),
            split_axis=1,
            concat_axis=0,
            tiled=True,
        ),
        lax.all_to_all(
            spread_cols(i_weight, block_total),
            ("seq", "hid"),
            split_axis=1,
            concat_axis=0,
            tiled=True,
        ),
        lax.all_to_all(
            spread_cols(o_weight, block_total),
            ("seq", "hid"),
            split_axis=1,
            concat_axis=0,
            tiled=True,
        ),
        lax.all_to_all(
            spread_cols(gate_weight, block_total),
            ("seq", "hid"),
            split_axis=1,
            concat_axis=0,
            tiled=True,
        ),
        lax.all_to_all(
            spread_cols(up_weight, block_total),
            ("seq", "hid"),
            split_axis=1,
            concat_axis=0,
            tiled=True,
        ),
        lax.all_to_all(
            spread_cols(down_weight, block_total),
            ("seq", "hid"),
            split_axis=1,
            concat_axis=0,
            tiled=True,
        ),
    )
    positions = block_id * block_len + lax.iota(jnp.int32, block_len)
    documents = doc_ids(lengths, positions)
    before = doc_ids(lengths, jnp.reshape(block_id * block_len - 1, (1,)))[0]
    first_norm, first_back = jax.vjp(normed, entries, first_gain)
    first_low = first_norm.astype(jnp.bfloat16)
    first_rows = lax.all_to_all(fan_rows(first_low), "hid", split_axis=0, concat_axis=0, tiled=True)
    q_lin = jnp.dot(first_rows, q_block, preferred_element_type=jnp.float32)
    f_lin = jnp.dot(first_rows, f_block, preferred_element_type=jnp.float32)
    i_lin = jnp.dot(first_rows, i_block, preferred_element_type=jnp.float32)
    gap_part = lax.dynamic_slice_in_dim(gap_log, head_id * head_width, head_width)
    queries, key_gate, log_decay = gates(q_lin, f_lin, gap_part)
    cumulative = running_sum(log_decay)
    last_cum = cumulative[-1]
    tail_key_rows = (
        jnp.exp(last_cum[None, :] - cumulative)
        * key_gate
        * (documents == documents[-1]).astype(jnp.float32)[:, None]
    )
    local_state = outer_high(tail_key_rows, i_lin)
    decay = jnp.exp(last_cum) * (documents[-1] == before).astype(jnp.float32)
    state_in = jnp.zeros_like(local_state)
    for number in range(block_total - 1):
        state_out = decay[:, None] * state_in + local_state
        state_in = from_behind(state_out.astype(jnp.bfloat16), ("seq", "hid"), H).astype(
            state_out.dtype
        )

    def core(q_part, f_part, i_part, gap_piece):
        queries_in, keys_in, logs_in = gates(q_part, f_part, gap_piece)
        mixed_all, memory_state = recur(
            queries_in[None],
            keys_in[None],
            i_part[None],
            logs_in[None],
            documents,
            before,
            state_in[None],
        )
        return (mixed_all[0], memory_state[0])

    (mixed_out, _), core_back = jax.vjp(core, q_lin, f_lin, i_lin, gap_part)
    head_normed, norm_back = jax.vjp(normed, mixed_out, group_gain)
    head_low = head_normed.astype(jnp.bfloat16)
    mix_out = sum_heads(
        lax.all_to_all(
            times_t(head_low, o_block).astype(jnp.bfloat16),
            "hid",
            split_axis=0,
            concat_axis=0,
            tiled=True,
        ).astype(jnp.float32),
        per_seq,
    )
    middle = entries + mix_out
    second_norm, second_back = jax.vjp(normed, middle, second_gain)
    second_low = second_norm.astype(jnp.bfloat16)
    second_rows, cot_rows = (
        lax.all_to_all(fan_rows(second_low), "hid", split_axis=0, concat_axis=0, tiled=True),
        lax.all_to_all(fan_rows(cotangent), "hid", split_axis=0, concat_axis=0, tiled=True),
    )
    gate_lin = jnp.dot(second_rows, gate_block, preferred_element_type=jnp.float32)
    up_lin = jnp.dot(second_rows, up_block, preferred_element_type=jnp.float32)
    hidden = (jax.nn.silu(gate_lin) * up_lin).astype(jnp.bfloat16)
    glu_out = sum_heads(
        lax.all_to_all(
            times_t(hidden, down_block).astype(jnp.bfloat16),
            "hid",
            split_axis=0,
            concat_axis=0,
            tiled=True,
        ).astype(jnp.float32),
        per_seq,
    )
    output = (middle + glu_out).astype(jnp.bfloat16)
    down_part = outer_sum(cot_rows, hidden)
    hidden_grad = jnp.dot(cot_rows, down_block, preferred_element_type=jnp.float32)
    gate_sig = jax.nn.sigmoid(gate_lin)
    gate_low = (hidden_grad * up_lin * gate_sig * (1.0 + gate_lin * (1.0 - gate_sig))).astype(
        jnp.bfloat16
    )
    up_low = (hidden_grad * gate_lin * gate_sig).astype(jnp.bfloat16)
    gate_part = outer_sum(second_rows, gate_low)
    up_part = outer_sum(second_rows, up_low)
    second_sum = lax.all_to_all(
        (times_t(gate_low, gate_block) + times_t(up_low, up_block)).astype(jnp.bfloat16),
        "hid",
        split_axis=0,
        concat_axis=0,
        tiled=True,
    ).astype(jnp.float32)
    middle_part, second_part = second_back(sum_heads(second_sum, per_seq))
    middle_grad = cotangent.astype(jnp.float32) + middle_part
    mix_grad = middle_grad.astype(jnp.bfloat16)
    mix_rows = lax.all_to_all(fan_rows(mix_grad), "hid", split_axis=0, concat_axis=0, tiled=True)
    normed_grad = jnp.dot(mix_rows, o_block, preferred_element_type=jnp.float32)
    o_part = outer_sum(mix_rows, head_low)
    mixed_grad, group_part = norm_back(normed_grad)
    carried_state = (documents == before).astype(jnp.float32)[:, None]
    grad_local = outer_high(queries * jnp.exp(cumulative) * carried_state, mixed_grad)
    state_grad = jnp.zeros_like(grad_local)
    for number in range(block_total - 1):
        grad_in = decay[:, None] * state_grad + grad_local
        state_grad = from_behind(grad_in.astype(jnp.bfloat16), ("seq", "hid"), -H).astype(
            grad_in.dtype
        )
    q_grad_lin, f_grad_lin, i_grad_lin, gap_piece_grad = core_back((mixed_grad, state_grad))
    q_low = q_grad_lin.astype(jnp.bfloat16)
    f_low = f_grad_lin.astype(jnp.bfloat16)
    i_low = i_grad_lin.astype(jnp.bfloat16)
    q_part = outer_sum(first_rows, q_low)
    f_part = outer_sum(first_rows, f_low)
    i_part = outer_sum(first_rows, i_low)
    first_sum = lax.all_to_all(
        (times_t(q_low, q_block) + times_t(f_low, f_block) + times_t(i_low, i_block)).astype(
            jnp.bfloat16
        ),
        "hid",
        split_axis=0,
        concat_axis=0,
        tiled=True,
    ).astype(jnp.float32)
    entry_part, first_part = first_back(sum_heads(first_sum, per_seq))
    input_grad = middle_grad + entry_part
    q_back, f_back, i_back, o_back, gate_back, up_back, down_back = (
        lax.all_to_all(
            q_part.astype(jnp.bfloat16), ("seq", "hid"), split_axis=0, concat_axis=1, tiled=True
        ).astype(q_part.dtype),
        lax.all_to_all(
            f_part.astype(jnp.bfloat16), ("seq", "hid"), split_axis=0, concat_axis=1, tiled=True
        ).astype(f_part.dtype),
        lax.all_to_all(
            i_part.astype(jnp.bfloat16), ("seq", "hid"), split_axis=0, concat_axis=1, tiled=True
        ).astype(i_part.dtype),
        lax.all_to_all(
            o_part.astype(jnp.bfloat16), ("seq", "hid"), split_axis=0, concat_axis=1, tiled=True
        ).astype(o_part.dtype),
        lax.all_to_all(
            gate_part.astype(jnp.bfloat16), ("seq", "hid"), split_axis=0, concat_axis=1, tiled=True
        ).astype(gate_part.dtype),
        lax.all_to_all(
            up_part.astype(jnp.bfloat16), ("seq", "hid"), split_axis=0, concat_axis=1, tiled=True
        ).astype(up_part.dtype),
        lax.all_to_all(
            down_part.astype(jnp.bfloat16), ("seq", "hid"), split_axis=0, concat_axis=1, tiled=True
        ).astype(down_part.dtype),
    )
    o_grad = fold_copies(o_back, block_total)
    head_pick = (lax.iota(jnp.int32, H) == head_id).astype(jnp.float32)
    gap_full = (head_pick[:, None] * gap_piece_grad[None, :]).reshape(model)
    first_grad, second_grad, group_grad, gap_grad = lax.psum(
        (first_part, second_part, group_part, gap_full), ("seq", "hid")
    )
    return (
        output,
        input_grad,
        first_grad,
        fold_copies(q_back, block_total),
        fold_copies(f_back, block_total),
        fold_copies(i_back, block_total),
        o_grad,
        group_grad,
        gap_grad,
        second_grad,
        fold_copies(gate_back, block_total),
        fold_copies(up_back, block_total),
        fold_copies(down_back, block_total),
    )


F32 = jnp.float32
BF = jnp.bfloat16
MESH = pl.DeviceIdType.MESH
DMA = pltpu.SemaphoreType.DMA
VMEM = pltpu.VMEM
PIECES = 3
PARTS = 4
CUTS = PIECES * PARTS
AHEAD = (4, 4, 4, 4, 4, 4)
PACE = (4, 8)
TIMES = ((4, 5), (-1, 1), (16, 6), (8, 2), (8, 1), (0, 8))
VSPEC = pl.BlockSpec(memory_space=pltpu.VMEM)
ASPEC = pl.BlockSpec(memory_space=pl.ANY)
SSPEC = pl.BlockSpec(memory_space=pltpu.SMEM)


def place():
    h = lax.axis_index("hid")
    return h, h // 4, lax.rem(h // 2, 2), lax.rem(h, 2)


def partners():
    h, z, y, x = place()
    column = [lax.rem(z + k, 4) * 4 + lax.rem(h, 4) for k in (1, 2, 3)]
    return column, h + 2 - 4 * y, h + 1 - 2 * x


def greet(chips, core=False):
    gate = pltpu.get_barrier_semaphore()
    for chip in chips:
        pl.semaphore_signal(gate, inc=1, device_id={"hid": chip}, device_id_type=MESH)
    if core:
        other = 1 - lax.axis_index("seq")
        pl.semaphore_signal(gate, inc=1, device_id={"seq": other}, device_id_type=MESH)
    pl.semaphore_wait(gate, len(chips) + int(core))


def to_chip(src, dst, send, recv, chip):
    return pltpu.make_async_remote_copy(
        src_ref=src,
        dst_ref=dst,
        send_sem=send,
        recv_sem=recv,
        device_id={"hid": chip},
        device_id_type=MESH,
    )


def to_core(src, dst, send, recv):
    return pltpu.make_async_remote_copy(
        src_ref=src,
        dst_ref=dst,
        send_sem=send,
        recv_sem=recv,
        device_id={"seq": 1 - lax.axis_index("seq")},
        device_id_type=MESH,
    )


def comm_params(collective_id):
    return pltpu.CompilerParams(
        collective_id=collective_id, has_side_effects=True, vmem_limit_bytes=62 << 20
    )


class Cuts:
    def cut(self, c):
        i, j = c // PARTS, c % PARTS
        rows, cols = self.ref.shape[3] // PIECES, self.ref.shape[4] // PARTS
        return pl.ds(i * rows, rows), pl.ds(j * cols, cols), j % 2


class Gather(Cuts):
    def __init__(self, ref, sems):
        self.ref = ref
        self.s1, self.s2, self.s3, self.r1, self.r2, self.r3 = sems

    def start(self, c):
        h, z, y, x = place()
        column, py, px = partners()
        a, b, j = self.cut(c)
        ref = self.ref.at[z, y, x, a, b]
        for k in range(3):
            to_chip(ref, ref, self.s1, self.r1.at[c], column[k]).start()

    def second(self, c):
        h, z, y, x = place()
        column, py, px = partners()
        a, b, j = self.cut(c)
        three = self.ref.at[0:3, y, x, a, b]
        to_chip(three, three, self.s1, self.r1.at[c], px).wait_recv()
        ref = self.ref.at[:, y, x, a, b]
        to_chip(ref, ref, self.s2, self.r2.at[c], py if j else px).start()

    def third(self, c):
        h, z, y, x = place()
        column, py, px = partners()
        a, b, j = self.cut(c)
        got = self.ref.at[:, y, x, a, b]
        to_chip(got, got, self.s2, self.r2.at[c], px).wait_recv()
        ref = self.ref.at[:, :, x, a, b] if j else self.ref.at[:, y, :, a, b]
        to_chip(ref, ref, self.s3, self.r3, px if j else py).start()

    def finish(self):
        h, z, y, x = place()
        half, quarter, three = self.ref.at[:, 0], self.ref.at[:, 0, 0], self.ref.at[0:3, 0, 0]
        to_chip(half, half, self.s3, self.r3, x).wait_recv()
        for ref, sem in ((three, self.s1), (quarter, self.s2), (half, self.s3)):
            to_chip(ref, ref, sem, self.r3, x).wait_send()


def gather_sems():
    return [DMA, DMA, DMA, DMA((CUTS,)), DMA((CUTS,)), DMA]


class Scatter(Cuts):
    def __init__(self, ref, bufs, sems):
        self.ref, self.bufs = ref, bufs
        self.s1, self.s2, self.s3, self.r1, self.r2, self.r3 = sems

    def start(self, c):
        h, z, y, x = place()
        column, py, px = partners()
        a, b, j = self.cut(c)
        src = self.ref.at[:, :, 1 - x, a, b] if j else self.ref.at[:, 1 - y, :, a, b]
        to_chip(src, self.bufs[0].at[c], self.s1, self.r1.at[c], px if j else py).start()

    def second(self, c):
        h, z, y, x = place()
        column, py, px = partners()
        b1, t1, b2 = self.bufs[:3]
        a, b, j = self.cut(c)
        q = y if j else x
        to_chip(b1.at[c], b1.at[c], self.s1, self.r1.at[c], px).wait_recv()
        theirs = self.ref[:, 1 - q, x, a, b] if j else self.ref[:, y, 1 - q, a, b]
        b1[c, :, 1 - q] = (theirs.astype(F32) + b1[c, :, 1 - q].astype(F32)).astype(BF)
        to_chip(b1.at[c, :, 1 - q], b2.at[c], self.s2, self.r2.at[c], py if j else px).start()
        mine = self.ref[:, q, x, a, b] if j else self.ref[:, y, q, a, b]
        t1[c] = mine.astype(F32) + b1[c, :, q].astype(F32)

    def third(self, c):
        h, z, y, x = place()
        column, py, px = partners()
        b1, t1, b2, t2, b3 = self.bufs
        to_chip(b2.at[c], b2.at[c], self.s2, self.r2.at[c], px).wait_recv()
        t2[c] = t1[c, z] + b2[c, z].astype(F32)
        b2[c] = (t1[c] + b2[c].astype(F32)).astype(BF)
        for k in range(3):
            to_chip(
                b2.at[c, lax.rem(z + k + 1, 4)], b3.at[c, k], self.s3, self.r3.at[c], column[k]
            ).start()

    def last(self, c):
        h, z, y, x = place()
        b3, t2 = self.bufs[4], self.bufs[3]
        to_chip(b3.at[c], b3.at[c], self.s3, self.r3.at[c], x).wait_recv()
        return t2[c] + b3[c, 0].astype(F32) + b3[c, 1].astype(F32) + b3[c, 2].astype(F32)

    def finish(self):
        h, z, y, x = place()
        whole = self.bufs[0].at[:], self.bufs[2].at[:], self.bufs[4].at[:]
        for ref, sem in zip(whole, (self.s1, self.s2, self.s3)):
            to_chip(ref, ref, sem, self.r1.at[0], x).wait_send()


def scatter_bufs(rows, cols):
    n, r, w = CUTS, rows // PIECES, cols // PARTS
    return [
        VMEM((n, 4, 2, r, w), BF),
        VMEM((n, 4, r, w), F32),
        VMEM((n, 4, r, w), BF),
        VMEM((n, r, w), F32),
        VMEM((n, 3, r, w), BF),
    ]


def scatter_sems():
    return [DMA, DMA, DMA, DMA((CUTS,)), DMA((CUTS,)), DMA((CUTS,))]


def all_chips():
    h = lax.axis_index("hid")
    return [lax.rem(h + k, H) for k in range(1, H)]


class Plan:
    def __init__(self, *entries):
        self.entries = [[list(jobs), start, pace] for jobs, start, pace in entries]

    def step(self, t):
        for entry in self.entries:
            jobs, start, pace = entry
            if t >= start:
                for job in jobs[:pace]:
                    job()
                entry[0] = jobs[pace:]

    def rest(self):
        for entry in self.entries:
            for job in entry[0]:
                job()
            entry[0] = []

    def left(self, n):
        jobs, self.entries[n][0] = self.entries[n][0], []
        return jobs

    def during(self, jobs):
        for t, job in enumerate(jobs):
            job()
            self.step(t)


def unit_span(tiles, h):
    first = (tiles * h) // H
    return first, (tiles * (h + 1)) // H - first


def lanes(tile, count):
    return pl.ds(pl.multiple_of(tile * 128, 128), count * 128)


class Bulk:
    def __init__(self, items, tiles, depth, sems):
        self.items, self.tiles, self.depth = items, tiles, depth
        self.ss, self.rs, self.ls, self.xs, self.xr = sems
        self.least = tiles // H

    def sized(self, n, chip, act):
        if not self.items[n][3]:
            act(chip, 1)
            return
        first, count = unit_span(self.tiles, chip)
        if self.tiles % H == 0:
            act(first, self.least)
            return
        for number in (self.least, self.least + 1):
            pl.when(count == number)(functools.partial(act, first, number))

    def ours(self, view):
        half = H * self.depth
        return pl.ds(pl.multiple_of(view * half, half), half)

    def row(self, core, chip):
        return pl.ds(pl.multiple_of((core * H + chip) * self.depth, self.depth), self.depth)


class Fetch(Bulk):
    def copy(self, n, k, chip, first, count):
        h, b = lax.axis_index("hid"), lax.axis_index("seq")
        src, dst, at, _ = self.items[n]
        return to_chip(
            src.at[:, lanes(first, count)],
            dst.at[self.row(b, h), lanes(at, count)],
            self.ss.at[n],
            self.rs.at[n],
            chip,
        )

    def own(self, n, first, count):
        h, b = lax.axis_index("hid"), lax.axis_index("seq")
        src, dst, at, _ = self.items[n]
        return pltpu.make_async_copy(
            src.at[:, lanes(first, count)], dst.at[self.row(b, h), lanes(at, count)], self.ls.at[n]
        )

    def job(self, n, k):
        def run():
            chip = lax.rem(lax.axis_index("hid") + k, H)
            self.sized(
                n, chip, lambda first, count: self.copy(n, k, chip, first, count).start()
            )

        return run

    def jobs(self):
        return [self.job(n, k) for n in range(len(self.items)) for k in range(1, H)]

    def start_own(self):
        h = lax.axis_index("hid")
        for n, (_, dst, _, split) in enumerate(self.items):
            self.sized(n, h, lambda first, count: self.own(n, first, count).start())
            if split and self.tiles % H:

                @pl.when(unit_span(self.tiles, h)[1] == self.least)
                def _():
                    dst[:, self.least * 128 :] = jnp.zeros((dst.shape[0], 128), BF)

    def swap(self, n, tile, count, slot):
        b = lax.axis_index("seq")
        view = self.items[n][1].at[self.ours(b), lanes(tile, count)]
        return to_core(view, view, self.xs.at[n, slot], self.xr.at[n, slot])

    def each_swap(self, n, act):
        at, split = self.items[n][2:]
        act(self.swap(n, at, self.least if split else 1, 0))
        if split and self.tiles % H:

            @pl.when(unit_span(self.tiles, lax.axis_index("hid"))[1] > self.least)
            def _():
                act(self.swap(n, self.least, 1, 1))

    def arrive(self, n):
        h = lax.axis_index("hid")
        self.sized(n, h, lambda first, count: self.own(n, first, count).wait())
        self.sized(n, h, lambda first, count: self.rest(n, count).wait_recv())
        self.each_swap(n, lambda copy: copy.start())

    def settle(self, ns):
        for n in ns:
            self.each_swap(n, lambda copy: copy.wait())

    def finish(self):
        h = lax.axis_index("hid")
        for n in range(len(self.items)):
            self.sized(n, h, lambda first, count: self.rest(n, count).wait_send())

    def rest(self, n, count):
        src, dst, at, split = self.items[n]
        others = self.tiles - count if split else H - 1
        return to_chip(
            src.at[:, lanes(0, others)],
            dst.at[pl.ds(0, (H - 1) * self.depth), lanes(at, count)],
            self.ss.at[n],
            self.rs.at[n],
            lax.axis_index("hid"),
        )


class Return(Bulk):
    def __init__(self, items, parts, tiles, depth, sems):
        super().__init__(items, tiles, depth, sems)
        self.parts = parts

    def swap(self, p):
        part, total, _ = self.parts[p]
        return to_core(
            part.at[self.ours(1 - lax.axis_index("seq"))], total, self.xs.at[p, 0], self.xr.at[p, 0]
        )

    def add(self, p):
        def run():
            part, total, _ = self.parts[p]
            b = lax.axis_index("seq")
            self.swap(p).wait()
            half, step = total.shape[0], 128

            @pl.loop(0, half // step)
            def _(t):
                at = pl.ds(pl.multiple_of(t * step, step), step)
                own = pl.ds(pl.multiple_of(b * half + t * step, step), step)
                total[at] = (total[at].astype(F32) + part[own].astype(F32)).astype(BF)

            for n in self.parts[p][2]:
                h = lax.axis_index("hid")
                self.sized(n, h, lambda first, count: self.own(n, first, count).start())

        return run

    def copy(self, n, k, chip, first, count):
        dst, src, at, _ = self.items[n]
        return to_chip(
            src.at[self.row(0, chip), lanes(at, count)],
            dst.at[:, lanes(first, count)],
            self.ss.at[n],
            self.rs.at[n],
            chip,
        )

    def own(self, n, first, count):
        dst, src, at, _ = self.items[n]
        return pltpu.make_async_copy(
            src.at[self.row(0, lax.axis_index("hid")), lanes(at, count)],
            dst.at[:, lanes(first, count)],
            self.ls.at[n],
        )

    def job(self, n, k):
        def run():
            h = lax.axis_index("hid")
            chip = lax.rem(h + k, H)
            self.sized(n, h, lambda first, count: self.copy(n, k, chip, first, count).start())

        return run

    def jobs(self, p):
        return [self.add(p)] + [self.job(n, k) for n in self.parts[p][2] for k in range(1, H)]

    def finish(self):
        h = lax.axis_index("hid")
        for n in range(len(self.items)):
            self.sized(n, h, lambda first, count: self.own(n, first, count).wait())
            self.sized(n, h, lambda first, count: self.rest(n, count).wait())

    def rest(self, n, count):
        dst, src, at, split = self.items[n]
        others = self.tiles - count if split else H - 1
        return to_chip(
            src.at[pl.ds(0, (H - 1) * self.depth), lanes(at, count)],
            dst.at[:, lanes(0, others)],
            self.ss.at[n],
            self.rs.at[n],
            lax.axis_index("hid"),
        )


def bulk_sems(n):
    return [DMA((n,)), DMA((n,)), DMA((n,)), DMA((n, 2)), DMA((n, 2))]


def split_refs(refs, *counts):
    groups, at = [], 0
    for count in counts:
        groups.append(refs[at : at + count])
        at += count
    assert at == len(refs)
    return groups


def row_norm(rows):
    return lax.rsqrt(jnp.mean(rows * rows, axis=-1, keepdims=True) + EPS)


def gather_jobs(gather, ahead):
    lag = PARTS

    def step(t):
        def run():
            if t == 0:
                for c in range(ahead):
                    gather.start(c)
            if t < CUTS:
                gather.second(t)
                if t + ahead < CUTS:
                    gather.start(t + ahead)
            if t >= lag:
                gather.third(t - lag)

        return run

    return [step(t) for t in range(CUTS + lag)]


def scatter_jobs(scatter, ahead, rows_done, meanwhile=()):
    lag, held = PARTS, []

    def step(t):
        def run():
            if t == 0:
                for c in range(ahead):
                    scatter.start(c)
                for job in meanwhile:
                    job()
            if t < CUTS:
                scatter.second(t)
                if t + ahead < CUTS:
                    scatter.start(t + ahead)
            if 0 <= t - lag // 2 < CUTS:
                scatter.third(t - lag // 2)
            c = t - lag - lag // 2
            if c >= 0:
                held.append(scatter.last(c))
                if len(held) == PARTS:
                    rows_done(c // PARTS, jnp.concatenate(held, axis=1))
                    held.clear()

        return run

    return [step(t) for t in range(CUTS + lag + lag // 2)]


def turn_jobs(scatter, gather, ahead, rows_done, meanwhile=()):
    lag = PARTS

    def write(i, rows):
        rows_done(i, rows)
        if i == PIECES - 1:
            scatter.finish()
        for c in range(i * PARTS, (i + 1) * PARTS):
            gather.start(c)

    first = scatter_jobs(scatter, ahead, write, meanwhile)

    def step(t):
        def run():
            if t < len(first):
                first[t]()
            c = t - 2 * lag - lag // 2 - (PARTS - 1)
            if 0 <= c < CUTS:
                gather.second(c)
            if 0 <= c - lag < CUTS:
                gather.third(c - lag)

        return run

    return [step(t) for t in range(CUTS + 3 * lag + lag // 2 + PARTS - 1)]


def norm_back(rows, grad, gain):
    factor = row_norm(rows)
    normal = rows * factor
    scaled = grad * gain
    back = factor * (scaled - normal * jnp.mean(scaled * normal, axis=-1, keepdims=True))
    return back, jnp.sum(grad * normal, axis=0, keepdims=True)


def row_blocks(ref):
    size = 2 * ref.shape[1] * ref.shape[2] * ref.shape[3]
    return [(pl.ds(2 * n, 2), pl.ds(n * size, size)) for n in range(ref.shape[0] // 2)]


def merged(rows):
    return rows.reshape(-1, rows.shape[-1])


def doc_tile(lengths_ref, start, shape, dim):
    positions = start + lax.broadcasted_iota(jnp.int32, shape, dim)
    documents = jnp.full(shape, -1, jnp.int32)
    begin = jnp.int32(0)
    for n in range(lengths_ref.shape[0]):
        documents = documents + jnp.where(positions >= begin, 1, 0)
        begin = begin + lengths_ref[n]
    return documents


def layer_kernel(tiles, *refs):
    (
        (x_ref, c_ref, lengths, first_gain, second_gain, gain_ref, gap_all),
        weights,
        (out, in_grad, totals, *homes),
        (first, cot, second, mix, part, glu_part),
        (wqfi, wo, wg, wu, wd),
        (entry, middle, mid, dcol, drow, gap_ref),
        (lin, mixed, states, head, cum, d_head, d_lin, d_mixed, backs),
        (hidden, gate_low, up_low, gate_ref, up_ref),
        (gqfi, go, gg, gu, gd),
        (tqfi, to, tg, tu, td),
        main_bufs,
        glu_bufs,
        gather_sets,
        scatter_sets,
        (f_out, f_in, b_out, b_in, fs, fr, bs, br, ls),
        (mine, theirs, chips, vs, vr, ws, wr),
        bulk_sets,
    ) = split_refs(refs, 7, 7, 10, 6, 5, 6, 9, 5, 5, 5, 5, 5, 24, 24, 9, 7, 20)
    q, f, i, o, g, u, d = weights
    hq, hf, hi, ho, hg, hu, hd = homes
    h, z, y, x = place()
    core = lax.axis_index("seq")
    depth, size = q.shape[0], x_ref.shape[1] // PIECES
    extent = lin.shape[0]
    mixer_in = Fetch(
        [(q, wqfi, 0, False), (f, wqfi, 1, False), (i, wqfi, 2, False), (o, wo, 0, False)],
        H,
        depth,
        bulk_sets[0:5],
    )
    units_in = Fetch(
        [(g, wg, 0, True), (u, wu, 0, True), (d, wd, 0, True)], tiles, depth, bulk_sets[5:10]
    )
    units_out = Return(
        [(hd, td, 0, True), (hg, tg, 0, True), (hu, tu, 0, True)],
        [(gd, td, (0,)), (gg, tg, (1,)), (gu, tu, (2,))],
        tiles,
        depth,
        bulk_sets[10:15],
    )
    mixer_out = Return(
        [(ho, to, 0, False), (hq, tqfi, 0, False), (hf, tqfi, 1, False), (hi, tqfi, 2, False)],
        [(go, to, (0,)), (gqfi, tqfi, (1, 2, 3))],
        H,
        depth,
        bulk_sets[15:20],
    )
    gathers = [
        Gather(ref, gather_sets[6 * n : 6 * n + 6])
        for n, ref in enumerate((first, cot, second, mix))
    ]
    scatters = [
        Scatter(ref, bufs, scatter_sets[6 * n : 6 * n + 6])
        for n, (ref, bufs) in enumerate(
            ((part, main_bufs), (part, main_bufs), (part, main_bufs), (glu_part, glu_bufs))
        )
    ]

    own = pltpu.make_async_copy(c_ref.at[0], cot.at[z, y, x], ls)
    own.start()
    mixer_in.start_own()
    for n in range(PIECES):
        at = pl.ds(n * size, size)
        rows = x_ref[0, at].astype(F32)
        entry[at] = rows
        first[z, y, x, at] = (rows * row_norm(rows) * first_gain[...]).astype(BF)
    greet(all_chips(), core=True)
    own.wait()

    def documents():
        gap_ref[...] = gap_all[pl.ds(h, 1)]
        base = core * extent
        for c, at in spans(extent):
            dcol[at] = doc_tile(lengths, base + c * SPAN, (SPAN, SPAN), 0)
            drow[8 * c : 8 * c + 8] = doc_tile(lengths, base + c * SPAN, (8, SPAN), 1)
        drow[8 * len(spans(extent)) :] = doc_tile(lengths, base - 1, (8, SPAN), 0)
        mine[...] = jnp.zeros_like(mine)
        units_in.start_own()

    mixer_jobs = mixer_in.jobs()
    plan = Plan(([documents], 0, 1), (mixer_jobs[: 3 * (H - 1)], *TIMES[0]))
    plan.during(gather_jobs(gathers[0], AHEAD[0]))
    plan.rest()
    for job in mixer_jobs[3 * (H - 1) :]:
        job()
    for n in range(3):
        mixer_in.arrive(n)
    gathers[0].finish()
    mixer_in.settle((0, 1, 2))
    plan = Plan((gather_jobs(gathers[1], AHEAD[1]), *TIMES[1]), (units_in.jobs(), *TIMES[2]))

    for n, at in row_blocks(first):
        lin[at] = jnp.dot(merged(first[n]), wqfi[...], preferred_element_type=F32)
        plan.step(-1)
    blocks = (lin, gap_ref, gain_ref, dcol, drow)
    mix_forward(blocks, mixed, states, head, cum, (f_out, f_in, fs, fr), lambda: plan.step(-1))
    mixer_in.arrive(3)
    mixer_in.settle((3,))
    for n, at in row_blocks(part):
        part[n] = times_t(head[at], wo[...]).astype(BF).reshape((2,) + part.shape[1:])
        plan.step(-1)

    def middle_rows(n, total):
        at = pl.ds(n * size, size)
        rows = entry[at] + total
        middle[at] = rows
        second[z, y, x, at] = (rows * row_norm(rows) * second_gain[...]).astype(BF)

    plan.during(turn_jobs(scatters[0], gathers[2], AHEAD[2], middle_rows))
    plan.rest()
    units_in.arrive(0)
    units_in.arrive(1)
    gathers[2].finish()
    units_in.settle((0, 1))

    for n, at in row_blocks(second):
        rows = merged(second[n])
        gate_ref[at] = jnp.dot(rows, wg[...], preferred_element_type=F32)
        up_ref[at] = jnp.dot(rows, wu[...], preferred_element_type=F32)
    units_in.arrive(2)
    gathers[1].finish()
    mixer_in.finish()
    units_in.settle((2,))
    units_in.finish()
    for n, at in row_blocks(cot):
        gate_lin, up_lin = gate_ref[at], up_ref[at]
        d_hidden = jnp.dot(merged(cot[n]), wd[...], preferred_element_type=F32)
        s = jax.nn.sigmoid(gate_lin)
        silu = gate_lin * s
        hidden[at] = (silu * up_lin).astype(BF)
        gate_low[at] = (d_hidden * up_lin * s * (1.0 + gate_lin * (1.0 - s))).astype(BF)
        up_low[at] = (d_hidden * silu).astype(BF)
        total = times_t(gate_low[at], wg[...]) + times_t(up_low[at], wu[...])
        part[n] = total.astype(BF).reshape((2,) + part.shape[1:])

    def grad_rows(n, total):
        at = pl.ds(n * size, size)
        back, gains = norm_back(middle[at], total, second_gain[...])
        mine[16:32] = mine[16:32] + gains.reshape(16, 128)
        rows = c_ref[0, at].astype(F32) + back
        mid[at] = rows
        mix[z, y, x, at] = rows.astype(BF)

    def out_rows(n, total):
        at = pl.ds(n * size, size)
        out[0, at] = (middle[at] + total).astype(BF)

    def outer(dst, rows, cols, giver, p):
        width = 512

        def piece(start):
            def run():
                at = pl.ds(start, width)
                dst[at] = outer_sum(merged(rows[:, :, :, :, at]), cols[...]).astype(BF)

            return run

        return [piece(start) for start in range(0, rows.shape[4], width)] + [
            lambda: giver.swap(p).start()
        ]

    def glu_block(n, at):
        def run():
            rows = times_t(hidden[at], wd[...]).astype(BF)
            glu_part[n] = rows.reshape((2,) + glu_part.shape[1:])

        return run

    returns = outer(gg, second, gate_low, units_out, 1) + units_out.jobs(0)
    returns += outer(gu, second, up_low, units_out, 2) + units_out.jobs(1) + units_out.jobs(2)
    outward = [glu_block(n, at) for n, at in row_blocks(glu_part)]
    outward += scatter_jobs(scatters[3], AHEAD[4], out_rows)
    plan = Plan((returns, *TIMES[3]), (outward, *TIMES[4]))
    plan.during(
        turn_jobs(
            scatters[1], gathers[3], AHEAD[3], grad_rows, outer(gd, cot, hidden, units_out, 0)
        )
    )
    gathers[3].finish()

    kept = plan.left(0), plan.left(1)
    plan = Plan((outer(go, mix, head, mixer_out, 0), 0, 2), (kept[0], 0, PACE[0]), (kept[1], 0, 1))
    for n, at in row_blocks(mix):
        d_head[at] = jnp.dot(merged(mix[n]), wo[...], preferred_element_type=F32)
        plan.step(0)
    group, gap = mix_backward(
        blocks, mixed, states, cum, d_head, d_lin, d_mixed, backs, (b_out, b_in, bs, br),
        lambda: plan.step(0),
    )
    mine[32:33] = group
    mine[40:41] = gap
    for n, at in row_blocks(part):
        part[n] = times_t(d_lin[at], wqfi[...]).astype(BF).reshape((2,) + part.shape[1:])

    def in_rows(n, total):
        at = pl.ds(n * size, size)
        back, gains = norm_back(entry[at], total, first_gain[...])
        in_grad[0, at] = mid[at] + back
        mine[0:16] = mine[0:16] + gains.reshape(16, 128)
        if n == PIECES - 1:
            swap = to_core(mine, theirs, vs, vr)
            swap.start()
            swap.wait()
            chips[h] = mine[...] + theirs[...]
            for k in range(1, H):
                to_chip(chips.at[h], chips.at[h], ws, wr, lax.rem(h + k, H)).start()

    for job in plan.left(0):
        job()
    kept = plan.left(1), plan.left(2)
    plan = Plan(
        (kept[0], 0, PACE[1]), (mixer_out.jobs(0) + mixer_out.jobs(1), *TIMES[5]), (kept[1], 0, 1)
    )
    plan.during(
        scatter_jobs(
            scatters[2], AHEAD[5], in_rows, outer(gqfi, first, d_lin, mixer_out, 1)
        )
    )
    plan.rest()
    others = chips.at[0 : H - 1]
    to_chip(others, others, ws, wr, h).wait()
    acc = chips[0, 0:40]
    for chip in range(1, H):
        acc = acc + chips[chip, 0:40]
    totals[0:40] = acc
    for chip in range(H):
        totals[40 + chip : 41 + chip] = chips[chip, 40:41]
    scatters[2].finish()
    scatters[3].finish()
    units_out.finish()
    mixer_out.finish()


def layer(inputs, cotangent, lengths, first_gain, second_gain, group_gain, gap_log, weights):
    _, rows, cols = inputs.shape
    depth, units = weights[-1].shape
    extent, count = H * rows, 2 * H * depth
    tiles = units // 128
    wide = -(-tiles // H) * 128
    home = lambda width: jax.ShapeDtypeStruct((depth, width), BF)
    full = VMEM((4, 2, 2, rows, cols), BF)
    local = VMEM((rows, cols), F32)
    tile = VMEM((extent, SPAN), F32)
    square = VMEM((SPAN, SPAN), F32)
    squares = VMEM((extent // SPAN, SPAN, SPAN), F32)
    widths = (384, 128, wide, wide, wide)
    return pl.pallas_call(
        functools.partial(layer_kernel, tiles),
        out_shape=[
            jax.ShapeDtypeStruct((1, rows, cols), BF),
            jax.ShapeDtypeStruct((1, rows, cols), F32),
            jax.ShapeDtypeStruct((56, 128), F32),
        ]
        + [home(cols)] * 4
        + [home(units)] * 3,
        in_specs=[VSPEC] * 2 + [SSPEC] + [VSPEC] * 4 + [ASPEC] * 7,
        out_specs=[VSPEC] * 3 + [ASPEC] * 7,
        scratch_shapes=[full] * 6
        + [VMEM((count, width), BF) for width in widths]
        + [local, local, local, VMEM((extent, SPAN), jnp.int32)]
        + [VMEM((8 * (extent // SPAN) + 8, SPAN), jnp.int32), VMEM((1, SPAN), F32)]
        + [VMEM((extent, 384), F32), tile, squares, VMEM((extent, SPAN), BF), tile]
        + [tile, VMEM((extent, 384), BF), tile, squares]
        + [VMEM((extent, wide), BF)] * 3
        + [VMEM((extent, wide), F32)] * 2
        + [VMEM((count, width), BF) for width in widths]
        + [VMEM((count // 2, width), BF) for width in widths]
        + scatter_bufs(rows, cols)
        + scatter_bufs(rows, cols)
        + gather_sems() * 4
        + scatter_sems() * 4
        + [square] * 4
        + [DMA] * 5
        + [VMEM((48, 128), F32), VMEM((48, 128), F32), VMEM((H, 48, 128), F32)]
        + [DMA, DMA, DMA, DMA]
        + bulk_sems(4)
        + bulk_sems(3)
        + bulk_sems(3)
        + bulk_sems(4),
        compiler_params=comm_params(1),
    )(
        inputs,
        cotangent,
        lengths,
        first_gain[None],
        second_gain[None],
        group_gain[None],
        gap_log.reshape(H, SPAN),
        *weights,
    )


def product(left, right, at_left, at_right):
    return lax.dot_general(
        left, right, (((at_left,), (at_right,)), ((), ())), preferred_element_type=F32
    )


def halves(rows):
    high = rows.astype(BF)
    return high, (rows - high.astype(F32)).astype(BF)


def mm(left, right, at_left, at_right):
    left_high, left_low = halves(left)
    right_high, right_low = halves(right)
    small = product(left_high, right_low, at_left, at_right)
    small = small + product(left_low, right_high, at_left, at_right)
    return product(left_high, right_high, at_left, at_right) + small


def tri_sum(rows, reverse=False):
    r = lax.broadcasted_iota(jnp.int32, (SPAN, SPAN), 0)
    c = lax.broadcasted_iota(jnp.int32, (SPAN, SPAN), 1)
    picked = jnp.where((r <= c) if reverse else (r >= c), 1.0, 0.0).astype(BF)
    high = rows.astype(BF)
    rest = rows - high.astype(F32)
    middle, low = halves(rest)
    return product(picked, high, 1, 0) + product(picked, middle, 1, 0) + product(picked, low, 1, 0)


def span_gates(lin_ref, gap_ref, at):
    q_lin, f_lin, values = lin_ref[at, 0:128], lin_ref[at, 128:256], lin_ref[at, 256:384]
    s = jax.nn.sigmoid(q_lin)
    key = jnp.exp(gap_ref[...]) * jax.nn.sigmoid(-f_lin)
    return q_lin, f_lin, values, s, key


def span_masks(dcol_ref, drow_ref, c, at):
    r = lax.broadcasted_iota(jnp.int32, (SPAN, SPAN), 0)
    k = lax.broadcasted_iota(jnp.int32, (SPAN, SPAN), 1)
    dcol, drow = dcol_ref[at], drow_ref[8 * c : 8 * c + 1]
    last = (c + 1) * SPAN - 1
    end = dcol_ref[last : last + 1]
    if c:
        before = dcol_ref[c * SPAN - 1 : c * SPAN]
    else:
        count = drow_ref.shape[0]
        before = drow_ref[count - 8 : count - 7]
    same = jnp.where(jnp.logical_and(dcol == drow, r >= k), 1.0, 0.0)
    carried = jnp.where(dcol == before, 1.0, 0.0)
    keep = jnp.where(dcol == end, 1.0, 0.0)
    whole = jnp.where(end == before, 1.0, 0.0)
    return same, carried, keep, whole


def spans(extent):
    return [(c, pl.ds(c * SPAN, SPAN)) for c in range(extent // SPAN)]


def mix_forward(blocks, mixed_ref, states_ref, head_ref, cum_ref, handover, between):
    out_ref, in_ref, send, recv = handover
    lin_ref, gap_ref, gain_ref, dcol_ref, drow_ref = blocks
    steps = spans(lin_ref.shape[0])
    state = jnp.zeros((SPAN, SPAN), F32)
    for c, at in steps:
        q_lin, f_lin, values, s, key = span_gates(lin_ref, gap_ref, at)
        same, carried, keep, whole = span_masks(dcol_ref, drow_ref, c, at)
        cum = tri_sum(jnp.log1p(-key))
        cum_ref[at] = cum
        end = cum[SPAN - 1 : SPAN]
        fresh = mm(values, jnp.exp(end - cum) * key * keep, 0, 0)
        states_ref[c] = fresh
        state = state * (jnp.exp(end) * whole) + fresh
    out_ref[...] = state
    copy = to_core(out_ref, in_ref, send, recv)
    copy.start()
    between()
    copy.wait()
    state = in_ref[...] * lax.axis_index("seq").astype(F32)
    for c, at in steps:
        q_lin, f_lin, values, s, key = span_gates(lin_ref, gap_ref, at)
        same, carried, keep, whole = span_masks(dcol_ref, drow_ref, c, at)
        cum = cum_ref[at]
        end = cum[SPAN - 1 : SPAN]
        fresh = states_ref[c]
        states_ref[c] = state
        decayed = q_lin * s * jnp.exp(cum)
        scores = mm(decayed, key * jnp.exp(-cum), 1, 1) * same
        mixed = mm(scores, values, 1, 0) + carried * mm(decayed, state, 1, 1)
        mixed_ref[at] = mixed
        head_ref[at] = (mixed * row_norm(mixed) * gain_ref[...]).astype(BF)
        state = state * (jnp.exp(end) * whole) + fresh
        if c % 2:
            between()


def mix_backward(
    blocks, mixed_ref, states_ref, cum_ref, dhead_ref, dlin_ref, do_ref, back_ref, handover, between
):
    out_ref, in_ref, send, recv = handover
    lin_ref, gap_ref, gain_ref, dcol_ref, drow_ref = blocks
    steps = spans(lin_ref.shape[0])
    group = jnp.zeros((1, SPAN), F32)
    adjoint = jnp.zeros((SPAN, SPAN), F32)
    for c, at in reversed(steps):
        d_mixed, gains = norm_back(mixed_ref[at], dhead_ref[at], gain_ref[...])
        group = group + gains
        do_ref[at] = d_mixed
        q_lin, f_lin, values, s, key = span_gates(lin_ref, gap_ref, at)
        same, carried, keep, whole = span_masks(dcol_ref, drow_ref, c, at)
        cum = cum_ref[at]
        back = mm(d_mixed, carried * (q_lin * s * jnp.exp(cum)), 0, 0)
        back_ref[c] = back
        adjoint = adjoint * (jnp.exp(cum[SPAN - 1 : SPAN]) * whole) + back
    out_ref[...] = adjoint
    copy = to_core(out_ref, in_ref, send, recv)
    copy.start()
    between()
    copy.wait()
    adjoint = in_ref[...] * (1 - lax.axis_index("seq")).astype(F32)
    gap = jnp.zeros((1, SPAN), F32)
    for c, at in reversed(steps):
        q_lin, f_lin, values, s, key = span_gates(lin_ref, gap_ref, at)
        same, carried, keep, whole = span_masks(dcol_ref, drow_ref, c, at)
        cum, d_mixed, state = cum_ref[at], do_ref[at], states_ref[c]
        grow, shrink = jnp.exp(-cum), jnp.exp(cum)
        end = cum[SPAN - 1 : SPAN]
        decayed, grown = q_lin * s * shrink, key * grow
        rest = jnp.exp(end - cum) * keep
        tail, through = rest * key, jnp.exp(end) * whole
        scores = mm(decayed, grown, 1, 1) * same
        d_scores = mm(d_mixed, values, 1, 1) * same
        d_values = mm(scores, d_mixed, 0, 0) + mm(tail, adjoint, 1, 1)
        d_decayed = mm(d_scores, grown, 1, 0) + carried * mm(d_mixed, state, 1, 0)
        d_grown = mm(d_scores, decayed, 0, 0)
        d_tail = mm(values, adjoint, 1, 0)
        held = tail * d_tail
        d_cum = decayed * d_decayed - grown * d_grown - held
        d_end = jnp.sum(held, axis=0, keepdims=True) + through * jnp.sum(
            state * adjoint, axis=0, keepdims=True
        )
        d_log = tri_sum(d_cum, reverse=True) + d_end
        d_key = d_grown * grow + d_tail * rest - d_log / (1.0 - key)
        scaled = d_key * key
        gap = gap + jnp.sum(scaled, axis=0, keepdims=True)
        dlin_ref[at, 0:128] = (d_decayed * shrink * s * (1.0 + q_lin * (1.0 - s))).astype(BF)
        dlin_ref[at, 128:256] = (-scaled * jax.nn.sigmoid(f_lin)).astype(BF)
        dlin_ref[at, 256:384] = d_values.astype(BF)
        adjoint = adjoint * through + back_ref[c]
        if c % 2:
            between()
    return group, gap


def finish_kernel(out_ref, in_ref, totals_ref, *refs):
    out, in_grad, first, second, group, gap = refs[7:13]
    out[...] = out_ref[...]
    in_grad[...] = in_ref[...]
    first[...] = totals_ref[0:16]
    second[...] = totals_ref[16:32]
    group[...] = totals_ref[32:33]
    gap[...] = totals_ref[40:56]
    for src, dst in zip(refs[:7], refs[13:]):
        dst[...] = src[...].astype(F32)


def finish(output, input_grad, totals, grads):
    depth = grads[0].shape[0]
    rows, cols = output.shape[1:]
    steps = 4
    piece = depth // steps
    local = pl.BlockSpec((1, piece, cols), lambda n: (0, jnp.minimum(n, rows // piece - 1), 0))
    whole = lambda height: pl.BlockSpec((height, 128), lambda n: (0, 0))
    grad = [pl.BlockSpec((piece, g.shape[1]), lambda n: (n, 0)) for g in grads]
    vector = lambda height: jax.ShapeDtypeStruct((height, 128), F32)
    return pl.pallas_call(
        finish_kernel,
        grid=(steps,),
        out_shape=[
            jax.ShapeDtypeStruct(output.shape, BF),
            jax.ShapeDtypeStruct(input_grad.shape, F32),
            vector(16),
            vector(16),
            vector(1),
            vector(16),
        ]
        + [jax.ShapeDtypeStruct(g.shape, F32) for g in grads],
        in_specs=[local, local, whole(56)] + grad,
        out_specs=[local, local, whole(16), whole(16), whole(1), whole(16)] + grad,
        compiler_params=pltpu.CompilerParams(vmem_limit_bytes=62 << 20),
    )(output, input_grad, totals, *grads)


def fast_body(
    inputs,
    cotangent,
    lengths,
    first_gain,
    q_weight,
    f_weight,
    i_weight,
    o_weight,
    group_gain,
    gap_log,
    second_gain,
    gate_weight,
    up_weight,
    down_weight,
):
    model = inputs.shape[2]
    output, input_grad, totals, *grads = layer(
        inputs,
        cotangent,
        lengths,
        first_gain,
        second_gain,
        group_gain,
        gap_log,
        (q_weight, f_weight, i_weight, o_weight, gate_weight, up_weight, down_weight),
    )
    output, input_grad, first_grad, second_grad, group_grad, gap_grad, *grads = finish(
        output, input_grad, totals, grads
    )
    q_grad, f_grad, i_grad, o_grad, gate_grad, up_grad, down_grad = grads
    return (
        output,
        input_grad,
        first_grad.reshape(model),
        q_grad,
        f_grad,
        i_grad,
        o_grad,
        group_grad.reshape(SPAN),
        gap_grad.reshape(model),
        second_grad.reshape(model),
        gate_grad,
        up_grad,
        down_grad,
    )


def solution(mesh):
    placed = (
        P("seq", "hid", None),
        P("seq", "hid", None),
        P(),
        P(),
        P(("seq", "hid"), None),
        P(("seq", "hid"), None),
        P(("seq", "hid"), None),
        P(("seq", "hid"), None),
        P(),
        P(),
        P(),
        P(("seq", "hid"), None),
        P(("seq", "hid"), None),
        P(("seq", "hid"), None),
    )
    body = fast_body if mesh.shape["hid"] == H else wide_body
    return jax.shard_map(
        body,
        mesh=mesh,
        in_specs=placed,
        out_specs=(
            P("seq", "hid", None),
            P("seq", "hid", None),
            P(),
            P(("seq", "hid"), None),
            P(("seq", "hid"), None),
            P(("seq", "hid"), None),
            P(("seq", "hid"), None),
            P(),
            P(),
            P(),
            P(("seq", "hid"), None),
            P(("seq", "hid"), None),
            P(("seq", "hid"), None),
        ),
        check_vma=False,
    )
```

```python
import functools

import jax
import jax.numpy as jnp
from jax import lax
from jax.experimental import pallas as pl
from jax.experimental.pallas import tpu as pltpu
from jax.sharding import PartitionSpec as P

H = 16
SPAN = 128


EPS = 1e-06
HIGH_PRECISION = lax.Precision.HIGHEST


def from_behind(block, axis, distance):
    devices = range(lax.axis_size(axis))
    route = [(i - distance, i) for i in devices if i - distance in devices]
    return lax.ppermute(block, axis, route)


def normed(entries, gain_vec):
    factor = lax.rsqrt(jnp.mean(entries * entries, axis=-1, keepdims=True) + EPS)
    return entries * factor * gain_vec


def gates(q_part, f_part, gap_piece):
    key_gate = jnp.exp(gap_piece) * jax.nn.sigmoid(-f_part)
    return (jax.nn.silu(q_part), key_gate, jnp.log1p(-key_gate))


def doc_starts(lengths):
    count = lengths.shape[0]
    earlier = lax.broadcasted_iota(jnp.int32, (count, count), 0) > lax.broadcasted_iota(
        jnp.int32, (count, count), 1
    )
    return jnp.sum(jnp.where(earlier, lengths[None, :], 0), axis=1)


def running_sum(rows):
    extent = rows.shape[-2]
    lower = (
        lax.broadcasted_iota(jnp.int32, (extent, extent), 0)
        >= lax.broadcasted_iota(jnp.int32, (extent, extent), 1)
    ).astype(jnp.float32)
    return jnp.einsum("ts,...sk->...tk", lower, rows, precision=HIGH_PRECISION)


def doc_ids(lengths, positions):
    starts = doc_starts(lengths)
    covered = (starts[None, :] <= positions[:, None]).astype(jnp.int32)
    return jnp.sum(covered, axis=1) - 1


def span_step(memory_state, pieces):
    queries, key_gate, value_rows, log_decay, documents, before = pieces
    cumulative = running_sum(log_decay)
    query_decayed = queries * jnp.exp(cumulative)
    k_grown = key_gate * jnp.exp(-cumulative)
    extent = documents.shape[0]
    row_ids = lax.broadcasted_iota(jnp.int32, (extent, extent), 0)
    col_ids = lax.broadcasted_iota(jnp.int32, (extent, extent), 1)
    same_doc = jnp.logical_and(documents[:, None] == documents[None, :], row_ids >= col_ids).astype(
        jnp.float32
    )
    scores = (
        jnp.einsum("hck,hsk->hcs", query_decayed, k_grown, precision=HIGH_PRECISION)
        * same_doc[None]
    )
    within_block = jnp.einsum("hcs,hsv->hcv", scores, value_rows, precision=HIGH_PRECISION)
    carried_state = (documents == before).astype(jnp.float32)[None, :, None]
    output_rows = within_block + carried_state * jnp.einsum(
        "awn,ani->awi", query_decayed, memory_state, precision=HIGH_PRECISION
    )
    last_cum = cumulative[:, -1:, :]
    keep_mask = (documents == documents[-1]).astype(jnp.float32)[None, :, None]
    tail_key_rows = jnp.exp(last_cum - cumulative) * key_gate * keep_mask
    whole_block = (documents[-1] == before).astype(jnp.float32)
    fresh_state = jnp.einsum("wfx,wfg->wxg", tail_key_rows, value_rows, precision=HIGH_PRECISION)
    memory_state = jnp.exp(last_cum[:, 0, :])[:, :, None] * whole_block * memory_state + fresh_state
    return (memory_state, output_rows)


def recur(queries, key_gate, value_rows, log_decay, documents, before, memory_state):
    head_count, extent, columns = queries.shape
    span_count = extent // SPAN

    def by_span(tensor):
        return jnp.swapaxes(tensor.reshape(head_count, span_count, SPAN, tensor.shape[-1]), 0, 1)

    doc_rows = documents.reshape(span_count, SPAN)
    befores = jnp.concatenate([jnp.reshape(before, (1,)), doc_rows[:-1, -1]])
    memory_state, span_out = lax.scan(
        jax.checkpoint(span_step),
        memory_state,
        (
            by_span(queries),
            by_span(key_gate),
            by_span(value_rows),
            by_span(log_decay),
            doc_rows,
            befores,
        ),
    )
    return (
        jnp.swapaxes(span_out, 0, 1).reshape(head_count, extent, value_rows.shape[-1]),
        memory_state,
    )


def spread_cols(weight, copies):
    row_count = weight.shape[0]
    shaped = weight.reshape(row_count, 1, H, weight.shape[1] // H)
    return jnp.broadcast_to(shaped, (row_count, copies, H, shaped.shape[3])).reshape(
        row_count, copies * weight.shape[1]
    )


def fold_copies(received, copies):
    row_count = received.shape[0]
    return jnp.sum(received.reshape(row_count, copies, received.shape[1] // copies), axis=1)


def fan_rows(local_rows):
    blocks_here, row_count, columns = local_rows.shape
    return jnp.broadcast_to(local_rows[:, None], (blocks_here, H, row_count, columns)).reshape(
        blocks_here * H * row_count, columns
    )


def sum_heads(received, blocks_here):
    total_rows, columns = received.shape
    return jnp.sum(
        received.reshape(blocks_here, H, total_rows // (blocks_here * H), columns), axis=1
    )


def times_t(left_mat, right_mat):
    return lax.dot_general(
        left_mat, right_mat, (((1,), (1,)), ((), ())), preferred_element_type=jnp.float32
    )


def outer_sum(left_mat, right_mat):
    return lax.dot_general(
        left_mat, right_mat, (((0,), (0,)), ((), ())), preferred_element_type=jnp.float32
    )


def outer_high(left_mat, right_mat):
    return lax.dot_general(
        left_mat,
        right_mat,
        (((0,), (0,)), ((), ())),
        precision=HIGH_PRECISION,
        preferred_element_type=jnp.float32,
    )


def wide_body(
    inputs,
    cotangent,
    lengths,
    first_gain,
    q_weight,
    f_weight,
    i_weight,
    o_weight,
    group_gain,
    gap_log,
    second_gain,
    gate_weight,
    up_weight,
    down_weight,
):
    hid_size = lax.axis_size("hid")
    per_seq = hid_size // H
    block_total = lax.axis_size("seq") * per_seq
    hid_place = lax.axis_index("hid")
    head_id = hid_place % H
    block_id = lax.axis_index("seq") * per_seq + hid_place // H
    model = inputs.shape[2]
    head_width = model // H
    block_len = hid_size * inputs.shape[1]
    entries = inputs.astype(jnp.float32)
    q_block, f_block, i_block, o_block, gate_block, up_block, down_block = (
        lax.all_to_all(
            spread_cols(q_weight, block_total),
            ("seq", "hid"),
            split_axis=1,
            concat_axis=0,
            tiled=True,
        ),
        lax.all_to_all(
            spread_cols(f_weight, block_total),
            ("seq", "hid"),
            split_axis=1,
            concat_axis=0,
            tiled=True,
        ),
        lax.all_to_all(
            spread_cols(i_weight, block_total),
            ("seq", "hid"),
            split_axis=1,
            concat_axis=0,
            tiled=True,
        ),
        lax.all_to_all(
            spread_cols(o_weight, block_total),
            ("seq", "hid"),
            split_axis=1,
            concat_axis=0,
            tiled=True,
        ),
        lax.all_to_all(
            spread_cols(gate_weight, block_total),
            ("seq", "hid"),
            split_axis=1,
            concat_axis=0,
            tiled=True,
        ),
        lax.all_to_all(
            spread_cols(up_weight, block_total),
            ("seq", "hid"),
            split_axis=1,
            concat_axis=0,
            tiled=True,
        ),
        lax.all_to_all(
            spread_cols(down_weight, block_total),
            ("seq", "hid"),
            split_axis=1,
            concat_axis=0,
            tiled=True,
        ),
    )
    positions = block_id * block_len + lax.iota(jnp.int32, block_len)
    documents = doc_ids(lengths, positions)
    before = doc_ids(lengths, jnp.reshape(block_id * block_len - 1, (1,)))[0]
    first_norm, first_back = jax.vjp(normed, entries, first_gain)
    first_low = first_norm.astype(jnp.bfloat16)
    first_rows = lax.all_to_all(fan_rows(first_low), "hid", split_axis=0, concat_axis=0, tiled=True)
    q_lin = jnp.dot(first_rows, q_block, preferred_element_type=jnp.float32)
    f_lin = jnp.dot(first_rows, f_block, preferred_element_type=jnp.float32)
    i_lin = jnp.dot(first_rows, i_block, preferred_element_type=jnp.float32)
    gap_part = lax.dynamic_slice_in_dim(gap_log, head_id * head_width, head_width)
    queries, key_gate, log_decay = gates(q_lin, f_lin, gap_part)
    cumulative = running_sum(log_decay)
    last_cum = cumulative[-1]
    tail_key_rows = (
        jnp.exp(last_cum[None, :] - cumulative)
        * key_gate
        * (documents == documents[-1]).astype(jnp.float32)[:, None]
    )
    local_state = outer_high(tail_key_rows, i_lin)
    decay = jnp.exp(last_cum) * (documents[-1] == before).astype(jnp.float32)
    state_in = jnp.zeros_like(local_state)
    for number in range(block_total - 1):
        state_out = decay[:, None] * state_in + local_state
        state_in = from_behind(state_out.astype(jnp.bfloat16), ("seq", "hid"), H).astype(
            state_out.dtype
        )

    def core(q_part, f_part, i_part, gap_piece):
        queries_in, keys_in, logs_in = gates(q_part, f_part, gap_piece)
        mixed_all, memory_state = recur(
            queries_in[None],
            keys_in[None],
            i_part[None],
            logs_in[None],
            documents,
            before,
            state_in[None],
        )
        return (mixed_all[0], memory_state[0])

    (mixed_out, _), core_back = jax.vjp(core, q_lin, f_lin, i_lin, gap_part)
    head_normed, norm_back = jax.vjp(normed, mixed_out, group_gain)
    head_low = head_normed.astype(jnp.bfloat16)
    mix_out = sum_heads(
        lax.all_to_all(
            times_t(head_low, o_block).astype(jnp.bfloat16),
            "hid",
            split_axis=0,
            concat_axis=0,
            tiled=True,
        ).astype(jnp.float32),
        per_seq,
    )
    middle = entries + mix_out
    second_norm, second_back = jax.vjp(normed, middle, second_gain)
    second_low = second_norm.astype(jnp.bfloat16)
    second_rows, cot_rows = (
        lax.all_to_all(fan_rows(second_low), "hid", split_axis=0, concat_axis=0, tiled=True),
        lax.all_to_all(fan_rows(cotangent), "hid", split_axis=0, concat_axis=0, tiled=True),
    )
    gate_lin = jnp.dot(second_rows, gate_block, preferred_element_type=jnp.float32)
    up_lin = jnp.dot(second_rows, up_block, preferred_element_type=jnp.float32)
    hidden = (jax.nn.silu(gate_lin) * up_lin).astype(jnp.bfloat16)
    glu_out = sum_heads(
        lax.all_to_all(
            times_t(hidden, down_block).astype(jnp.bfloat16),
            "hid",
            split_axis=0,
            concat_axis=0,
            tiled=True,
        ).astype(jnp.float32),
        per_seq,
    )
    output = (middle + glu_out).astype(jnp.bfloat16)
    down_part = outer_sum(cot_rows, hidden)
    hidden_grad = jnp.dot(cot_rows, down_block, preferred_element_type=jnp.float32)
    gate_sig = jax.nn.sigmoid(gate_lin)
    gate_low = (hidden_grad * up_lin * gate_sig * (1.0 + gate_lin * (1.0 - gate_sig))).astype(
        jnp.bfloat16
    )
    up_low = (hidden_grad * gate_lin * gate_sig).astype(jnp.bfloat16)
    gate_part = outer_sum(second_rows, gate_low)
    up_part = outer_sum(second_rows, up_low)
    second_sum = lax.all_to_all(
        (times_t(gate_low, gate_block) + times_t(up_low, up_block)).astype(jnp.bfloat16),
        "hid",
        split_axis=0,
        concat_axis=0,
        tiled=True,
    ).astype(jnp.float32)
    middle_part, second_part = second_back(sum_heads(second_sum, per_seq))
    middle_grad = cotangent.astype(jnp.float32) + middle_part
    mix_grad = middle_grad.astype(jnp.bfloat16)
    mix_rows = lax.all_to_all(fan_rows(mix_grad), "hid", split_axis=0, concat_axis=0, tiled=True)
    normed_grad = jnp.dot(mix_rows, o_block, preferred_element_type=jnp.float32)
    o_part = outer_sum(mix_rows, head_low)
    mixed_grad, group_part = norm_back(normed_grad)
    carried_state = (documents == before).astype(jnp.float32)[:, None]
    grad_local = outer_high(queries * jnp.exp(cumulative) * carried_state, mixed_grad)
    state_grad = jnp.zeros_like(grad_local)
    for number in range(block_total - 1):
        grad_in = decay[:, None] * state_grad + grad_local
        state_grad = from_behind(grad_in.astype(jnp.bfloat16), ("seq", "hid"), -H).astype(
            grad_in.dtype
        )
    q_grad_lin, f_grad_lin, i_grad_lin, gap_piece_grad = core_back((mixed_grad, state_grad))
    q_low = q_grad_lin.astype(jnp.bfloat16)
    f_low = f_grad_lin.astype(jnp.bfloat16)
    i_low = i_grad_lin.astype(jnp.bfloat16)
    q_part = outer_sum(first_rows, q_low)
    f_part = outer_sum(first_rows, f_low)
    i_part = outer_sum(first_rows, i_low)
    first_sum = lax.all_to_all(
        (times_t(q_low, q_block) + times_t(f_low, f_block) + times_t(i_low, i_block)).astype(
            jnp.bfloat16
        ),
        "hid",
        split_axis=0,
        concat_axis=0,
        tiled=True,
    ).astype(jnp.float32)
    entry_part, first_part = first_back(sum_heads(first_sum, per_seq))
    input_grad = middle_grad + entry_part
    q_back, f_back, i_back, o_back, gate_back, up_back, down_back = (
        lax.all_to_all(
            q_part.astype(jnp.bfloat16), ("seq", "hid"), split_axis=0, concat_axis=1, tiled=True
        ).astype(q_part.dtype),
        lax.all_to_all(
            f_part.astype(jnp.bfloat16), ("seq", "hid"), split_axis=0, concat_axis=1, tiled=True
        ).astype(f_part.dtype),
        lax.all_to_all(
            i_part.astype(jnp.bfloat16), ("seq", "hid"), split_axis=0, concat_axis=1, tiled=True
        ).astype(i_part.dtype),
        lax.all_to_all(
            o_part.astype(jnp.bfloat16), ("seq", "hid"), split_axis=0, concat_axis=1, tiled=True
        ).astype(o_part.dtype),
        lax.all_to_all(
            gate_part.astype(jnp.bfloat16), ("seq", "hid"), split_axis=0, concat_axis=1, tiled=True
        ).astype(gate_part.dtype),
        lax.all_to_all(
            up_part.astype(jnp.bfloat16), ("seq", "hid"), split_axis=0, concat_axis=1, tiled=True
        ).astype(up_part.dtype),
        lax.all_to_all(
            down_part.astype(jnp.bfloat16), ("seq", "hid"), split_axis=0, concat_axis=1, tiled=True
        ).astype(down_part.dtype),
    )
    o_grad = fold_copies(o_back, block_total)
    head_pick = (lax.iota(jnp.int32, H) == head_id).astype(jnp.float32)
    gap_full = (head_pick[:, None] * gap_piece_grad[None, :]).reshape(model)
    first_grad, second_grad, group_grad, gap_grad = lax.psum(
        (first_part, second_part, group_part, gap_full), ("seq", "hid")
    )
    return (
        output,
        input_grad,
        first_grad,
        fold_copies(q_back, block_total),
        fold_copies(f_back, block_total),
        fold_copies(i_back, block_total),
        o_grad,
        group_grad,
        gap_grad,
        second_grad,
        fold_copies(gate_back, block_total),
        fold_copies(up_back, block_total),
        fold_copies(down_back, block_total),
    )


F32 = jnp.float32
BF = jnp.bfloat16
MESH = pl.DeviceIdType.MESH
DMA = pltpu.SemaphoreType.DMA
VMEM = pltpu.VMEM
PIECES = 3
PARTS = 4
CUTS = PIECES * PARTS
AHEAD = (4, 4, 3, 3, 4, 4)
PACE = (4, 8)
TIMES = ((4, 5), (-1, 1), (16, 6), (8, 2), (8, 1), (0, 8))
VSPEC = pl.BlockSpec(memory_space=pltpu.VMEM)
ASPEC = pl.BlockSpec(memory_space=pl.ANY)
SSPEC = pl.BlockSpec(memory_space=pltpu.SMEM)


def place():
    h = lax.axis_index("hid")
    return h, h // 4, lax.rem(h // 2, 2), lax.rem(h, 2)


def partners():
    h, z, y, x = place()
    column = [lax.rem(z + k, 4) * 4 + lax.rem(h, 4) for k in (1, 2, 3)]
    return column, h + 2 - 4 * y, h + 1 - 2 * x


def greet(chips, core=False):
    gate = pltpu.get_barrier_semaphore()
    for chip in chips:
        pl.semaphore_signal(gate, inc=1, device_id={"hid": chip}, device_id_type=MESH)
    if core:
        other = 1 - lax.axis_index("seq")
        pl.semaphore_signal(gate, inc=1, device_id={"seq": other}, device_id_type=MESH)
    pl.semaphore_wait(gate, len(chips) + int(core))


def to_chip(src, dst, send, recv, chip):
    return pltpu.make_async_remote_copy(
        src_ref=src,
        dst_ref=dst,
        send_sem=send,
        recv_sem=recv,
        device_id={"hid": chip},
        device_id_type=MESH,
    )


def to_core(src, dst, send, recv):
    return pltpu.make_async_remote_copy(
        src_ref=src,
        dst_ref=dst,
        send_sem=send,
        recv_sem=recv,
        device_id={"seq": 1 - lax.axis_index("seq")},
        device_id_type=MESH,
    )


def comm_params(collective_id):
    return pltpu.CompilerParams(
        collective_id=collective_id, has_side_effects=True, vmem_limit_bytes=62 << 20
    )


class Cuts:
    def cut(self, c):
        i, j = c // PARTS, c % PARTS
        rows, cols = self.ref.shape[3] // PIECES, self.ref.shape[4] // PARTS
        return pl.ds(i * rows, rows), pl.ds(j * cols, cols), j % 2


class Gather(Cuts):
    def __init__(self, ref, sems):
        self.ref = ref
        self.s1, self.s2, self.s3, self.r1, self.r2, self.r3 = sems

    def start(self, c):
        h, z, y, x = place()
        column, py, px = partners()
        a, b, j = self.cut(c)
        ref = self.ref.at[z, y, x, a, b]
        for k in range(3):
            to_chip(ref, ref, self.s1, self.r1.at[c], column[k]).start()

    def second(self, c):
        h, z, y, x = place()
        column, py, px = partners()
        a, b, j = self.cut(c)
        three = self.ref.at[0:3, y, x, a, b]
        to_chip(three, three, self.s1, self.r1.at[c], px).wait_recv()
        ref = self.ref.at[:, y, x, a, b]
        to_chip(ref, ref, self.s2, self.r2.at[c], py if j else px).start()

    def third(self, c):
        h, z, y, x = place()
        column, py, px = partners()
        a, b, j = self.cut(c)
        got = self.ref.at[:, y, x, a, b]
        to_chip(got, got, self.s2, self.r2.at[c], px).wait_recv()
        ref = self.ref.at[:, :, x, a, b] if j else self.ref.at[:, y, :, a, b]
        to_chip(ref, ref, self.s3, self.r3, px if j else py).start()

    def finish(self):
        h, z, y, x = place()
        half, quarter, three = self.ref.at[:, 0], self.ref.at[:, 0, 0], self.ref.at[0:3, 0, 0]
        to_chip(half, half, self.s3, self.r3, x).wait_recv()
        for ref, sem in ((three, self.s1), (quarter, self.s2), (half, self.s3)):
            to_chip(ref, ref, sem, self.r3, x).wait_send()


def gather_sems():
    return [DMA, DMA, DMA, DMA((CUTS,)), DMA((CUTS,)), DMA]


class Scatter(Cuts):
    def __init__(self, ref, bufs, sems):
        self.ref, self.bufs = ref, bufs
        self.s1, self.s2, self.s3, self.r1, self.r2, self.r3 = sems

    def start(self, c):
        h, z, y, x = place()
        column, py, px = partners()
        a, b, j = self.cut(c)
        src = self.ref.at[:, :, 1 - x, a, b] if j else self.ref.at[:, 1 - y, :, a, b]
        to_chip(src, self.bufs[0].at[c], self.s1, self.r1.at[c], px if j else py).start()

    def second(self, c):
        h, z, y, x = place()
        column, py, px = partners()
        b1, t1, b2 = self.bufs[:3]
        a, b, j = self.cut(c)
        q = y if j else x
        to_chip(b1.at[c], b1.at[c], self.s1, self.r1.at[c], px).wait_recv()
        theirs = self.ref[:, 1 - q, x, a, b] if j else self.ref[:, y, 1 - q, a, b]
        b1[c, :, 1 - q] = (theirs.astype(F32) + b1[c, :, 1 - q].astype(F32)).astype(BF)
        to_chip(b1.at[c, :, 1 - q], b2.at[c], self.s2, self.r2.at[c], py if j else px).start()
        mine = self.ref[:, q, x, a, b] if j else self.ref[:, y, q, a, b]
        t1[c] = mine.astype(F32) + b1[c, :, q].astype(F32)

    def third(self, c):
        h, z, y, x = place()
        column, py, px = partners()
        b1, t1, b2, t2, b3 = self.bufs
        to_chip(b2.at[c], b2.at[c], self.s2, self.r2.at[c], px).wait_recv()
        t2[c] = t1[c, z] + b2[c, z].astype(F32)
        b2[c] = (t1[c] + b2[c].astype(F32)).astype(BF)
        for k in range(3):
            to_chip(
                b2.at[c, lax.rem(z + k + 1, 4)], b3.at[c, k], self.s3, self.r3.at[c], column[k]
            ).start()

    def last(self, c):
        h, z, y, x = place()
        b3, t2 = self.bufs[4], self.bufs[3]
        to_chip(b3.at[c], b3.at[c], self.s3, self.r3.at[c], x).wait_recv()
        return t2[c] + b3[c, 0].astype(F32) + b3[c, 1].astype(F32) + b3[c, 2].astype(F32)

    def finish(self):
        h, z, y, x = place()
        whole = self.bufs[0].at[:], self.bufs[2].at[:], self.bufs[4].at[:]
        for ref, sem in zip(whole, (self.s1, self.s2, self.s3)):
            to_chip(ref, ref, sem, self.r1.at[0], x).wait_send()


def scatter_bufs(rows, cols):
    n, r, w = CUTS, rows // PIECES, cols // PARTS
    return [
        VMEM((n, 4, 2, r, w), BF),
        VMEM((n, 4, r, w), F32),
        VMEM((n, 4, r, w), BF),
        VMEM((n, r, w), F32),
        VMEM((n, 3, r, w), BF),
    ]


def scatter_sems():
    return [DMA, DMA, DMA, DMA((CUTS,)), DMA((CUTS,)), DMA((CUTS,))]


def all_chips():
    h = lax.axis_index("hid")
    return [lax.rem(h + k, H) for k in range(1, H)]


class Plan:
    def __init__(self, *entries):
        self.entries = [[list(jobs), start, pace] for jobs, start, pace in entries]

    def step(self, t):
        for entry in self.entries:
            jobs, start, pace = entry
            if t >= start:
                for job in jobs[:pace]:
                    job()
                entry[0] = jobs[pace:]

    def rest(self):
        for entry in self.entries:
            for job in entry[0]:
                job()
            entry[0] = []

    def left(self, n):
        jobs, self.entries[n][0] = self.entries[n][0], []
        return jobs

    def during(self, jobs):
        for t, job in enumerate(jobs):
            job()
            self.step(t)


def unit_span(tiles, h):
    first = (tiles * h) // H
    return first, (tiles * (h + 1)) // H - first


def lanes(tile, count):
    return pl.ds(pl.multiple_of(tile * 128, 128), count * 128)


class Bulk:
    def __init__(self, items, tiles, depth, sems):
        self.items, self.tiles, self.depth = items, tiles, depth
        self.ss, self.rs, self.ls, self.xs, self.xr = sems
        self.least = tiles // H

    def sized(self, n, chip, act):
        if not self.items[n][3]:
            act(chip, 1)
            return
        first, count = unit_span(self.tiles, chip)
        if self.tiles % H == 0:
            act(first, self.least)
            return
        for number in (self.least, self.least + 1):
            pl.when(count == number)(functools.partial(act, first, number))

    def ours(self, view):
        half = H * self.depth
        return pl.ds(pl.multiple_of(view * half, half), half)

    def row(self, core, chip):
        return pl.ds(pl.multiple_of((core * H + chip) * self.depth, self.depth), self.depth)


class Fetch(Bulk):
    def copy(self, n, k, chip, first, count):
        h, b = lax.axis_index("hid"), lax.axis_index("seq")
        src, dst, at, _ = self.items[n]
        return to_chip(
            src.at[:, lanes(first, count)],
            dst.at[self.row(b, h), lanes(at, count)],
            self.ss.at[n],
            self.rs.at[n],
            chip,
        )

    def own(self, n, first, count):
        h, b = lax.axis_index("hid"), lax.axis_index("seq")
        src, dst, at, _ = self.items[n]
        return pltpu.make_async_copy(
            src.at[:, lanes(first, count)], dst.at[self.row(b, h), lanes(at, count)], self.ls.at[n]
        )

    def job(self, n, k):
        def run():
            chip = lax.rem(lax.axis_index("hid") + k, H)
            self.sized(
                n, chip, lambda first, count: self.copy(n, k, chip, first, count).start()
            )

        return run

    def jobs(self):
        return [self.job(n, k) for n in range(len(self.items)) for k in range(1, H)]

    def start_own(self):
        h = lax.axis_index("hid")
        for n, (_, dst, _, split) in enumerate(self.items):
            self.sized(n, h, lambda first, count: self.own(n, first, count).start())
            if split and self.tiles % H:

                @pl.when(unit_span(self.tiles, h)[1] == self.least)
                def _():
                    dst[:, self.least * 128 :] = jnp.zeros((dst.shape[0], 128), BF)

    def swap(self, n, tile, count, slot):
        b = lax.axis_index("seq")
        view = self.items[n][1].at[self.ours(b), lanes(tile, count)]
        return to_core(view, view, self.xs.at[n, slot], self.xr.at[n, slot])

    def each_swap(self, n, act):
        at, split = self.items[n][2:]
        act(self.swap(n, at, self.least if split else 1, 0))
        if split and self.tiles % H:

            @pl.when(unit_span(self.tiles, lax.axis_index("hid"))[1] > self.least)
            def _():
                act(self.swap(n, self.least, 1, 1))

    def arrive(self, n):
        h = lax.axis_index("hid")
        self.sized(n, h, lambda first, count: self.own(n, first, count).wait())
        self.sized(n, h, lambda first, count: self.rest(n, count).wait_recv())
        self.each_swap(n, lambda copy: copy.start())

    def settle(self, ns):
        for n in ns:
            self.each_swap(n, lambda copy: copy.wait())

    def finish(self):
        h = lax.axis_index("hid")
        for n in range(len(self.items)):
            self.sized(n, h, lambda first, count: self.rest(n, count).wait_send())

    def rest(self, n, count):
        src, dst, at, split = self.items[n]
        others = self.tiles - count if split else H - 1
        return to_chip(
            src.at[:, lanes(0, others)],
            dst.at[pl.ds(0, (H - 1) * self.depth), lanes(at, count)],
            self.ss.at[n],
            self.rs.at[n],
            lax.axis_index("hid"),
        )


class Return(Bulk):
    def __init__(self, items, parts, tiles, depth, sems):
        super().__init__(items, tiles, depth, sems)
        self.parts = parts

    def swap(self, p):
        part, total, _ = self.parts[p]
        return to_core(
            part.at[self.ours(1 - lax.axis_index("seq"))], total, self.xs.at[p, 0], self.xr.at[p, 0]
        )

    def add(self, p):
        def run():
            part, total, _ = self.parts[p]
            b = lax.axis_index("seq")
            self.swap(p).wait()
            half, step = total.shape[0], 128

            @pl.loop(0, half // step)
            def _(t):
                at = pl.ds(pl.multiple_of(t * step, step), step)
                own = pl.ds(pl.multiple_of(b * half + t * step, step), step)
                total[at] = (total[at].astype(F32) + part[own].astype(F32)).astype(BF)

            for n in self.parts[p][2]:
                h = lax.axis_index("hid")
                self.sized(n, h, lambda first, count: self.own(n, first, count).start())

        return run

    def copy(self, n, k, chip, first, count):
        dst, src, at, _ = self.items[n]
        return to_chip(
            src.at[self.row(0, chip), lanes(at, count)],
            dst.at[:, lanes(first, count)],
            self.ss.at[n],
            self.rs.at[n],
            chip,
        )

    def own(self, n, first, count):
        dst, src, at, _ = self.items[n]
        return pltpu.make_async_copy(
            src.at[self.row(0, lax.axis_index("hid")), lanes(at, count)],
            dst.at[:, lanes(first, count)],
            self.ls.at[n],
        )

    def job(self, n, k):
        def run():
            h = lax.axis_index("hid")
            chip = lax.rem(h + k, H)
            self.sized(n, h, lambda first, count: self.copy(n, k, chip, first, count).start())

        return run

    def jobs(self, p):
        return [self.add(p)] + [self.job(n, k) for n in self.parts[p][2] for k in range(1, H)]

    def finish(self):
        h = lax.axis_index("hid")
        for n in range(len(self.items)):
            self.sized(n, h, lambda first, count: self.own(n, first, count).wait())
            self.sized(n, h, lambda first, count: self.rest(n, count).wait())

    def rest(self, n, count):
        dst, src, at, split = self.items[n]
        others = self.tiles - count if split else H - 1
        return to_chip(
            src.at[pl.ds(0, (H - 1) * self.depth), lanes(at, count)],
            dst.at[:, lanes(0, others)],
            self.ss.at[n],
            self.rs.at[n],
            lax.axis_index("hid"),
        )


def bulk_sems(n):
    return [DMA((n,)), DMA((n,)), DMA((n,)), DMA((n, 2)), DMA((n, 2))]


def split_refs(refs, *counts):
    groups, at = [], 0
    for count in counts:
        groups.append(refs[at : at + count])
        at += count
    assert at == len(refs)
    return groups


def row_norm(rows):
    return lax.rsqrt(jnp.mean(rows * rows, axis=-1, keepdims=True) + EPS)


def gather_jobs(gather, ahead):
    lag = PARTS

    def step(t):
        def run():
            if t == 0:
                for c in range(ahead):
                    gather.start(c)
            if t < CUTS:
                gather.second(t)
                if t + ahead < CUTS:
                    gather.start(t + ahead)
            if t >= lag:
                gather.third(t - lag)

        return run

    return [step(t) for t in range(CUTS + lag)]


def scatter_jobs(scatter, ahead, rows_done, meanwhile=()):
    lag, held = PARTS, []

    def step(t):
        def run():
            if t == 0:
                for c in range(ahead):
                    scatter.start(c)
                for job in meanwhile:
                    job()
            if t < CUTS:
                scatter.second(t)
                if t + ahead < CUTS:
                    scatter.start(t + ahead)
            if 0 <= t - lag // 2 < CUTS:
                scatter.third(t - lag // 2)
            c = t - lag - lag // 2
            if c >= 0:
                held.append(scatter.last(c))
                if len(held) == PARTS:
                    rows_done(c // PARTS, jnp.concatenate(held, axis=1))
                    held.clear()

        return run

    return [step(t) for t in range(CUTS + lag + lag // 2)]


def turn_jobs(scatter, gather, ahead, rows_done, meanwhile=()):
    lag = PARTS

    def write(i, rows):
        rows_done(i, rows)
        if i == PIECES - 1:
            scatter.finish()
        for c in range(i * PARTS, (i + 1) * PARTS):
            gather.start(c)

    first = scatter_jobs(scatter, ahead, write, meanwhile)

    def step(t):
        def run():
            if t < len(first):
                first[t]()
            c = t - 2 * lag - lag // 2 - (PARTS - 1)
            if 0 <= c < CUTS:
                gather.second(c)
            if 0 <= c - lag < CUTS:
                gather.third(c - lag)

        return run

    return [step(t) for t in range(CUTS + 3 * lag + lag // 2 + PARTS - 1)]


def norm_back(rows, grad, gain):
    factor = row_norm(rows)
    normal = rows * factor
    scaled = grad * gain
    back = factor * (scaled - normal * jnp.mean(scaled * normal, axis=-1, keepdims=True))
    return back, jnp.sum(grad * normal, axis=0, keepdims=True)


def row_blocks(ref):
    size = 2 * ref.shape[1] * ref.shape[2] * ref.shape[3]
    return [(pl.ds(2 * n, 2), pl.ds(n * size, size)) for n in range(ref.shape[0] // 2)]


def merged(rows):
    return rows.reshape(-1, rows.shape[-1])


def doc_tile(lengths_ref, start, shape, dim):
    positions = start + lax.broadcasted_iota(jnp.int32, shape, dim)
    documents = jnp.full(shape, -1, jnp.int32)
    begin = jnp.int32(0)
    for n in range(lengths_ref.shape[0]):
        documents = documents + jnp.where(positions >= begin, 1, 0)
        begin = begin + lengths_ref[n]
    return documents


def layer_kernel(tiles, *refs):
    (
        (x_ref, c_ref, lengths, first_gain, second_gain, gain_ref, gap_all),
        weights,
        (out, in_grad, totals, *homes),
        (first, cot, second, mix, part, glu_part),
        (wqfi, wo, wg, wu, wd),
        (entry, middle, mid, dcol, drow, gap_ref),
        (lin, mixed, states, head, cum, d_head, d_lin, d_mixed, backs),
        (hidden, gate_low, up_low, gate_ref, up_ref),
        (gqfi, go, gg, gu, gd),
        (tqfi, to, tg, tu, td),
        main_bufs,
        glu_bufs,
        gather_sets,
        scatter_sets,
        (f_out, f_in, b_out, b_in, fs, fr, bs, br, ls),
        (mine, theirs, chips, vs, vr, ws, wr),
        bulk_sets,
    ) = split_refs(refs, 7, 7, 10, 6, 5, 6, 9, 5, 5, 5, 5, 5, 24, 24, 9, 7, 20)
    q, f, i, o, g, u, d = weights
    hq, hf, hi, ho, hg, hu, hd = homes
    h, z, y, x = place()
    core = lax.axis_index("seq")
    depth, size = q.shape[0], x_ref.shape[1] // PIECES
    extent = lin.shape[0]
    mixer_in = Fetch(
        [(q, wqfi, 0, False), (f, wqfi, 1, False), (i, wqfi, 2, False), (o, wo, 0, False)],
        H,
        depth,
        bulk_sets[0:5],
    )
    units_in = Fetch(
        [(g, wg, 0, True), (u, wu, 0, True), (d, wd, 0, True)], tiles, depth, bulk_sets[5:10]
    )
    units_out = Return(
        [(hd, td, 0, True), (hg, tg, 0, True), (hu, tu, 0, True)],
        [(gd, td, (0,)), (gg, tg, (1,)), (gu, tu, (2,))],
        tiles,
        depth,
        bulk_sets[10:15],
    )
    mixer_out = Return(
        [(ho, to, 0, False), (hq, tqfi, 0, False), (hf, tqfi, 1, False), (hi, tqfi, 2, False)],
        [(go, to, (0,)), (gqfi, tqfi, (1, 2, 3))],
        H,
        depth,
        bulk_sets[15:20],
    )
    gathers = [
        Gather(ref, gather_sets[6 * n : 6 * n + 6])
        for n, ref in enumerate((first, cot, second, mix))
    ]
    scatters = [
        Scatter(ref, bufs, scatter_sets[6 * n : 6 * n + 6])
        for n, (ref, bufs) in enumerate(
            ((part, main_bufs), (part, main_bufs), (part, main_bufs), (glu_part, glu_bufs))
        )
    ]

    own = pltpu.make_async_copy(c_ref.at[0], cot.at[z, y, x], ls)
    own.start()
    mixer_in.start_own()
    for n in range(PIECES):
        at = pl.ds(n * size, size)
        rows = x_ref[0, at].astype(F32)
        entry[at] = rows
        first[z, y, x, at] = (rows * row_norm(rows) * first_gain[...]).astype(BF)
    greet(all_chips(), core=True)
    own.wait()

    def documents():
        gap_ref[...] = gap_all[pl.ds(h, 1)]
        base = core * extent
        for c, at in spans(extent):
            dcol[at] = doc_tile(lengths, base + c * SPAN, (SPAN, SPAN), 0)
            drow[8 * c : 8 * c + 8] = doc_tile(lengths, base + c * SPAN, (8, SPAN), 1)
        drow[8 * len(spans(extent)) :] = doc_tile(lengths, base - 1, (8, SPAN), 0)
        mine[...] = jnp.zeros_like(mine)
        units_in.start_own()

    mixer_jobs = mixer_in.jobs()
    plan = Plan(([documents], 0, 1), (mixer_jobs[: 3 * (H - 1)], *TIMES[0]))
    plan.during(gather_jobs(gathers[0], AHEAD[0]))
    plan.rest()
    for job in mixer_jobs[3 * (H - 1) :]:
        job()
    for n in range(3):
        mixer_in.arrive(n)
    gathers[0].finish()
    mixer_in.settle((0, 1, 2))
    plan = Plan((gather_jobs(gathers[1], AHEAD[1]), *TIMES[1]), (units_in.jobs(), *TIMES[2]))

    for n, at in row_blocks(first):
        lin[at] = jnp.dot(merged(first[n]), wqfi[...], preferred_element_type=F32)
        plan.step(-1)
    blocks = (lin, gap_ref, gain_ref, dcol, drow)
    mix_forward(blocks, mixed, states, head, cum, (f_out, f_in, fs, fr), lambda: plan.step(-1))
    mixer_in.arrive(3)
    mixer_in.settle((3,))
    for n, at in row_blocks(part):
        part[n] = times_t(head[at], wo[...]).astype(BF).reshape((2,) + part.shape[1:])
        plan.step(-1)

    def middle_rows(n, total):
        at = pl.ds(n * size, size)
        rows = entry[at] + total
        middle[at] = rows
        second[z, y, x, at] = (rows * row_norm(rows) * second_gain[...]).astype(BF)

    plan.during(turn_jobs(scatters[0], gathers[2], AHEAD[2], middle_rows))
    plan.rest()
    units_in.arrive(0)
    units_in.arrive(1)
    gathers[2].finish()
    units_in.settle((0, 1))

    for n, at in row_blocks(second):
        rows = merged(second[n])
        gate_ref[at] = jnp.dot(rows, wg[...], preferred_element_type=F32)
        up_ref[at] = jnp.dot(rows, wu[...], preferred_element_type=F32)
    units_in.arrive(2)
    gathers[1].finish()
    mixer_in.finish()
    units_in.settle((2,))
    units_in.finish()
    for n, at in row_blocks(cot):
        gate_lin, up_lin = gate_ref[at], up_ref[at]
        d_hidden = jnp.dot(merged(cot[n]), wd[...], preferred_element_type=F32)
        s = jax.nn.sigmoid(gate_lin)
        silu = gate_lin * s
        hidden[at] = (silu * up_lin).astype(BF)
        gate_low[at] = (d_hidden * up_lin * s * (1.0 + gate_lin * (1.0 - s))).astype(BF)
        up_low[at] = (d_hidden * silu).astype(BF)
        total = times_t(gate_low[at], wg[...]) + times_t(up_low[at], wu[...])
        part[n] = total.astype(BF).reshape((2,) + part.shape[1:])

    def grad_rows(n, total):
        at = pl.ds(n * size, size)
        back, gains = norm_back(middle[at], total, second_gain[...])
        mine[16:32] = mine[16:32] + gains.reshape(16, 128)
        rows = c_ref[0, at].astype(F32) + back
        mid[at] = rows
        mix[z, y, x, at] = rows.astype(BF)

    def out_rows(n, total):
        at = pl.ds(n * size, size)
        out[0, at] = (middle[at] + total).astype(BF)

    def outer(dst, rows, cols, giver, p):
        width = 512

        def piece(start):
            def run():
                at = pl.ds(start, width)
                dst[at] = outer_sum(merged(rows[:, :, :, :, at]), cols[...]).astype(BF)

            return run

        return [piece(start) for start in range(0, rows.shape[4], width)] + [
            lambda: giver.swap(p).start()
        ]

    def glu_block(n, at):
        def run():
            rows = times_t(hidden[at], wd[...]).astype(BF)
            glu_part[n] = rows.reshape((2,) + glu_part.shape[1:])

        return run

    returns = outer(gg, second, gate_low, units_out, 1) + units_out.jobs(0)
    returns += outer(gu, second, up_low, units_out, 2) + units_out.jobs(1) + units_out.jobs(2)
    outward = [glu_block(n, at) for n, at in row_blocks(glu_part)]
    outward += scatter_jobs(scatters[3], AHEAD[4], out_rows)
    plan = Plan((returns, *TIMES[3]), (outward, *TIMES[4]))
    plan.during(
        turn_jobs(
            scatters[1], gathers[3], AHEAD[3], grad_rows, outer(gd, cot, hidden, units_out, 0)
        )
    )
    gathers[3].finish()

    kept = plan.left(0), plan.left(1)
    plan = Plan((outer(go, mix, head, mixer_out, 0), 0, 2), (kept[0], 0, PACE[0]), (kept[1], 0, 1))
    for n, at in row_blocks(mix):
        d_head[at] = jnp.dot(merged(mix[n]), wo[...], preferred_element_type=F32)
        plan.step(0)
    group, gap = mix_backward(
        blocks, mixed, states, cum, d_head, d_lin, d_mixed, backs, (b_out, b_in, bs, br),
        lambda: plan.step(0),
    )
    mine[32:33] = group
    mine[40:41] = gap
    for n, at in row_blocks(part):
        part[n] = times_t(d_lin[at], wqfi[...]).astype(BF).reshape((2,) + part.shape[1:])

    def in_rows(n, total):
        at = pl.ds(n * size, size)
        back, gains = norm_back(entry[at], total, first_gain[...])
        in_grad[0, at] = mid[at] + back
        mine[0:16] = mine[0:16] + gains.reshape(16, 128)
        if n == PIECES - 1:
            swap = to_core(mine, theirs, vs, vr)
            swap.start()
            swap.wait()
            chips[h] = mine[...] + theirs[...]
            for k in range(1, H):
                to_chip(chips.at[h], chips.at[h], ws, wr, lax.rem(h + k, H)).start()

    for job in plan.left(0):
        job()
    kept = plan.left(1), plan.left(2)
    plan = Plan(
        (kept[0], 0, PACE[1]), (mixer_out.jobs(0) + mixer_out.jobs(1), *TIMES[5]), (kept[1], 0, 1)
    )
    plan.during(
        scatter_jobs(
            scatters[2], AHEAD[5], in_rows, outer(gqfi, first, d_lin, mixer_out, 1)
        )
    )
    plan.rest()
    others = chips.at[0 : H - 1]
    to_chip(others, others, ws, wr, h).wait()
    acc = chips[0, 0:40]
    for chip in range(1, H):
        acc = acc + chips[chip, 0:40]
    totals[0:40] = acc
    for chip in range(H):
        totals[40 + chip : 41 + chip] = chips[chip, 40:41]
    scatters[2].finish()
    scatters[3].finish()
    units_out.finish()
    mixer_out.finish()


def layer(inputs, cotangent, lengths, first_gain, second_gain, group_gain, gap_log, weights):
    _, rows, cols = inputs.shape
    depth, units = weights[-1].shape
    extent, count = H * rows, 2 * H * depth
    tiles = units // 128
    wide = -(-tiles // H) * 128
    home = lambda width: jax.ShapeDtypeStruct((depth, width), BF)
    full = VMEM((4, 2, 2, rows, cols), BF)
    local = VMEM((rows, cols), F32)
    tile = VMEM((extent, SPAN), F32)
    square = VMEM((SPAN, SPAN), F32)
    squares = VMEM((extent // SPAN, SPAN, SPAN), F32)
    widths = (384, 128, wide, wide, wide)
    return pl.pallas_call(
        functools.partial(layer_kernel, tiles),
        out_shape=[
            jax.ShapeDtypeStruct((1, rows, cols), BF),
            jax.ShapeDtypeStruct((1, rows, cols), F32),
            jax.ShapeDtypeStruct((56, 128), F32),
        ]
        + [home(cols)] * 4
        + [home(units)] * 3,
        in_specs=[VSPEC] * 2 + [SSPEC] + [VSPEC] * 4 + [ASPEC] * 7,
        out_specs=[VSPEC] * 3 + [ASPEC] * 7,
        scratch_shapes=[full] * 6
        + [VMEM((count, width), BF) for width in widths]
        + [local, local, local, VMEM((extent, SPAN), jnp.int32)]
        + [VMEM((8 * (extent // SPAN) + 8, SPAN), jnp.int32), VMEM((1, SPAN), F32)]
        + [VMEM((extent, 384), F32), tile, squares, VMEM((extent, SPAN), BF), tile]
        + [tile, VMEM((extent, 384), BF), tile, squares]
        + [VMEM((extent, wide), BF)] * 3
        + [VMEM((extent, wide), F32)] * 2
        + [VMEM((count, width), BF) for width in widths]
        + [VMEM((count // 2, width), BF) for width in widths]
        + scatter_bufs(rows, cols)
        + scatter_bufs(rows, cols)
        + gather_sems() * 4
        + scatter_sems() * 4
        + [square] * 4
        + [DMA] * 5
        + [VMEM((48, 128), F32), VMEM((48, 128), F32), VMEM((H, 48, 128), F32)]
        + [DMA, DMA, DMA, DMA]
        + bulk_sems(4)
        + bulk_sems(3)
        + bulk_sems(3)
        + bulk_sems(4),
        compiler_params=comm_params(1),
    )(
        inputs,
        cotangent,
        lengths,
        first_gain[None],
        second_gain[None],
        group_gain[None],
        gap_log.reshape(H, SPAN),
        *weights,
    )


def product(left, right, at_left, at_right):
    return lax.dot_general(
        left, right, (((at_left,), (at_right,)), ((), ())), preferred_element_type=F32
    )


def halves(rows):
    high = rows.astype(BF)
    return high, (rows - high.astype(F32)).astype(BF)


def mm(left, right, at_left, at_right):
    left_high, left_low = halves(left)
    right_high, right_low = halves(right)
    small = product(left_high, right_low, at_left, at_right)
    small = small + product(left_low, right_high, at_left, at_right)
    return product(left_high, right_high, at_left, at_right) + small


def tri_sum(rows, reverse=False):
    r = lax.broadcasted_iota(jnp.int32, (SPAN, SPAN), 0)
    c = lax.broadcasted_iota(jnp.int32, (SPAN, SPAN), 1)
    picked = jnp.where((r <= c) if reverse else (r >= c), 1.0, 0.0).astype(BF)
    high = rows.astype(BF)
    rest = rows - high.astype(F32)
    middle, low = halves(rest)
    return product(picked, high, 1, 0) + product(picked, middle, 1, 0) + product(picked, low, 1, 0)


def span_gates(lin_ref, gap_ref, at):
    q_lin, f_lin, values = lin_ref[at, 0:128], lin_ref[at, 128:256], lin_ref[at, 256:384]
    s = jax.nn.sigmoid(q_lin)
    key = jnp.exp(gap_ref[...]) * jax.nn.sigmoid(-f_lin)
    return q_lin, f_lin, values, s, key


def span_masks(dcol_ref, drow_ref, c, at):
    r = lax.broadcasted_iota(jnp.int32, (SPAN, SPAN), 0)
    k = lax.broadcasted_iota(jnp.int32, (SPAN, SPAN), 1)
    dcol, drow = dcol_ref[at], drow_ref[8 * c : 8 * c + 1]
    last = (c + 1) * SPAN - 1
    end = dcol_ref[last : last + 1]
    if c:
        before = dcol_ref[c * SPAN - 1 : c * SPAN]
    else:
        count = drow_ref.shape[0]
        before = drow_ref[count - 8 : count - 7]
    same = jnp.where(jnp.logical_and(dcol == drow, r >= k), 1.0, 0.0)
    carried = jnp.where(dcol == before, 1.0, 0.0)
    keep = jnp.where(dcol == end, 1.0, 0.0)
    whole = jnp.where(end == before, 1.0, 0.0)
    return same, carried, keep, whole


def spans(extent):
    return [(c, pl.ds(c * SPAN, SPAN)) for c in range(extent // SPAN)]


def mix_forward(blocks, mixed_ref, states_ref, head_ref, cum_ref, handover, between):
    out_ref, in_ref, send, recv = handover
    lin_ref, gap_ref, gain_ref, dcol_ref, drow_ref = blocks
    steps = spans(lin_ref.shape[0])
    state = jnp.zeros((SPAN, SPAN), F32)
    for c, at in steps:
        q_lin, f_lin, values, s, key = span_gates(lin_ref, gap_ref, at)
        same, carried, keep, whole = span_masks(dcol_ref, drow_ref, c, at)
        cum = tri_sum(jnp.log1p(-key))
        cum_ref[at] = cum
        end = cum[SPAN - 1 : SPAN]
        fresh = mm(values, jnp.exp(end - cum) * key * keep, 0, 0)
        states_ref[c] = fresh
        state = state * (jnp.exp(end) * whole) + fresh
    out_ref[...] = state
    copy = to_core(out_ref, in_ref, send, recv)
    copy.start()
    between()
    copy.wait()
    state = in_ref[...] * lax.axis_index("seq").astype(F32)
    for c, at in steps:
        q_lin, f_lin, values, s, key = span_gates(lin_ref, gap_ref, at)
        same, carried, keep, whole = span_masks(dcol_ref, drow_ref, c, at)
        cum = cum_ref[at]
        end = cum[SPAN - 1 : SPAN]
        fresh = states_ref[c]
        states_ref[c] = state
        decayed = q_lin * s * jnp.exp(cum)
        scores = mm(decayed, key * jnp.exp(-cum), 1, 1) * same
        mixed = mm(scores, values, 1, 0) + carried * mm(decayed, state, 1, 1)
        mixed_ref[at] = mixed
        head_ref[at] = (mixed * row_norm(mixed) * gain_ref[...]).astype(BF)
        state = state * (jnp.exp(end) * whole) + fresh
        if c % 2:
            between()


def mix_backward(
    blocks, mixed_ref, states_ref, cum_ref, dhead_ref, dlin_ref, do_ref, back_ref, handover, between
):
    out_ref, in_ref, send, recv = handover
    lin_ref, gap_ref, gain_ref, dcol_ref, drow_ref = blocks
    steps = spans(lin_ref.shape[0])
    group = jnp.zeros((1, SPAN), F32)
    adjoint = jnp.zeros((SPAN, SPAN), F32)
    for c, at in reversed(steps):
        d_mixed, gains = norm_back(mixed_ref[at], dhead_ref[at], gain_ref[...])
        group = group + gains
        do_ref[at] = d_mixed
        q_lin, f_lin, values, s, key = span_gates(lin_ref, gap_ref, at)
        same, carried, keep, whole = span_masks(dcol_ref, drow_ref, c, at)
        cum = cum_ref[at]
        back = mm(d_mixed, carried * (q_lin * s * jnp.exp(cum)), 0, 0)
        back_ref[c] = back
        adjoint = adjoint * (jnp.exp(cum[SPAN - 1 : SPAN]) * whole) + back
    out_ref[...] = adjoint
    copy = to_core(out_ref, in_ref, send, recv)
    copy.start()
    between()
    copy.wait()
    adjoint = in_ref[...] * (1 - lax.axis_index("seq")).astype(F32)
    gap = jnp.zeros((1, SPAN), F32)
    for c, at in reversed(steps):
        q_lin, f_lin, values, s, key = span_gates(lin_ref, gap_ref, at)
        same, carried, keep, whole = span_masks(dcol_ref, drow_ref, c, at)
        cum, d_mixed, state = cum_ref[at], do_ref[at], states_ref[c]
        grow, shrink = jnp.exp(-cum), jnp.exp(cum)
        end = cum[SPAN - 1 : SPAN]
        decayed, grown = q_lin * s * shrink, key * grow
        rest = jnp.exp(end - cum) * keep
        tail, through = rest * key, jnp.exp(end) * whole
        scores = mm(decayed, grown, 1, 1) * same
        d_scores = mm(d_mixed, values, 1, 1) * same
        d_values = mm(scores, d_mixed, 0, 0) + mm(tail, adjoint, 1, 1)
        d_decayed = mm(d_scores, grown, 1, 0) + carried * mm(d_mixed, state, 1, 0)
        d_grown = mm(d_scores, decayed, 0, 0)
        d_tail = mm(values, adjoint, 1, 0)
        held = tail * d_tail
        d_cum = decayed * d_decayed - grown * d_grown - held
        d_end = jnp.sum(held, axis=0, keepdims=True) + through * jnp.sum(
            state * adjoint, axis=0, keepdims=True
        )
        d_log = tri_sum(d_cum, reverse=True) + d_end
        d_key = d_grown * grow + d_tail * rest - d_log / (1.0 - key)
        scaled = d_key * key
        gap = gap + jnp.sum(scaled, axis=0, keepdims=True)
        dlin_ref[at, 0:128] = (d_decayed * shrink * s * (1.0 + q_lin * (1.0 - s))).astype(BF)
        dlin_ref[at, 128:256] = (-scaled * jax.nn.sigmoid(f_lin)).astype(BF)
        dlin_ref[at, 256:384] = d_values.astype(BF)
        adjoint = adjoint * through + back_ref[c]
        if c % 2:
            between()
    return group, gap


def finish_kernel(out_ref, in_ref, totals_ref, *refs):
    out, in_grad, first, second, group, gap = refs[7:13]
    out[...] = out_ref[...]
    in_grad[...] = in_ref[...]
    first[...] = totals_ref[0:16]
    second[...] = totals_ref[16:32]
    group[...] = totals_ref[32:33]
    gap[...] = totals_ref[40:56]
    for src, dst in zip(refs[:7], refs[13:]):
        dst[...] = src[...].astype(F32)


def finish(output, input_grad, totals, grads):
    depth = grads[0].shape[0]
    rows, cols = output.shape[1:]
    steps = 4
    piece = depth // steps
    local = pl.BlockSpec((1, piece, cols), lambda n: (0, jnp.minimum(n, rows // piece - 1), 0))
    whole = lambda height: pl.BlockSpec((height, 128), lambda n: (0, 0))
    grad = [pl.BlockSpec((piece, g.shape[1]), lambda n: (n, 0)) for g in grads]
    vector = lambda height: jax.ShapeDtypeStruct((height, 128), F32)
    return pl.pallas_call(
        finish_kernel,
        grid=(steps,),
        out_shape=[
            jax.ShapeDtypeStruct(output.shape, BF),
            jax.ShapeDtypeStruct(input_grad.shape, F32),
            vector(16),
            vector(16),
            vector(1),
            vector(16),
        ]
        + [jax.ShapeDtypeStruct(g.shape, F32) for g in grads],
        in_specs=[local, local, whole(56)] + grad,
        out_specs=[local, local, whole(16), whole(16), whole(1), whole(16)] + grad,
        compiler_params=pltpu.CompilerParams(vmem_limit_bytes=62 << 20),
    )(output, input_grad, totals, *grads)


def fast_body(
    inputs,
    cotangent,
    lengths,
    first_gain,
    q_weight,
    f_weight,
    i_weight,
    o_weight,
    group_gain,
    gap_log,
    second_gain,
    gate_weight,
    up_weight,
    down_weight,
):
    model = inputs.shape[2]
    output, input_grad, totals, *grads = layer(
        inputs,
        cotangent,
        lengths,
        first_gain,
        second_gain,
        group_gain,
        gap_log,
        (q_weight, f_weight, i_weight, o_weight, gate_weight, up_weight, down_weight),
    )
    output, input_grad, first_grad, second_grad, group_grad, gap_grad, *grads = finish(
        output, input_grad, totals, grads
    )
    q_grad, f_grad, i_grad, o_grad, gate_grad, up_grad, down_grad = grads
    return (
        output,
        input_grad,
        first_grad.reshape(model),
        q_grad,
        f_grad,
        i_grad,
        o_grad,
        group_grad.reshape(SPAN),
        gap_grad.reshape(model),
        second_grad.reshape(model),
        gate_grad,
        up_grad,
        down_grad,
    )


def solution(mesh):
    placed = (
        P("seq", "hid", None),
        P("seq", "hid", None),
        P(),
        P(),
        P(("seq", "hid"), None),
        P(("seq", "hid"), None),
        P(("seq", "hid"), None),
        P(("seq", "hid"), None),
        P(),
        P(),
        P(),
        P(("seq", "hid"), None),
        P(("seq", "hid"), None),
        P(("seq", "hid"), None),
    )
    body = fast_body if mesh.shape["hid"] == H else wide_body
    return jax.shard_map(
        body,
        mesh=mesh,
        in_specs=placed,
        out_specs=(
            P("seq", "hid", None),
            P("seq", "hid", None),
            P(),
            P(("seq", "hid"), None),
            P(("seq", "hid"), None),
            P(("seq", "hid"), None),
            P(("seq", "hid"), None),
            P(),
            P(),
            P(),
            P(("seq", "hid"), None),
            P(("seq", "hid"), None),
            P(("seq", "hid"), None),
        ),
        check_vma=False,
    )
```
